256 devices in a mesh: chan: 8 (over x_lo, y), lon: 32 (over x_hi, z, core).
Axes of the slice: x: 4 (x_hi: 2, x_lo: 2; x = x_hi * 2 + x_lo), y: 4, z: 8, core: 2. Of those that a mesh axis runs over, the one named last changes fastest.
Arguments:
- symbols: int32 [320, 4, 128, 128], P('chan', None, 'lon'), may hold values from -3 to 3
- hyper_mean: bfloat16 [320, 4, 128, 128], P('chan', None, 'lon'), may hold values from -6 to 6
- slice_order: int32 [8], replicated, may hold values from 0 to 7, each once
- hyper_weight: bfloat16 [8, 15, 224, 40], P('chan'), may hold values from -0.25 to 0.25
- ctx_weight: bfloat16 [8, 15, 224, 320], P('chan'), may hold values from -0.09375 to 0.09375
- ctx_bias: float32 [8, 224], P('chan'), may hold values from -6 to 6
- out_weight: bfloat16 [8, 40, 224], P('chan'), may hold values from -0.375 to 0.375
- gdn_beta: float32 [320], replicated, may hold values from 0.5 to 4
- gdn_gamma: float32 [320, 320], replicated, may hold values from 0 to 0.006
- tconv_weight: bfloat16 [27, 64, 320], P(None, 'chan'), may hold values from -0.078125 to 0.078125
Outputs:
- upsampled: bfloat16 [64, 8, 256, 256], P('chan', None, 'lon')
The draws below stay inside these ranges and needn't reach their ends.
Inputs may be any that keep to these rules, and one draw needn't show every extreme that they name: `slice_order`: each slice number appears exactly once.
All inputs are finite; a program needn't handle non-finite values.
Results may differ from the reference program's by a relative error of at most 0.014.
Values may be sent and summed in bfloat16 or wider, within the bound.
No kernel may reach another device: no remote copies, remote signals or barrier semaphores. Data moves between devices by JAX's collectives and lax.ppermute only.
A program may use at most 64 MiB of HBM per device.

```python
import math
import jax
import jax.numpy as jnp
from jax import lax

C = 320
HID = 224
COUT = 64
LEV = 4
LAT = 128
SLICES = 8
SW = 40
LON = 128


def touch_ends(entries, own_key, low, top_value):
    index_at = [jax.random.randint(jax.random.fold_in(own_key, axis), (), 0, length) for axis, length in enumerate(entries.shape)]
    main_axis = entries.shape.index(max(entries.shape))
    beside = index_at[:main_axis] + [(index_at[main_axis] + 1) % entries.shape[main_axis]] + index_at[main_axis + 1:]
    return entries.at[tuple(index_at)].set(low).at[tuple(beside)].set(top_value)


def block_levels(own_key, shape, shards, smallest, top_value):
    loudness, own = 1.0, jax.random.fold_in(own_key, 6)
    for dim, blocks in shards:
        steps = jnp.exp(jax.random.uniform(jax.random.fold_in(own, dim), (blocks,), jnp.float32, smallest / len(shards), top_value / len(shards)))
        loudness = loudness * jnp.repeat(steps, shape[dim] // blocks).reshape([-1 if axis == dim else 1 for axis in range(len(shape))])
    return loudness


def bell_draw(rng, extent, spread, limit, split=(), dtype=jnp.bfloat16):
    values = spread * jax.random.normal(rng, extent, jnp.float32)
    if split:
        values = values * block_levels(rng, extent, split, -0.22, 0.18)
    return jnp.clip(values, -limit, limit).astype(dtype)


def setup_inputs(seed: int = 0) -> dict:
    streams_of = jax.random.split(jax.random.key(seed), 11)
    symbols = touch_ends(jax.random.randint(streams_of[0], (C, LEV, LON, LAT), -3, 4), jax.random.fold_in(streams_of[0], 1), -3, 3).astype(jnp.int32)
    hyper_mean = bell_draw(streams_of[1], (C, LEV, LON, LAT), 1.0, 6.0, ((0, 8), (2, 32)))
    slice_order = jax.random.permutation(streams_of[2], SLICES).astype(jnp.int32)
    hyper_weight = bell_draw(streams_of[3], (SLICES, 15, HID, SW), (15 * SW) ** -0.5, 0.25, ((0, 8),))
    ctx_weight = bell_draw(streams_of[4], (SLICES, 15, HID, C), (15 * C) ** -0.5, 0.09375, ((0, 8),))
    ctx_bias = bell_draw(streams_of[5], (SLICES, HID), 1.0, 6.0, ((0, 8),), jnp.float32)
    out_weight = bell_draw(streams_of[6], (SLICES, SW, HID), HID ** -0.5, 0.375, ((0, 8),))
    gdn_beta = jnp.clip(jnp.exp(jax.random.uniform(streams_of[7], (C,), jnp.float32, math.log(0.5), math.log(4.0))), 0.5, 4.0)
    gdn_gamma = jnp.clip(jax.random.uniform(streams_of[8], (C, C), jnp.float32, 0.0, 0.006), 0.0, 0.006)
    tconv_weight = bell_draw(streams_of[9], (27, COUT, C), (16 * C) ** -0.5, 0.078125, ((1, 8),))
    return dict(symbols=symbols, hyper_mean=hyper_mean, slice_order=slice_order, hyper_weight=hyper_weight, ctx_weight=ctx_weight, ctx_bias=ctx_bias, out_weight=out_weight, gdn_beta=gdn_beta, gdn_gamma=gdn_gamma, tconv_weight=tconv_weight)


def band_conv(field, weight):
    padded = jnp.pad(field.astype(jnp.float32), ((0, 0), (0, 0), (0, 0), (1, 1)))
    lat_len = field.shape[3]
    summed = jnp.zeros((weight.shape[1],) + field.shape[1:], jnp.float32)
    for shift_lon in range(5):
        rolled = jnp.roll(padded, 2 - shift_lon, axis=2)
        for shift_lat in range(3):
            section = rolled[:, :, :, shift_lat:shift_lat + lat_len]
            tap_weight = weight[shift_lon * 3 + shift_lat].astype(jnp.float32)
            summed = summed + jnp.einsum('hc,cvxt->hvxt', tap_weight, section)
    return summed

def upsample(extended, weight):
    lev_len = extended.shape[1] - 1
    lon_len = extended.shape[2] - 1
    lat_len = extended.shape[3] - 1
    tap_table = (((1, 0),), ((2, 0), (0, 1)))
    parity_parts = []
    for par_lev in range(2):
        for par_lon in range(2):
            for par_lat in range(2):
                summed = jnp.zeros((weight.shape[1], lev_len, lon_len, lat_len), jnp.float32)
                for tap_lev, off_lev in tap_table[par_lev]:
                    for tap_lon, off_lon in tap_table[par_lon]:
                        for tap_lat, off_lat in tap_table[par_lat]:
                            section = extended[:, off_lev:off_lev + lev_len, off_lon:off_lon + lon_len, off_lat:off_lat + lat_len]
                            tap_weight = weight[tap_lev * 9 + tap_lon * 3 + tap_lat]
                            summed = summed + jnp.einsum('oc,cvxt->ovxt', tap_weight, section, preferred_element_type=jnp.float32)
                parity_parts.append(summed)
    stacked = jnp.stack(parity_parts).reshape((2, 2, 2) + parity_parts[0].shape)
    reordered = jnp.transpose(stacked, (3, 4, 0, 5, 1, 6, 2))
    return reordered.reshape(weight.shape[1], 2 * lev_len, 2 * lon_len, 2 * lat_len)

def reference(symbols, hyper_mean, slice_order, hyper_weight, ctx_weight, ctx_bias, out_weight, gdn_beta, gdn_gamma, tconv_weight):
    decoded = jnp.zeros(hyper_mean.shape, jnp.bfloat16)

    def decode(step_id, decoded):
        slice_id = slice_order[step_id]
        first_row = (slice_id * SW).astype(jnp.int32)
        hyper_rows = lax.dynamic_slice_in_dim(hyper_mean, first_row, SW, 0)
        pre_act = band_conv(hyper_rows, hyper_weight[slice_id]) + band_conv(decoded, ctx_weight[slice_id])
        pre_act = pre_act + ctx_bias[slice_id][:, None, None, None]
        hidden = jax.nn.gelu(pre_act, approximate=False).astype(jnp.bfloat16)
        slice_mean = jnp.einsum('ch,hvxt->cvxt', out_weight[slice_id].astype(jnp.float32), hidden.astype(jnp.float32))
        symbol_values = lax.dynamic_slice_in_dim(symbols, first_row, SW, 0).astype(jnp.float32)
        decoded_rows = (symbol_values + slice_mean).astype(jnp.bfloat16)
        return lax.dynamic_update_slice_in_dim(decoded, decoded_rows, first_row, 0)
    decoded = lax.fori_loop(0, SLICES, decode, decoded)
    values = decoded.astype(jnp.float32)
    energy = gdn_beta[:, None, None, None] + jnp.einsum('ij,jvxt->ivxt', gdn_gamma, values * values, precision=lax.Precision.HIGHEST)
    normed = (values * jnp.sqrt(energy)).astype(jnp.bfloat16)
    extended = jnp.concatenate([normed, normed[:, :, :1]], axis=2)
    extended = jnp.pad(extended, ((0, 0), (0, 1), (0, 0), (0, 1)))
    result = upsample(extended.astype(jnp.float32), tconv_weight.astype(jnp.float32))
    return result.astype(jnp.bfloat16)
```

```python
import jax
import jax.numpy as jnp
from jax import lax
from jax.sharding import PartitionSpec as P

BF = jnp.bfloat16
F32 = jnp.float32
SW = 40
HALF = 112
Y_GROUPS = [[0, 1, 2, 3], [4, 5, 6, 7]]


def x_swap(value):
    return lax.ppermute(value, "chan", [(i, i ^ 4) for i in range(8)])


def core_swap(value):
    return lax.ppermute(value, "lon", [(i, i ^ 1) for i in range(32)])


def from_lon(value, distance):
    return lax.ppermute(value, "lon", [(i, (i - distance) % 32) for i in range(32)])


def gather_chunk(chunk, x_id, core):
    mine = lax.dynamic_slice_in_dim(chunk, core * 80, 80, 1)
    low, high = mine[:, :, :HALF], mine[:, :, HALF:]
    keep = jnp.where(x_id == 0, low, high)
    give = jnp.where(x_id == 0, high, low)
    pair = jnp.stack([keep, x_swap(give)])
    half = lax.all_gather(pair, "chan", axis_index_groups=Y_GROUPS)
    other = core_swap(half)
    first = jnp.where(core == 0, half, other)
    second = jnp.where(core == 0, other, half)
    return jnp.concatenate([first, second], axis=3)


def conv(field, weight):
    return lax.conv_general_dilated(
        field[:, None],
        weight.reshape(5, 3, weight.shape[1], weight.shape[2]),
        (1, 1),
        ((0, 0), (1, 1)),
        dimension_numbers=("CNHW", "HWIO", "CNHW"),
        preferred_element_type=F32,
    )[:, 0]


def local(
    symbols,
    hyper_mean,
    slice_order,
    hyper_weight,
    ctx_weight,
    ctx_bias,
    out_weight,
    gdn_beta,
    gdn_gamma,
    tconv_weight,
):
    chan = lax.axis_index("chan")
    x_id = chan // 4
    core = lax.axis_index("lon") % 2

    small = jnp.concatenate([out_weight[0].astype(F32), ctx_bias], axis=0)
    small = lax.all_gather(small, "chan")
    tconv_all = lax.all_gather(tconv_weight, "chan", axis_index_groups=Y_GROUPS)

    ctx = jnp.transpose(ctx_weight[0], (0, 2, 1))
    units = [jnp.transpose(hyper_weight[0], (0, 2, 1))] + [
        lax.dynamic_slice_in_dim(ctx, slice_order[j] * SW, SW, 1) for j in range(7)
    ]
    weight_a = gather_chunk(jnp.concatenate(units[:4], axis=1), x_id, core)
    weight_b = gather_chunk(jnp.concatenate(units[4:], axis=1), x_id, core)

    both = jnp.stack([symbols.astype(BF), hyper_mean])
    send = jnp.transpose(both, (2, 0, 1, 3, 4))
    recv = lax.all_to_all(jnp.concatenate([send, send]), "chan", 0, 0)
    ranked = jnp.stack(
        [lax.dynamic_index_in_dim(recv, slice_order[k], 0, keepdims=False) for k in range(8)]
    )
    far = jnp.concatenate([ranked[0:2], ranked[4:6]])
    left1, right1 = from_lon(ranked, -1), from_lon(ranked, 1)
    left2, right2 = from_lon(far, -2), from_lon(far, 2)
    fields = []
    for k in range(8):
        parts = [left1[k], ranked[k], right1[k]]
        base = -4
        if k % 4 < 2:
            j = (k // 4) * 2 + k % 4
            parts = [left2[j]] + parts + [right2[j]]
            base = -8
        fields.append((base, jnp.concatenate(parts, axis=2)))

    known = []
    for k in range(8):
        reach = 2 * (3 - k % 4)
        low, high = -reach, 4 + reach
        s = slice_order[k]
        where = (s % 4, jnp.where(s // 4 == x_id, 0, 1), 0, 0, 0)
        base, field = fields[k]
        inputs = [field[1][:, low - 2 - base : high + 2 - base]]
        for other_base, value in known:
            inputs.append(value[:, low - 2 - other_base : high + 2 - other_base])
        pre = conv(
            jnp.concatenate(inputs[:4]),
            lax.dynamic_slice(weight_a, where, (1, 1, 15, 160, HALF))[0, 0][:, : SW * min(k + 1, 4)],
        )
        if k >= 4:
            pre = pre + conv(
                jnp.concatenate(inputs[4:]),
                lax.dynamic_slice(weight_b, where, (1, 1, 15, 160, HALF))[0, 0][:, : SW * (k - 3)],
            )
        slim = lax.dynamic_index_in_dim(small, s, 0, keepdims=False)
        slim = jnp.where(x_id == 0, slim[:, :HALF], slim[:, HALF:])
        pre = pre + slim[SW][:, None, None]
        hidden = jax.nn.gelu(pre, approximate=False).astype(BF)
        part = jnp.einsum("ch,hxt->cxt", slim[:SW].astype(BF), hidden, preferred_element_type=F32)
        part = part.astype(BF)
        mean = part.astype(F32) + x_swap(part).astype(F32)
        symbol = field[0][:, low - base : high - base].astype(F32)
        known.append((low, (symbol + mean).astype(BF)))
        if k == 3:
            done = jnp.concatenate([v[:, -b : 4 - b] for b, v in known])
            wide = jnp.concatenate(
                [from_lon(done, -2), from_lon(done, -1), done, from_lon(done, 1), from_lon(done, 2)],
                axis=1,
            )
            known = [(-8, wide[SW * j : SW * (j + 1)]) for j in range(4)]

    stacked = jnp.stack([v[:, -b : 4 - b] for b, v in known])
    rank_of = [jnp.argmax(slice_order == s) for s in range(8)]
    decoded = jnp.concatenate(
        [lax.dynamic_index_in_dim(stacked, rank_of[s], 0, keepdims=False) for s in range(8)]
    ).astype(F32)
    energy = gdn_beta[:, None, None] + jnp.einsum(
        "ij,jxt->ixt", gdn_gamma, decoded * decoded, precision=lax.Precision.HIGHEST
    )
    normed = (decoded * jnp.sqrt(energy)).astype(BF)

    edge = normed[:, :1]
    down = [(i + 1, i) for i in range(8) if i % 4 < 3]
    both_axes = [(i * 32 + (j + 1) % 32, (i - 1) * 32 + j) for i in range(8) if i % 4 > 0 for j in range(32)]
    column = from_lon(edge, 1)
    above = lax.ppermute(normed, "chan", down)
    corner = lax.ppermute(edge, ("chan", "lon"), both_axes)
    extended = jnp.stack(
        [jnp.concatenate([normed, column], axis=1), jnp.concatenate([above, corner], axis=1)]
    )
    extended = jnp.pad(extended, ((0, 0), (0, 0), (0, 0), (0, 1)))
    taps = {0: {0: 1, 1: 2}, 1: {1: 0}}
    totals = {}
    tconv_all = jnp.transpose(tconv_all, (1, 0, 2, 3)).reshape(27, 32, 320)
    for dl in range(2):
        for dx in range(2):
            for dt in range(2):
                names, rows = [], []
                for p, kl in taps[dl].items():
                    for q, kx in taps[dx].items():
                        for r, kt in taps[dt].items():
                            names.append((p, q, r))
                            rows.append(tconv_all[kl * 9 + kx * 3 + kt])
                got = jnp.einsum(
                    "oc,cxt->oxt",
                    jnp.concatenate(rows),
                    extended[dl, :, dx : dx + 4, dt : dt + 128],
                    preferred_element_type=F32,
                )
                for i, name in enumerate(names):
                    piece = got[32 * i : 32 * (i + 1)]
                    totals[name] = totals[name] + piece if name in totals else piece
    result = jnp.stack(
        [totals[(p, q, r)] for p in range(2) for q in range(2) for r in range(2)]
    ).astype(BF)
    result = jnp.transpose(result.reshape(8, 4, 8, 4, 128), (1, 0, 2, 3, 4))
    result = lax.all_to_all(result, "chan", 0, 0, axis_index_groups=Y_GROUPS)
    result = result.reshape(4, 2, 2, 2, 8, 4, 128)
    return jnp.transpose(result, (4, 0, 1, 5, 2, 6, 3)).reshape(8, 8, 8, 256)


def solution(mesh):
    placed = (
        P("chan", None, "lon", None),
        P("chan", None, "lon", None),
        P(),
        P("chan", None, None, None),
        P("chan", None, None, None),
        P("chan", None),
        P("chan", None, None),
        P(),
        P(),
        P(None, "chan", None),
    )
    return jax.shard_map(
        local, mesh=mesh, in_specs=placed, out_specs=P("chan", None, "lon", None), check_vma=False
    )
```

```python
import functools
import jax
import jax.numpy as jnp
from jax import lax
from jax.experimental import pallas as pl
from jax.experimental.pallas import tpu as pltpu
from jax.sharding import PartitionSpec as P

BF = jnp.bfloat16
F32 = jnp.float32
SW = 40
HALF = 112
LAT = 128
UNIT = 640
Y_GROUPS = [[0, 1, 2, 3], [4, 5, 6, 7]]
LANES = (2816, 2560)
ANY = pl.BlockSpec(memory_space=pl.ANY)
VMEM = pl.BlockSpec(memory_space=pltpu.VMEM)
SMEM = pl.BlockSpec(memory_space=pltpu.SMEM)
PARAMS = pltpu.CompilerParams(vmem_limit_bytes=48 << 20)


def x_swap(value):
    return lax.ppermute(value, "chan", [(i, i ^ 4) for i in range(8)])


def core_swap(value):
    return lax.ppermute(value, "lon", [(i, i ^ 1) for i in range(32)])


def from_y(value, distance):
    return lax.ppermute(
        value, "chan", [(i, (i // 4) * 4 + (i - distance) % 4) for i in range(8)]
    )


def from_lon(value, distance):
    return lax.ppermute(value, "lon", [(i, (i - distance) % 32) for i in range(32)])


def bias_rows(bias):
    high = bias.astype(BF)
    rest = bias - high.astype(F32)
    mid = rest.astype(BF)
    low = (rest - mid.astype(F32)).astype(BF)
    return jnp.stack([high, mid, low])


def pack_weights(slice_order, hyper_weight, ctx_weight, ctx_bias, out_weight):
    ctx = jnp.transpose(ctx_weight[0], (0, 2, 1))
    pad = jnp.zeros((5, 8, 224), BF)

    def unit(taps, tail):
        return jnp.concatenate([taps.reshape(5, 120, 224), tail], axis=1).reshape(UNIT, 224)

    bias = jnp.zeros((5, 8, 224), BF).at[2, :3].set(bias_rows(ctx_bias[0]))
    units = [unit(jnp.transpose(hyper_weight[0], (0, 2, 1)), bias)]
    for j in range(7):
        units.append(unit(lax.dynamic_slice_in_dim(ctx, slice_order[j] * SW, SW, 1), pad))
    outs = jnp.pad(out_weight[0], ((0, 216), (0, 0)))
    return (jnp.concatenate(units[:4] + [outs]).T, jnp.concatenate(units[4:]).T)


def spread_chunk(chunk, x_id, core):
    lanes = chunk.shape[1] // 2
    keep = lax.dynamic_slice(chunk, (HALF * x_id, core * lanes), (HALF, lanes))
    keep_other = lax.dynamic_slice(chunk, (HALF * x_id, (1 - core) * lanes), (HALF, lanes))
    give = lax.dynamic_slice(chunk, (HALF * (1 - x_id), core * lanes), (HALF, lanes))
    got = x_swap(give)
    pair = jnp.concatenate([keep, got])
    up, down = from_y(pair, -1), from_y(pair, 1)
    far_own, far_other = from_y(up[:HALF], -1), from_y(down[HALF:], 1)
    mine = [pair, down, up, far_own, far_other]
    other = [keep_other, core_swap(got), core_swap(down), core_swap(up), core_swap(far_own), core_swap(far_other)]
    return mine + other


def fetch_chunk(refs, where_ref, dest, sem):
    pair, down, up, far_own, far_other, keep_o, got_o, down_o, up_o, far_own_o, far_other_o = refs
    relative, side, core = where_ref[0], where_ref[1], where_ref[2]
    lanes = pair.shape[1]
    mine = dest.at[:, pl.ds(pl.multiple_of(core * lanes, 128), lanes)]
    other = dest.at[:, pl.ds(pl.multiple_of((1 - core) * lanes, 128), lanes)]

    def rows(ref, i):
        return ref.at[pl.ds(i * HALF, HALF)]

    for i in range(2):
        choices = (
            (rows(pair, i), (keep_o, got_o)[i]),
            (rows(down, i), rows(down_o, i)),
            ((far_own, far_other)[i], (far_own_o, far_other_o)[i]),
            (rows(up, i), rows(up_o, i)),
        )
        for r, (first, second) in enumerate(choices):

            @pl.when((relative == r) & (side == i))
            def _(first=first, second=second):
                pltpu.make_async_copy(first, mine, sem.at[0]).start()
                pltpu.make_async_copy(second, other, sem.at[1]).start()

    def wait():
        pltpu.make_async_copy(far_own, mine, sem.at[0]).wait()
        pltpu.make_async_copy(far_own_o, other, sem.at[1]).wait()

    return wait


def stack_taps(plane, fill):
    lane = lax.broadcasted_iota(jnp.int32, plane.shape, 1)
    before = jnp.where(lane == 0, 0.0, pltpu.roll(plane, 1, 1))
    after = jnp.where(lane == LAT - 1, 0.0, pltpu.roll(plane, LAT - 1, 1))
    tail = jnp.full((8, LAT), fill, F32)
    return jnp.concatenate([before, plane, after, tail], axis=0).astype(BF)


def tap_pair(stack_ref, start):
    first = stack_ref[pl.ds(start, 5)].reshape(UNIT, LAT)
    second = stack_ref[pl.ds(start + 1, 5)].reshape(UNIT, LAT)
    return jnp.concatenate([first, second], axis=1)


def early_kernel(n_chunks, n_prior, offsets, has_last, *refs):
    where_ref = refs[0]
    chunks = [refs[1 + 11 * i : 12 + 11 * i] for i in range(n_chunks)]
    at = 1 + 11 * n_chunks
    hyper_ref = refs[at]
    priors = refs[at + 1 : at + 1 + n_prior]
    at += 1 + n_prior
    acc_ref, out_ref = refs[at : at + 2]
    at += 2
    if has_last:
        last_ref = refs[at]
        at += 1
    hyper_stack, weights, sems = refs[at], refs[at + 1 : at + 1 + n_chunks], refs[at + 1 + n_chunks]
    waits = [fetch_chunk(chunks[i], where_ref, weights[i], sems.at[i]) for i in range(n_chunks)]

    @pl.loop(0, hyper_stack.shape[0])
    def _(i):
        hyper_stack[i] = stack_taps(hyper_ref[i].astype(F32), 1.0)

    for wait in waits:
        wait()

    def weight(u):
        return weights[u // 4].at[:, pl.ds(UNIT * (u % 4), UNIT)]

    outs = weights[0][:, 2560:2688].astype(F32)
    outs = jnp.concatenate([outs, jnp.zeros((16, 128), F32)], axis=0)
    out_ref[...] = outs.T.astype(BF)
    if has_last:
        last_ref[...] = weight(n_prior + 1)[...]

    @pl.loop(0, acc_ref.shape[0])
    def _(p):
        total = jnp.dot(weight(0)[...], tap_pair(hyper_stack, 2 * p), preferred_element_type=F32)
        for j in range(n_prior):
            total = total + jnp.dot(
                weight(j + 1)[...],
                tap_pair(priors[j], 2 * p + offsets[j]),
                preferred_element_type=F32,
            )
        acc_ref[p] = total


def early(where, chunks, hyper, priors, offsets, has_last):
    planes = hyper.shape[0]
    pairs = (planes - 4) // 2
    shapes = [jax.ShapeDtypeStruct((pairs, HALF, 2 * LAT), F32), jax.ShapeDtypeStruct((128, 128), BF)]
    if has_last:
        shapes.append(jax.ShapeDtypeStruct((HALF, UNIT), BF))
    flops = 2 * pairs * 256 * UNIT * HALF * (1 + len(priors))
    return pl.pallas_call(
        functools.partial(early_kernel, len(chunks), len(priors), offsets, has_last),
        out_shape=shapes,
        in_specs=[SMEM] + [ANY] * (11 * len(chunks)) + [VMEM] * (1 + len(priors)),
        out_specs=[VMEM] * len(shapes),
        scratch_shapes=[pltpu.VMEM((planes, 128, LAT), BF)]
        + [pltpu.VMEM((HALF, LANES[i]), BF) for i in range(len(chunks))]
        + [pltpu.SemaphoreType.DMA((len(chunks), 2))],
        compiler_params=PARAMS,
        cost_estimate=pl.CostEstimate(flops=2 * flops, bytes_accessed=2 << 20, transcendentals=0),
        name="early",
    )(where, *[ref for chunk in chunks for ref in chunk], hyper, *priors)


ERF_TOP = (0.00022905065861350646, 0.0034082910107109506, 0.050955695062380861, 0.18520832239976145, 1.128379143519084)
ERF_LOW = (-1.1791602954361697e-7, 0.000023547966471313185, 0.0010179625278914885, 0.014070470171167667, 0.11098505178285362, 0.49746925110067538, 1.0)


def gelu(v):
    z = jnp.clip(v * 0.7071067811865476, -3.7439211627767994, 3.7439211627767994)
    square = z * z
    top = jnp.full_like(z, ERF_TOP[0])
    for c in ERF_TOP[1:]:
        top = top * square + c
    low = jnp.full_like(z, ERF_LOW[0])
    for c in ERF_LOW[1:]:
        low = low * square + c
    half = 0.5 * v
    return half + half * (z * top / low)


def finish_kernel(has_last, *refs):
    if has_last:
        acc_ref, out_ref, last_ref, own_ref, got_ref, symbol_ref, part_ref, value_ref, stack_ref = refs

        @pl.loop(0, value_ref.shape[0])
        def _(i):
            mean = own_ref[i].astype(F32) + got_ref[i].astype(F32)
            value = (symbol_ref[i].astype(F32) + mean).astype(BF)
            value_ref[i] = value
            stack_ref[i] = stack_taps(value.astype(F32), 0.0)
    else:
        acc_ref, out_ref, part_ref = refs

    @pl.loop(0, acc_ref.shape[0])
    def _(p):
        total = acc_ref[p]
        if has_last:
            total = total + jnp.dot(last_ref[...], tap_pair(stack_ref, 2 * p), preferred_element_type=F32)
        hidden = gelu(total).astype(BF)
        part = jnp.dot(out_ref[:SW, :HALF], hidden, preferred_element_type=F32).astype(BF)
        part_ref[2 * p] = part[:, :LAT]
        part_ref[2 * p + 1] = part[:, LAT:]


def finish(acc, outs, last=None, own=None, got=None, symbol=None):
    lons = 2 * acc.shape[0]
    shapes = [jax.ShapeDtypeStruct((lons, SW, LAT), BF)]
    operands = [acc, outs]
    if last is not None:
        operands += [last, own, got, symbol]
        shapes += [
            jax.ShapeDtypeStruct(own.shape, BF),
            jax.ShapeDtypeStruct((own.shape[0], 128, LAT), BF),
        ]
    return pl.pallas_call(
        functools.partial(finish_kernel, last is not None),
        out_shape=shapes,
        in_specs=[VMEM] * len(operands),
        out_specs=[VMEM] * len(shapes),
        compiler_params=PARAMS,
        cost_estimate=pl.CostEstimate(
            flops=4 * lons * LAT * UNIT * HALF, bytes_accessed=1 << 20, transcendentals=0
        ),
        name="finish",
    )(*operands)


def widen_kernel(*refs):
    stack_ref = refs[5]
    for b in range(5):
        for j in range(stack_ref.shape[0]):
            for i in range(4):
                stack_ref[j, 4 * b + i] = stack_taps(refs[b][j, i].astype(F32), 0.0)


def widen(bands):
    count = bands[0].shape[0]
    return pl.pallas_call(
        widen_kernel,
        out_shape=jax.ShapeDtypeStruct((count, 20, 128, LAT), BF),
        in_specs=[VMEM] * 5,
        out_specs=VMEM,
        compiler_params=PARAMS,
        name="widen",
    )(*bands)


def local(
    symbols,
    hyper_mean,
    slice_order,
    hyper_weight,
    ctx_weight,
    ctx_bias,
    out_weight,
    gdn_beta,
    gdn_gamma,
    tconv_weight,
):
    chan = lax.axis_index("chan")
    x_id, y_id = chan // 4, chan % 4
    core = lax.axis_index("lon") % 2

    both = jnp.stack([symbols.astype(BF), hyper_mean])
    send = jnp.transpose(both, (2, 0, 3, 1, 4))
    recv = lax.all_to_all(jnp.concatenate([send, send]), "chan", 0, 0)
    packed = pack_weights(slice_order, hyper_weight, ctx_weight, ctx_bias, out_weight)
    chunks = [spread_chunk(chunk, x_id, core) for chunk in packed]

    ranked = jnp.stack(
        [lax.dynamic_index_in_dim(recv, slice_order[k], 0, keepdims=False) for k in range(8)]
    )
    far = jnp.concatenate([ranked[0:2], ranked[4:6]])
    left1, right1 = from_lon(ranked, -1), from_lon(ranked, 1)
    left2, right2 = from_lon(far, -2), from_lon(far, 2)
    fields = []
    for k in range(8):
        parts = [left1[k], ranked[k], right1[k]]
        base = -4
        if k % 4 < 2:
            j = (k // 4) * 2 + k % 4
            parts = [left2[j]] + parts + [right2[j]]
            base = -8
        fields.append((base, jnp.concatenate(parts, axis=1)))

    def span(k, kind, margin):
        base, field = fields[k]
        reach = 2 * (3 - k % 4) + margin
        return field[kind, -reach - base : 4 + reach - base]

    values, stacks, part = [], [], None
    for k in range(8):
        s = slice_order[k]
        where = jnp.stack([(s % 4 - y_id) % 4, jnp.where(s // 4 == x_id, 0, 1), core]).astype(jnp.int32)
        has_last = k % 4 > 0
        n_prior = k - 1 if has_last else k
        low = -2 * (3 - k % 4) - 2
        acc, outs, *last = early(
            where,
            chunks[: 1 + (k >= 4)],
            span(k, 1, 2),
            [stack for _, stack in stacks[:n_prior]],
            [low - base for base, _ in stacks[:n_prior]],
            has_last,
        )
        if has_last:
            part, value, stack = finish(acc, outs, last[0], part, x_swap(part), span(k - 1, 0, 0))
            values.append(value)
            stacks.append((-2 * (3 - (k - 1) % 4), stack))
        else:
            (part,) = finish(acc, outs)
        if k % 4 == 3:
            mean = part.astype(F32) + x_swap(part).astype(F32)
            values.append((span(k, 0, 0).astype(F32) + mean).astype(BF))
        if k == 3:
            stacks = []
            early_done = jnp.stack([v[v.shape[0] // 2 - 2 : v.shape[0] // 2 + 2] for v in values[:3]])
            for done in (early_done, values[3][None]):
                wide = widen([from_lon(done, -2), from_lon(done, -1), done, from_lon(done, 1), from_lon(done, 2)])
                stacks += [(-8, wide[j]) for j in range(done.shape[0])]

    stacked = jnp.stack([v[v.shape[0] // 2 - 2 : v.shape[0] // 2 + 2] for v in values])
    rank_of = [jnp.argmax(slice_order == s) for s in range(8)]
    decoded = jnp.concatenate(
        [lax.dynamic_index_in_dim(stacked, rank_of[s], 0, keepdims=False) for s in range(8)], axis=1
    )
    decoded = jnp.transpose(decoded, (1, 0, 2)).astype(F32)
    energy = gdn_beta[:, None, None] + jnp.einsum(
        "ij,jxt->ixt", gdn_gamma, decoded * decoded, precision=lax.Precision.HIGHEST
    )
    normed = (decoded * jnp.sqrt(energy)).astype(BF)

    edge = normed[:, :1]
    down = [(i + 1, i) for i in range(8) if i % 4 < 3]
    both_axes = [(i * 32 + (j + 1) % 32, (i - 1) * 32 + j) for i in range(8) if i % 4 > 0 for j in range(32)]
    column = from_lon(edge, 1)
    above = lax.ppermute(normed, "chan", down)
    corner = lax.ppermute(edge, ("chan", "lon"), both_axes)
    extended = jnp.stack(
        [jnp.concatenate([normed, column], axis=1), jnp.concatenate([above, corner], axis=1)]
    )
    extended = jnp.pad(extended, ((0, 0), (0, 0), (0, 0), (0, 1)))
    taps = {0: {0: 1, 1: 2}, 1: {1: 0}}
    totals = {}
    gathered = lax.all_gather(tconv_weight, "chan", axis_index_groups=Y_GROUPS)
    tconv_all = jnp.transpose(gathered, (1, 0, 2, 3)).reshape(27, 32, 320)
    for dl in range(2):
        for dx in range(2):
            for dt in range(2):
                names, rows = [], []
                for p, kl in taps[dl].items():
                    for q, kx in taps[dx].items():
                        for r, kt in taps[dt].items():
                            names.append((p, q, r))
                            rows.append(tconv_all[kl * 9 + kx * 3 + kt])
                got = jnp.einsum(
                    "oc,cxt->oxt",
                    jnp.concatenate(rows),
                    extended[dl, :, dx : dx + 4, dt : dt + 128],
                    preferred_element_type=F32,
                )
                for i, name in enumerate(names):
                    piece = got[32 * i : 32 * (i + 1)]
                    totals[name] = totals[name] + piece if name in totals else piece
    result = jnp.stack(
        [totals[(p, q, r)] for p in range(2) for q in range(2) for r in range(2)]
    ).astype(BF)
    result = jnp.transpose(result.reshape(8, 4, 8, 4, 128), (1, 0, 2, 3, 4))
    result = lax.all_to_all(result, "chan", 0, 0, axis_index_groups=Y_GROUPS)
    result = result.reshape(4, 2, 2, 2, 8, 4, 128)
    return jnp.transpose(result, (4, 0, 1, 5, 2, 6, 3)).reshape(8, 8, 8, 256)


def solution(mesh):
    placed = (
        P("chan", None, "lon", None),
        P("chan", None, "lon", None),
        P(),
        P("chan", None, None, None),
        P("chan", None, None, None),
        P("chan", None),
        P("chan", None, None),
        P(),
        P(),
        P(None, "chan", None),
    )
    return jax.shard_map(
        local, mesh=mesh, in_specs=placed, out_specs=P("chan", None, "lon", None), check_vma=False
    )
```

```python
import functools
import jax
import jax.numpy as jnp
from jax import lax
from jax.experimental import pallas as pl
from jax.experimental.pallas import tpu as pltpu
from jax.sharding import PartitionSpec as P

BF = jnp.bfloat16
F32 = jnp.float32
SW = 40
HALF = 112
LAT = 128
UNIT = 640
LANES = (2816, 2560)
ANY = pl.BlockSpec(memory_space=pl.ANY)
VMEM = pl.BlockSpec(memory_space=pltpu.VMEM)
SMEM = pl.BlockSpec(memory_space=pltpu.SMEM)
COST = pl.CostEstimate(flops=200_000_000, bytes_accessed=1 << 20, transcendentals=0)
PARAMS = pltpu.CompilerParams(vmem_limit_bytes=48 << 20)


def x_swap(value):
    return lax.ppermute(value, "chan", [(i, i ^ 4) for i in range(8)])


def core_swap(value):
    return lax.ppermute(value, "lon", [(i, i ^ 1) for i in range(32)])


def from_y(value, distance):
    return lax.ppermute(
        value, "chan", [(i, (i // 4) * 4 + (i - distance) % 4) for i in range(8)]
    )


def from_lon(value, distance):
    return lax.ppermute(value, "lon", [(i, (i - distance) % 32) for i in range(32)])


def pack_kernel(order_ref, hyper_ref, ctx_ref, bias_ref, out_ref, *refs):
    keeps, keep_others, gives = refs[0:2], refs[2:4], refs[4:6]
    blocks, packed, sem = refs[6], refs[7:9], refs[9]
    x_id = lax.axis_index("chan") // 4
    core = lax.axis_index("lon") % 2
    copies = []
    for j in range(7):
        rows = pl.ds(pl.multiple_of(order_ref[j] * SW, 8), SW)
        copies.append(pltpu.make_async_copy(ctx_ref.at[:, rows, :], blocks.at[j], sem.at[j]))
        copies[-1].start()
    bias = bias_ref[...]
    high = bias.astype(BF).astype(F32)
    mid = (bias - high).astype(BF).astype(F32)
    low = (bias - high - mid).astype(BF).astype(F32)
    parts = jnp.concatenate([high, mid, low, jnp.zeros((5, 224), F32)], axis=0)

    def put(u, taps):
        for a in range(5):
            tail = parts if u == 0 and a == 2 else jnp.zeros((8, 224), F32)
            block = jnp.concatenate([taps[3 * a + b].astype(F32) for b in range(3)] + [tail], axis=0)
            block = jnp.concatenate([block, jnp.zeros((128, 32), F32)], axis=1)
            lanes = UNIT * (u % 4) + 128 * a
            packed[u // 4][:, lanes : lanes + 128] = block.T[:224].astype(BF)

    put(0, hyper_ref)
    outs = jnp.concatenate([out_ref[...].astype(F32), jnp.zeros((88, 224), F32)], axis=0)
    outs = jnp.concatenate([outs, jnp.zeros((128, 32), F32)], axis=1)
    packed[0][:, 2560:2688] = outs.T[:224].astype(BF)
    packed[0][:, 2688:] = jnp.zeros((224, 128), BF)
    for j in range(7):
        copies[j].wait()
        put(j + 1, blocks.at[j])
    for i in range(2):
        lanes = LANES[i] // 2
        near = pl.ds(pl.multiple_of(core * lanes, 128), lanes)
        away = pl.ds(pl.multiple_of((1 - core) * lanes, 128), lanes)
        own = pl.ds(pl.multiple_of(HALF * x_id, 16), HALF)
        theirs = pl.ds(pl.multiple_of(HALF * (1 - x_id), 16), HALF)
        keeps[i][...] = packed[i][own, near]
        keep_others[i][...] = packed[i][own, away]
        gives[i][...] = packed[i][theirs, near]


def pack(slice_order, hyper_weight, ctx_weight, ctx_bias, out_weight):
    ctx = jnp.transpose(ctx_weight[0], (0, 2, 1))
    hyper = jnp.transpose(hyper_weight[0], (0, 2, 1))
    shapes = [jax.ShapeDtypeStruct((HALF, LANES[i % 2] // 2), BF) for i in range(6)]
    return pl.pallas_call(
        pack_kernel,
        out_shape=shapes,
        in_specs=[SMEM, VMEM, ANY, VMEM, VMEM],
        out_specs=[VMEM] * 6,
        scratch_shapes=[
            pltpu.VMEM((7, 15, SW, 224), BF),
            pltpu.VMEM((224, LANES[0]), BF),
            pltpu.VMEM((224, LANES[1]), BF),
            pltpu.SemaphoreType.DMA((7,)),
        ],
        compiler_params=PARAMS,
        cost_estimate=COST,
        name="pack",
    )(slice_order, hyper, ctx, ctx_bias, out_weight[0])


def spread(keep, keep_other, give):
    got = x_swap(give)
    pair = jnp.concatenate([keep, got])
    up, down = from_y(pair, -1), from_y(pair, 1)
    far_own, far_other = from_y(up[:HALF], -1), from_y(down[HALF:], 1)
    mine = [pair, down, up, far_own, far_other]
    return mine + [keep_other, core_swap(got), core_swap(down), core_swap(up), core_swap(far_own), core_swap(far_other)]


def fetch_chunk(refs, slice_id, dest, sem):
    pair, down, up, far_own, far_other, keep_o, got_o, down_o, up_o, far_own_o, far_other_o = refs
    chan = lax.axis_index("chan")
    core = lax.axis_index("lon") % 2
    relative = (slice_id + 4 - chan % 4) % 4
    side = (slice_id // 4 + chan // 4) % 2
    lanes = pair.shape[1]
    mine = dest.at[:, pl.ds(pl.multiple_of(core * lanes, 128), lanes)]
    other = dest.at[:, pl.ds(pl.multiple_of((1 - core) * lanes, 128), lanes)]

    def rows(ref, i):
        return ref.at[pl.ds(i * HALF, HALF)]

    for i in range(2):
        choices = (
            (rows(pair, i), (keep_o, got_o)[i]),
            (rows(down, i), rows(down_o, i)),
            ((far_own, far_other)[i], (far_own_o, far_other_o)[i]),
            (rows(up, i), rows(up_o, i)),
        )
        for r, (first, second) in enumerate(choices):

            @pl.when((relative == r) & (side == i))
            def _(first=first, second=second):
                pltpu.make_async_copy(first, mine, sem.at[0]).start()
                pltpu.make_async_copy(second, other, sem.at[1]).start()

    def wait():
        pltpu.make_async_copy(far_own, mine, sem.at[0]).wait()
        pltpu.make_async_copy(far_own_o, other, sem.at[1]).wait()

    return wait


def rank_kernel(order_ref, recv_ref, ranked_ref, far_ref):
    for k in range(8):
        s = order_ref[k]

        @pl.loop(0, 8)
        def _(i, s=s, k=k):
            plane = recv_ref[s * 8 + i]
            ranked_ref[k * 8 + i] = plane
            if k % 4 < 2:
                far_ref[(k // 4 * 2 + k % 4) * 8 + i] = plane


def to_ranks(slice_order, recv):
    ranked, far = pl.pallas_call(
        rank_kernel,
        out_shape=[jax.ShapeDtypeStruct((64, SW, LAT), BF), jax.ShapeDtypeStruct((32, SW, LAT), BF)],
        in_specs=[SMEM, VMEM],
        out_specs=[VMEM] * 2,
        compiler_params=PARAMS,
        cost_estimate=COST,
        name="rank",
    )(slice_order, recv.reshape(64, SW, LAT))
    return ranked.reshape(8, 2, 4, SW, LAT), far.reshape(4, 2, 4, SW, LAT)


def stack_taps(plane, fill):
    lane = lax.broadcasted_iota(jnp.int32, plane.shape, 1)
    before = jnp.where(lane == 0, 0.0, pltpu.roll(plane, 1, 1))
    after = jnp.where(lane == LAT - 1, 0.0, pltpu.roll(plane, LAT - 1, 1))
    tail = jnp.full((8, LAT), fill, F32)
    return jnp.concatenate([before, plane, after, tail], axis=0).astype(BF)


def tap_pair(stack_ref, start):
    first = stack_ref[pl.ds(start, 5)].reshape(UNIT, LAT)
    second = stack_ref[pl.ds(start + 1, 5)].reshape(UNIT, LAT)
    return jnp.concatenate([first, second], axis=1)


def bands_of(k, halos):
    left2, left1, ranked, right1, right2 = halos
    if k % 4 < 2:
        j = k // 4 * 2 + k % 4
        return [(left2, j), (left1, k), (ranked, k), (right1, k), (right2, j)], -8
    return [(left1, k), (ranked, k), (right1, k)], -4


def band_spec(rank, kind):
    return pl.BlockSpec((1, 1, 4, SW, LAT), lambda i: (rank, kind, 0, 0, 0))


def whole(value):
    return pl.BlockSpec(value.shape, lambda i: (0,) * value.ndim)


def over_planes(bands, base, low, count, body):
    for b, band in enumerate(bands):
        first = max(0, low - base - 4 * b)
        last = min(4, low + count - base - 4 * b)
        if first < last:
            shift = base + 4 * b - low

            @pl.loop(first, last)
            def _(i, band=band, shift=shift):
                body(i + shift, band, i)


def early_kernel(rank, n_bands, base, low, n_chunks, n_prior, offsets, has_last, *refs):
    order_ref = refs[0]
    chunks = [refs[1 + 11 * i : 12 + 11 * i] for i in range(n_chunks)]
    at = 1 + 11 * n_chunks
    bands = refs[at : at + n_bands]
    at += n_bands
    priors = refs[at : at + n_prior]
    at += n_prior
    acc_ref, out_ref = refs[at : at + 2]
    at += 2
    if has_last:
        last_ref = refs[at]
        at += 1
    hyper_stack, weights, sems = refs[at], refs[at + 1 : at + 1 + n_chunks], refs[at + 1 + n_chunks]
    slice_id = order_ref[rank]
    waits = [fetch_chunk(chunks[i], slice_id, weights[i], sems.at[i]) for i in range(n_chunks)]

    def stack_hyper(place, band, i):
        hyper_stack[place] = stack_taps(band[0, 0, i].astype(F32), 1.0)

    over_planes(bands, base, low, hyper_stack.shape[0], stack_hyper)
    for wait in waits:
        wait()

    def weight(u):
        return weights[u // 4].at[:, pl.ds(UNIT * (u % 4), UNIT)]

    outs = weights[0][:, 2560:2688].astype(F32)
    outs = jnp.concatenate([outs, jnp.zeros((16, 128), F32)], axis=0)
    out_ref[...] = outs.T.astype(BF)
    if has_last:
        last_ref[...] = weight(n_prior + 1)[...]

    @pl.loop(0, acc_ref.shape[0])
    def _(p):
        total = jnp.dot(weight(0)[...], tap_pair(hyper_stack, 2 * p), preferred_element_type=F32)
        for j in range(n_prior):
            total = total + jnp.dot(
                weight(j + 1)[...],
                tap_pair(priors[j], 2 * p + offsets[j]),
                preferred_element_type=F32,
            )
        acc_ref[p] = total


def early(rank, slice_order, chunks, halos, stacks, has_last):
    reach = 2 * (3 - rank % 4)
    bands, base = bands_of(rank, halos)
    low, planes = -reach - 2, 8 + 2 * reach
    pairs = (planes - 4) // 2
    shapes = [jax.ShapeDtypeStruct((pairs, HALF, 2 * LAT), F32), jax.ShapeDtypeStruct((128, 128), BF)]
    if has_last:
        shapes.append(jax.ShapeDtypeStruct((HALF, UNIT), BF))
    offsets = [low - start for start, _ in stacks]
    priors = [stack for _, stack in stacks]
    return pl.pallas_call(
        functools.partial(
            early_kernel, rank, len(bands), base, low, len(chunks), len(priors), offsets, has_last
        ),
        grid=(1,),
        out_shape=shapes,
        in_specs=[SMEM]
        + [ANY] * (11 * len(chunks))
        + [band_spec(j, 1) for _, j in bands]
        + [whole(prior) for prior in priors],
        out_specs=[whole(shape) for shape in shapes],
        scratch_shapes=[pltpu.VMEM((planes, 128, LAT), BF)]
        + [pltpu.VMEM((HALF, LANES[i]), BF) for i in range(len(chunks))]
        + [pltpu.SemaphoreType.DMA((len(chunks), 2))],
        compiler_params=PARAMS,
        cost_estimate=COST,
        name="early",
    )(slice_order, *[ref for chunk in chunks for ref in chunk], *[band for band, _ in bands], *priors)


ERF_TOP = (0.00022905065861350646, 0.0034082910107109506, 0.050955695062380861, 0.18520832239976145, 1.128379143519084)
ERF_LOW = (-1.1791602954361697e-7, 0.000023547966471313185, 0.0010179625278914885, 0.014070470171167667, 0.11098505178285362, 0.49746925110067538, 1.0)


def gelu(v):
    z = jnp.clip(v * 0.7071067811865476, -3.7439211627767994, 3.7439211627767994)
    square = z * z
    top = jnp.full_like(z, ERF_TOP[0])
    for c in ERF_TOP[1:]:
        top = top * square + c
    low = jnp.full_like(z, ERF_LOW[0])
    for c in ERF_LOW[1:]:
        low = low * square + c
    half = 0.5 * v
    return half + half * (z * top / low)


def finish_kernel(kind, n_bands, base, low, *refs):
    acc_ref, out_ref = refs[:2]
    if kind == "newest":
        last_ref, own_ref, got_ref = refs[2:5]
        bands = refs[5 : 5 + n_bands]
        part_ref, value_ref, stack_ref = refs[5 + n_bands :]

        def decode(place, band, i):
            mean = own_ref[place].astype(F32) + got_ref[place].astype(F32)
            value = (band[0, 0, i].astype(F32) + mean).astype(BF)
            value_ref[place] = value
            stack_ref[place] = stack_taps(value.astype(F32), 0.0)

        over_planes(bands, base, low, own_ref.shape[0], decode)
    elif kind == "widened":
        last_ref = refs[2]
        part_ref, stack_ref = refs[8:]

        def widen(place, band, i):
            stack_ref[place] = stack_taps(band[0, i].astype(F32), 0.0)

        over_planes(refs[3:8], 0, 0, 20, widen)
    else:
        part_ref = refs[2]

    @pl.loop(0, acc_ref.shape[0])
    def _(p):
        total = acc_ref[p]
        if kind != "plain":
            total = total + jnp.dot(last_ref[...], tap_pair(stack_ref, 2 * p), preferred_element_type=F32)
        hidden = gelu(total).astype(BF)
        part = jnp.dot(out_ref[:SW, :HALF], hidden, preferred_element_type=F32).astype(BF)
        part_ref[2 * p] = part[:, :LAT]
        part_ref[2 * p + 1] = part[:, LAT:]


def finish(kind, acc, outs, *more, rank=None, halos=None):
    lons = 2 * acc.shape[0]
    shapes = [jax.ShapeDtypeStruct((lons, SW, LAT), BF)]
    operands = [acc, outs, *more]
    specs = [whole(value) for value in operands]
    bands, base, low = [], 0, 0
    if kind == "newest":
        bands, base = bands_of(rank, halos)
        low = -2 * (3 - rank % 4)
        operands += [band for band, _ in bands]
        specs += [band_spec(j, 0) for _, j in bands]
        shapes.append(jax.ShapeDtypeStruct(more[1].shape, BF))
        shapes.append(jax.ShapeDtypeStruct((more[1].shape[0], 128, LAT), BF))
    elif kind == "widened":
        shapes.append(jax.ShapeDtypeStruct((20, 128, LAT), BF))
    return pl.pallas_call(
        functools.partial(finish_kernel, kind, len(bands), base, low),
        grid=(1,),
        out_shape=shapes,
        in_specs=specs,
        out_specs=[whole(shape) for shape in shapes],
        compiler_params=PARAMS,
        cost_estimate=COST,
        name="finish",
    )(*operands)


def widen_kernel(*refs):
    stacks = refs[5:]
    for j, stack_ref in enumerate(stacks):

        def widen(place, band, i, j=j, stack_ref=stack_ref):
            stack_ref[place] = stack_taps(band[j, i].astype(F32), 0.0)

        over_planes(refs[:5], 0, 0, 20, widen)


def widen(bands):
    return pl.pallas_call(
        widen_kernel,
        out_shape=[jax.ShapeDtypeStruct((20, 128, LAT), BF)] * 3,
        in_specs=[VMEM] * 5,
        out_specs=[VMEM] * 3,
        compiler_params=PARAMS,
        cost_estimate=COST,
        name="widen",
    )(*bands)


TAPS = (((1, 0),), ((2, 0), (0, 1)))


def upsample_kernel(
    order_ref, beta_ref, gamma_ref, weight_ref,
    own_a, own_b, own_c, own_d, up_a, up_b, up_c, up_d,
    out0, out1, out2, out3, fields, normed, shifted, totals,
):
    for level, (first, second, third, fourth) in enumerate(
        ((own_a, own_b, own_c, own_d), (up_a, up_b, up_c, up_d))
    ):
        for k in range(8):
            rows = pl.ds(pl.multiple_of(order_ref[k] * SW, 8), SW)
            for x in range(5):
                if k < 4:
                    plane = first[k, x]
                elif k < 7:
                    plane = second[k - 4, x]
                elif x < 4:
                    plane = third[x]
                else:
                    plane = fourth[0]
                fields[level, x, rows, :] = plane.astype(F32)
    gamma = gamma_ref[...].astype(BF)
    lane = lax.broadcasted_iota(jnp.int32, (320, LAT), 1)

    for level in range(2):

        @pl.loop(0, 5)
        def _(x, level=level):
            value = fields[level, x]
            energy = jnp.dot(gamma, (value * value).astype(BF), preferred_element_type=F32)
            field = (value * jnp.sqrt(energy + beta_ref[...])).astype(BF)
            normed[level, x] = field
            later = pltpu.roll(field.astype(F32), LAT - 1, 1)
            shifted[level, x] = jnp.where(lane == LAT - 1, 0.0, later).astype(BF)

    started = set()
    for dl in range(2):
        for dx in range(2):
            for dt in range(2):
                pars, rows = [], []
                for p in range(2):
                    for q in range(2):
                        for r in range(2):
                            for kl, ol in TAPS[p]:
                                for kx, ox in TAPS[q]:
                                    for kt, ot in TAPS[r]:
                                        if (ol, ox, ot) == (dl, dx, dt):
                                            tap = kl * 9 + kx * 3 + kt
                                            pars.append(4 * p + 2 * q + r)
                                            rows.append(weight_ref[32 * tap : 32 * tap + 32, :])
                source = (normed, shifted)[dt]
                field = jnp.concatenate([source[dl, dx + x] for x in range(4)], axis=1)
                got = jnp.dot(jnp.concatenate(rows, axis=0), field, preferred_element_type=F32)
                for i, par in enumerate(pars):
                    piece = got[32 * i : 32 * i + 32]
                    if par in started:
                        totals[par] += piece
                    else:
                        totals[par] = piece
                        started.add(par)
    source = lax.broadcasted_iota(jnp.int32, (2 * LAT, 2 * LAT), 0)
    target = lax.broadcasted_iota(jnp.int32, (2 * LAT, 2 * LAT), 1)
    mixing = (target == jnp.where(source < LAT, 2 * source, 2 * source - 2 * LAT + 1)).astype(F32).astype(BF)
    for p in range(2):
        rows = []
        for x in range(4):
            for q in range(2):
                even = totals[4 * p + 2 * q, :, LAT * x : LAT * x + LAT]
                odd = totals[4 * p + 2 * q + 1, :, LAT * x : LAT * x + LAT]
                rows.append(jnp.concatenate([even, odd], axis=1))
        mixed = jnp.dot(jnp.concatenate(rows, axis=0).astype(BF), mixing, preferred_element_type=F32)
        mixed = mixed.reshape(8, 4, 8, 2 * LAT)
        for relative, out_ref in enumerate((out0, out1, out2, out3)):
            out_ref[:, p] = jnp.transpose(mixed[:, relative], (1, 0, 2)).astype(BF)


def upsample(slice_order, beta, gamma, weight, own, up):
    shape = jax.ShapeDtypeStruct((8, 2, 8, 2 * LAT), BF)
    return pl.pallas_call(
        upsample_kernel,
        out_shape=[shape] * 4,
        in_specs=[SMEM] + [VMEM] * 11,
        out_specs=[VMEM] * 4,
        scratch_shapes=[
            pltpu.VMEM((2, 5, 320, LAT), F32),
            pltpu.VMEM((2, 5, 320, LAT), BF),
            pltpu.VMEM((2, 5, 320, LAT), BF),
            pltpu.VMEM((8, 32, 4 * LAT), F32),
        ],
        compiler_params=PARAMS,
        cost_estimate=COST,
        name="upsample",
    )(slice_order, beta, gamma, weight, *own, *up)


def place_kernel(in0, in1, in2, in3, out_ref):
    y_id = lax.axis_index("chan") % 4
    for relative, in_ref in enumerate((in0, in1, in2, in3)):
        level = (y_id + 4 - relative) % 4
        for o in range(8):
            for p in range(2):
                out_ref[o, 2 * level + p] = in_ref[o, p]


def place(pieces):
    return pl.pallas_call(
        place_kernel,
        out_shape=jax.ShapeDtypeStruct((8, 8, 8, 2 * LAT), BF),
        in_specs=[VMEM] * 4,
        out_specs=VMEM,
        compiler_params=PARAMS,
        cost_estimate=COST,
        name="place",
    )(*pieces)


def local(
    symbols,
    hyper_mean,
    slice_order,
    hyper_weight,
    ctx_weight,
    ctx_bias,
    out_weight,
    gdn_beta,
    gdn_gamma,
    tconv_weight,
):
    both = jnp.stack([symbols.astype(BF), hyper_mean])
    send = jnp.transpose(both, (2, 0, 3, 1, 4))
    recv = lax.all_to_all(jnp.concatenate([send, send]), "chan", 0, 0)
    keep_a, keep_b, rest_a, rest_b, give_a, give_b = pack(
        slice_order, hyper_weight, ctx_weight, ctx_bias, out_weight
    )
    chunks = [spread(keep_a, rest_a, give_a), spread(keep_b, rest_b, give_b)]
    ranked, far = to_ranks(slice_order, recv)
    halos = (from_lon(far, -2), from_lon(ranked, -1), ranked, from_lon(ranked, 1), from_lon(far, 2))
    weight = jnp.stack([from_y(tconv_weight, r) if r else tconv_weight for r in range(4)], axis=1)

    values, stacks, part = [], [], None
    for k in range(8):
        has_last = k > 0
        acc, outs, *last = early(
            k, slice_order, chunks[: 1 + (k >= 4)], halos, stacks[: max(k - 1, 0)], has_last
        )
        if k == 0:
            (part,) = finish("plain", acc, outs)
        elif k == 4:
            part, stack = finish("widened", acc, outs, last[0], *wide_last)
            stacks.append((-8, stack))
        else:
            part, value, stack = finish(
                "newest", acc, outs, last[0], part, x_swap(part), rank=k - 1, halos=halos
            )
            values.append(value)
            stacks.append((-2 * (3 - (k - 1) % 4), stack))
        if k == 3:
            mean = part.astype(F32) + x_swap(part).astype(F32)
            newest = (ranked[k, 0].astype(F32) + mean).astype(BF)
            done = jnp.stack([v[v.shape[0] // 2 - 2 : v.shape[0] // 2 + 2] for v in values])
            wide = [from_lon(done, d) if d else done for d in (-2, -1, 0, 1, 2)]
            stacks = [(-8, stack) for stack in widen(wide)]
            newest = newest[None]
            wide_last = [from_lon(newest, d) if d else newest for d in (-2, -1, 0, 1, 2)]
            own_a = jnp.concatenate(
                [
                    jnp.concatenate([done, newest]),
                    jnp.concatenate([wide[3][:, :1], wide_last[3][:, :1]]),
                ],
                axis=1,
            )
    mean = part.astype(F32) + x_swap(part).astype(F32)
    own_c = (ranked[7, 0].astype(F32) + mean).astype(BF)
    own_b = jnp.stack([v[v.shape[0] // 2 - 2 : v.shape[0] // 2 + 3] for v in values[3:]])
    edge = own_c[:1]
    down = [(i + 1, i) for i in range(8) if i % 4 < 3]
    corner = [(i * 32 + (j + 1) % 32, (i - 1) * 32 + j) for i in range(8) if i % 4 > 0 for j in range(32)]
    own = [own_a, own_b, own_c, from_lon(edge, 1)]
    up = [lax.ppermute(v, "chan", down) for v in own[:3]] + [lax.ppermute(edge, ("chan", "lon"), corner)]
    pieces = upsample(
        slice_order, gdn_beta[:, None], gdn_gamma, weight.reshape(27 * 32, 320), own, up
    )
    return place([from_y(v, -r) if r else v for r, v in enumerate(pieces)])


def solution(mesh):
    placed = (
        P("chan", None, "lon", None),
        P("chan", None, "lon", None),
        P(),
        P("chan", None, None, None),
        P("chan", None, None, None),
        P("chan", None),
        P("chan", None, None),
        P(),
        P(),
        P(None, "chan", None),
    )
    return jax.shard_map(
        local, mesh=mesh, in_specs=placed, out_specs=P("chan", None, "lon", None), check_vma=False
    )
```

```python
import functools
import jax
import jax.numpy as jnp
from jax import lax
from jax.experimental import pallas as pl
from jax.experimental.pallas import tpu as pltpu
from jax.sharding import PartitionSpec as P

BF = jnp.bfloat16
F32 = jnp.float32
SW = 40
HALF = 112
LAT = 128
UNIT = 640
LANES = 5376
NEAR = LANES // 2
KEEP = 144
ANY = pl.BlockSpec(memory_space=pl.ANY)
VMEM = pl.BlockSpec(memory_space=pltpu.VMEM)
HBM = pl.BlockSpec(memory_space=pltpu.HBM)
SMEM = pl.BlockSpec(memory_space=pltpu.SMEM)
COST = pl.CostEstimate(flops=200_000_000, bytes_accessed=1 << 20, transcendentals=0)
PARAMS = pltpu.CompilerParams(vmem_limit_bytes=48 << 20)


def x_swap(value):
    return lax.ppermute(value, "chan", [(i, i ^ 4) for i in range(8)])


def core_swap(value):
    return lax.ppermute(value, "lon", [(i, i ^ 1) for i in range(32)])


def from_y(value, distance):
    return lax.ppermute(
        value, "chan", [(i, (i // 4) * 4 + (i - distance) % 4) for i in range(8)]
    )


def from_lon(value, distance):
    return lax.ppermute(value, "lon", [(i, (i - distance) % 32) for i in range(32)])


def pack_kernel(order_ref, bias_ref, hyper_hbm, ctx_hbm, out_hbm, tconv_hbm, keep, keep_other, give, hyper_ref, out_ref, blocks, packed, sem):
    x_id = lax.axis_index("chan") // 4
    core = lax.axis_index("lon") % 2
    first = [
        pltpu.make_async_copy(hyper_hbm, hyper_ref, sem.at[7]),
        pltpu.make_async_copy(out_hbm, out_ref, sem.at[8]),
        pltpu.make_async_copy(tconv_hbm, keep.at[HALF:], sem.at[9]),
    ]
    for copy in first:
        copy.start()
    copies = []
    for j in range(7):
        rows = pl.ds(pl.multiple_of(order_ref[j] * SW, 8), SW)
        copies.append(pltpu.make_async_copy(ctx_hbm.at[:, rows, :], blocks.at[j], sem.at[j]))
        copies[-1].start()
    bias = bias_ref[...]
    high = bias.astype(BF).astype(F32)
    mid = (bias - high).astype(BF).astype(F32)
    low = (bias - high - mid).astype(BF).astype(F32)
    parts = jnp.concatenate([high, mid, low, jnp.zeros((5, 224), F32)], axis=0)

    def put(u, taps):
        for a in range(5):
            tail = parts if u == 0 and a == 2 else jnp.zeros((8, 224), F32)
            block = jnp.concatenate([taps[3 * a + b].astype(F32) for b in range(3)] + [tail], axis=0)
            block = jnp.concatenate([block, jnp.zeros((128, 32), F32)], axis=1)
            lanes = UNIT * u + 128 * a
            packed[:, lanes : lanes + 128] = block.T[:224].astype(BF)

    packed[:, 8 * UNIT + 128 :] = jnp.zeros((224, 128), BF)
    first[0].wait()
    put(0, hyper_ref)
    first[1].wait()
    outs = jnp.concatenate([out_ref[...].astype(F32), jnp.zeros((88, 224), F32)], axis=0)
    outs = jnp.concatenate([outs, jnp.zeros((128, 32), F32)], axis=1)
    packed[:, 8 * UNIT : 8 * UNIT + 128] = outs.T[:224].astype(BF)
    for j in range(7):
        copies[j].wait()
        put(j + 1, blocks.at[j])
    near = pl.ds(pl.multiple_of(core * NEAR, 128), NEAR)
    away = pl.ds(pl.multiple_of((1 - core) * NEAR, 128), NEAR)
    own = pl.ds(pl.multiple_of(HALF * x_id, 16), HALF)
    theirs = pl.ds(pl.multiple_of(HALF * (1 - x_id), 16), HALF)
    keep[:HALF] = packed[own, near]
    keep_other[...] = packed[own, away]
    give[...] = packed[theirs, near]
    first[2].wait()


def pack(slice_order, hyper_weight, ctx_weight, ctx_bias, out_weight, tconv_weight):
    ctx = jnp.transpose(ctx_weight[0], (0, 2, 1))
    hyper = jnp.transpose(hyper_weight[0], (0, 2, 1))
    tconv = jnp.pad(tconv_weight.reshape(27, 2560), ((0, 5), (0, NEAR - 2560)))
    return pl.pallas_call(
        pack_kernel,
        out_shape=[jax.ShapeDtypeStruct((rows, NEAR), BF) for rows in (KEEP, HALF, HALF)],
        in_specs=[SMEM, VMEM, HBM, HBM, HBM, HBM],
        out_specs=[VMEM] * 3,
        scratch_shapes=[
            pltpu.VMEM((15, SW, 224), BF),
            pltpu.VMEM((SW, 224), BF),
            pltpu.VMEM((7, 15, SW, 224), BF),
            pltpu.VMEM((224, LANES), BF),
            pltpu.SemaphoreType.DMA((10,)),
        ],
        compiler_params=PARAMS,
        cost_estimate=COST,
        name="pack",
    )(slice_order, ctx_bias, hyper, ctx, out_weight[0], tconv)


def spread(keep, keep_other, give):
    up_k, down_k = from_y(keep, -1), from_y(keep, 1)
    got = x_swap(give)
    far_k = from_y(up_k, -1)
    up_g, down_g = from_y(got, -1), from_y(got, 1)
    far_g = from_y(down_g, 1)
    got_o = core_swap(got)
    near_k_o = core_swap(jnp.concatenate([up_k, down_k]))
    near_g_o = core_swap(jnp.concatenate([up_g, down_g]))
    far_o = core_swap(jnp.concatenate([far_k, far_g]))
    rows = [v[HALF : HALF + 27, :2560].reshape(27, 8, 320) for v in (keep, down_k, far_k, up_k)]
    tconv = jnp.stack(rows, axis=1).reshape(27 * 32, 320)
    mine = [keep, got, down_k, down_g, up_k, up_g, far_k, far_g]
    return mine + [keep_other, got_o, near_k_o, near_g_o, far_o], tconv


def fetch_weights(refs, slice_id, dest, sem):
    keep, got, down_k, down_g, up_k, up_g, far_k, far_g, keep_o, got_o, near_k_o, near_g_o, far_o = refs
    chan = lax.axis_index("chan")
    core = lax.axis_index("lon") % 2
    relative = (slice_id + 4 - chan % 4) % 4
    side = (slice_id // 4 + chan // 4) % 2
    mine = dest.at[:, pl.ds(pl.multiple_of(core * NEAR, 128), NEAR)]
    other = dest.at[:, pl.ds(pl.multiple_of((1 - core) * NEAR, 128), NEAR)]

    def rows(ref, start):
        return ref.at[pl.ds(start, HALF)]

    choices = {
        (0, 0): (rows(keep, 0), keep_o),
        (0, 1): (got, got_o),
        (1, 0): (rows(down_k, 0), rows(near_k_o, KEEP)),
        (1, 1): (down_g, rows(near_g_o, HALF)),
        (2, 0): (rows(far_k, 0), rows(far_o, 0)),
        (2, 1): (far_g, rows(far_o, KEEP)),
        (3, 0): (rows(up_k, 0), rows(near_k_o, 0)),
        (3, 1): (up_g, rows(near_g_o, 0)),
    }
    for (r, i), (first, second) in choices.items():

        @pl.when((relative == r) & (side == i))
        def _(first=first, second=second):
            pltpu.make_async_copy(first, mine, sem.at[0]).start()
            pltpu.make_async_copy(second, other, sem.at[1]).start()

    def wait():
        pltpu.make_async_copy(got, mine, sem.at[0]).wait()
        pltpu.make_async_copy(got_o, other, sem.at[1]).wait()

    return wait


def rank_kernel(order_ref, recv_ref, ranked_ref, far_ref):
    for k in range(8):
        s = order_ref[k]

        @pl.loop(0, 8)
        def _(i, s=s, k=k):
            plane = recv_ref[s * 8 + i]
            ranked_ref[k * 8 + i] = plane
            if k % 4 < 2:
                far_ref[(k // 4 * 2 + k % 4) * 8 + i] = plane


def to_ranks(slice_order, recv):
    ranked, far = pl.pallas_call(
        rank_kernel,
        out_shape=[jax.ShapeDtypeStruct((64, SW, LAT), BF), jax.ShapeDtypeStruct((32, SW, LAT), BF)],
        in_specs=[SMEM, VMEM],
        out_specs=[VMEM] * 2,
        compiler_params=PARAMS,
        cost_estimate=COST,
        name="rank",
    )(slice_order, recv.reshape(64, SW, LAT))
    return ranked.reshape(8, 2, 4, SW, LAT), far.reshape(4, 2, 4, SW, LAT)


def stack_taps(plane, fill):
    lane = lax.broadcasted_iota(jnp.int32, plane.shape, 1)
    before = jnp.where(lane == 0, 0.0, pltpu.roll(plane, 1, 1))
    after = jnp.where(lane == LAT - 1, 0.0, pltpu.roll(plane, LAT - 1, 1))
    tail = jnp.full((8, LAT), fill, F32)
    return jnp.concatenate([before, plane, after, tail], axis=0).astype(BF)


def tap_group(stack_ref, start):
    longitudes = [stack_ref[pl.ds(start + i, 5)].reshape(UNIT, LAT) for i in range(4)]
    return jnp.concatenate(longitudes, axis=1)


def bands_of(k, halos):
    left2, left1, ranked, right1, right2 = halos
    if k % 4 < 2:
        j = k // 4 * 2 + k % 4
        return [(left2, j), (left1, k), (ranked, k), (right1, k), (right2, j)], -8
    return [(left1, k), (ranked, k), (right1, k)], -4


def band_spec(rank, kind):
    return pl.BlockSpec((1, 1, 4, SW, LAT), lambda i: (rank, kind, 0, 0, 0))


def whole(value):
    return pl.BlockSpec(value.shape, lambda i: (0,) * value.ndim)


def over_planes(bands, base, low, count, body):
    for b, band in enumerate(bands):
        for i in range(4):
            spot = base + 4 * b + i - low
            if 0 <= spot < count:
                body(spot, band, i)


def early_kernel(rank, n_bands, base, low, n_prior, offsets, n_last, *refs):
    order_ref = refs[0]
    chunks = refs[1:14]
    bands = refs[14 : 14 + n_bands]
    at = 14 + n_bands
    prior_hbm = refs[at : at + n_prior]
    at += n_prior
    acc_ref, out_ref = refs[at : at + 2]
    at += 2
    if n_last:
        last_ref = refs[at]
        at += 1
    hyper_stack, weights = refs[at : at + 2]
    priors, sem = refs[at + 2 : at + 2 + n_prior], refs[at + 2 + n_prior]
    wait = fetch_weights(chunks, order_ref[rank], weights, sem)
    planes = hyper_stack.shape[0]
    copies = []
    for j in range(n_prior):
        copies.append(
            pltpu.make_async_copy(prior_hbm[j].at[pl.ds(offsets[j], planes)], priors[j], sem.at[2 + j])
        )
        copies[-1].start()

    def stack_hyper(place, band, i):
        hyper_stack[place] = stack_taps(band[0, 0, i].astype(F32), 1.0)

    over_planes(bands, base, low, planes, stack_hyper)
    wait()
    outs = weights[:, 8 * UNIT : 8 * UNIT + 128].astype(F32)
    outs = jnp.concatenate([outs, jnp.zeros((16, 128), F32)], axis=0)
    out_ref[...] = outs.T.astype(BF)
    if n_last:
        last_ref[...] = weights[:, UNIT * (n_prior + 1) : UNIT * (n_prior + 1 + n_last)]
    for copy in copies:
        copy.wait()

    @pl.loop(0, acc_ref.shape[0])
    def _(p):
        total = jnp.dot(weights[:, :UNIT], tap_group(hyper_stack, 4 * p), preferred_element_type=F32)
        for j in range(n_prior):
            total = total + jnp.dot(
                weights[:, UNIT * (j + 1) : UNIT * (j + 2)],
                tap_group(priors[j], 4 * p),
                preferred_element_type=F32,
            )
        acc_ref[p] = total


def early(rank, slice_order, chunks, halos, stacks, n_last):
    reach = 2 * (3 - rank % 4)
    bands, base = bands_of(rank, halos)
    low, planes = -reach - 2, 8 + 2 * reach
    groups = (planes - 4) // 4
    shapes = [jax.ShapeDtypeStruct((groups, HALF, 4 * LAT), F32), jax.ShapeDtypeStruct((128, 128), BF)]
    if n_last:
        shapes.append(jax.ShapeDtypeStruct((HALF, UNIT * n_last), BF))
    offsets = [low - start for start, _ in stacks]
    priors = [stack for _, stack in stacks]
    return pl.pallas_call(
        functools.partial(early_kernel, rank, len(bands), base, low, len(priors), offsets, n_last),
        grid=(1,),
        out_shape=shapes,
        in_specs=[SMEM] + [ANY] * 13 + [band_spec(j, 1) for _, j in bands] + [HBM] * len(priors),
        out_specs=[whole(shape) for shape in shapes],
        scratch_shapes=[pltpu.VMEM((planes, 128, LAT), BF), pltpu.VMEM((HALF, LANES), BF)]
        + [pltpu.VMEM((planes, 128, LAT), BF)] * len(priors)
        + [pltpu.SemaphoreType.DMA((2 + len(priors),))],
        compiler_params=PARAMS,
        cost_estimate=COST,
        name="early",
    )(slice_order, *chunks, *[band for band, _ in bands], *priors)


ERF_TOP = (0.00022905065861350646, 0.0034082910107109506, 0.050955695062380861, 0.18520832239976145, 1.128379143519084)
ERF_LOW = (-1.1791602954361697e-7, 0.000023547966471313185, 0.0010179625278914885, 0.014070470171167667, 0.11098505178285362, 0.49746925110067538, 1.0)


def gelu(v):
    z = jnp.clip(v * 0.7071067811865476, -3.7439211627767994, 3.7439211627767994)
    square = z * z
    top = jnp.full_like(z, ERF_TOP[0])
    for c in ERF_TOP[1:]:
        top = top * square + c
    low = jnp.full_like(z, ERF_LOW[0])
    for c in ERF_LOW[1:]:
        low = low * square + c
    half = 0.5 * v
    return half + half * (z * top / low)


def finish_kernel(kind, n_bands, base, low, *refs):
    acc_hbm, out_ref = refs[:2]
    acc_ref, sem = refs[-2:]
    refs = refs[2:-2]
    copy = pltpu.make_async_copy(acc_hbm, acc_ref, sem)
    copy.start()
    stacks = []
    if kind == "newest":
        last_ref, own_ref, got_ref = refs[:3]
        bands = refs[3 : 3 + n_bands]
        part_ref, value_ref, stack_ref = refs[3 + n_bands :]
        stacks = [stack_ref]

        def decode(place, band, i):
            mean = own_ref[place].astype(F32) + got_ref[place].astype(F32)
            value = (band[0, 0, i].astype(F32) + mean).astype(BF)
            value_ref[place] = value
            stack_ref[place] = stack_taps(value.astype(F32), 0.0)

        over_planes(bands, base, low, own_ref.shape[0], decode)
    elif kind == "widened":
        last_ref = refs[0]
        part_ref, *stacks = refs[6:]
        widen_bands(refs[1:6], stacks)
    else:
        part_ref = refs[0]
    copy.wait()

    @pl.loop(0, acc_ref.shape[0])
    def _(p):
        total = acc_ref[p]
        for j, stack_ref in enumerate(stacks):
            total = total + jnp.dot(
                last_ref[:, UNIT * j : UNIT * (j + 1)], tap_group(stack_ref, 4 * p), preferred_element_type=F32
            )
        for h in range(2):
            hidden = gelu(total[:, 2 * LAT * h : 2 * LAT * (h + 1)]).astype(BF)
            part = jnp.dot(out_ref[:SW, :HALF], hidden, preferred_element_type=F32).astype(BF)
            part_ref[4 * p + 2 * h] = part[:, :LAT]
            part_ref[4 * p + 2 * h + 1] = part[:, LAT:]


def finish(kind, acc, outs, *more, rank=None, halos=None):
    lons = 4 * acc.shape[0]
    shapes = [jax.ShapeDtypeStruct((lons, SW, LAT), BF)]
    operands = [acc, outs, *more]
    specs = [HBM] + [whole(value) for value in operands[1:]]
    bands, base, low = [], 0, 0
    if kind == "newest":
        bands, base = bands_of(rank, halos)
        low = -2 * (3 - rank % 4)
        operands += [band for band, _ in bands]
        specs += [band_spec(j, 0) for _, j in bands]
        shapes.append(jax.ShapeDtypeStruct(more[1].shape, BF))
        shapes.append(jax.ShapeDtypeStruct((more[1].shape[0], 128, LAT), BF))
    elif kind == "widened":
        shapes += [jax.ShapeDtypeStruct((20, 128, LAT), BF)] * 2
    return pl.pallas_call(
        functools.partial(finish_kernel, kind, len(bands), base, low),
        grid=(1,),
        out_shape=shapes,
        in_specs=specs,
        out_specs=[whole(shape) for shape in shapes],
        scratch_shapes=[pltpu.VMEM(acc.shape, F32), pltpu.SemaphoreType.DMA],
        compiler_params=PARAMS,
        cost_estimate=COST,
        name="finish",
    )(*operands)


def widen_bands(bands, stacks):
    for j, stack_ref in enumerate(stacks):

        def widen(place, band, i, j=j, stack_ref=stack_ref):
            stack_ref[place] = stack_taps(band[j, i].astype(F32), 0.0)

        over_planes(bands, 0, 0, 20, widen)


def widen_kernel(*refs):
    widen_bands(refs[:5], refs[5:])


def widen(bands):
    return pl.pallas_call(
        widen_kernel,
        out_shape=[jax.ShapeDtypeStruct((20, 128, LAT), BF)] * 2,
        in_specs=[VMEM] * 5,
        out_specs=[VMEM] * 2,
        compiler_params=PARAMS,
        cost_estimate=COST,
        name="widen",
    )(*bands)


TAPS = (((1, 0),), ((2, 0), (0, 1)))


def upsample_kernel(
    order_ref, beta_ref, gamma_ref, weight_ref,
    own_a, own_b, own_c, up_a, up_b, up_c,
    out0, out1, out2, out3, fields, normed, shifted, totals,
):
    for level, (first, second, third) in enumerate(((own_a, own_b, own_c), (up_a, up_b, up_c))):
        for k in range(8):
            rows = pl.ds(pl.multiple_of(order_ref[k] * SW, 8), SW)
            for x in range(5):
                if k < 7:
                    plane = first[k, x]
                elif x < 4:
                    plane = second[x]
                else:
                    plane = third[0]
                fields[level, x, rows, :] = plane.astype(F32)
    gamma = gamma_ref[...].astype(BF)
    lane = lax.broadcasted_iota(jnp.int32, (320, LAT), 1)

    for level in range(2):

        @pl.loop(0, 5)
        def _(x, level=level):
            value = fields[level, x]
            energy = jnp.dot(gamma, (value * value).astype(BF), preferred_element_type=F32)
            field = (value * jnp.sqrt(energy + beta_ref[...])).astype(BF)
            normed[level, x] = field
            later = pltpu.roll(field.astype(F32), LAT - 1, 1)
            shifted[level, x] = jnp.where(lane == LAT - 1, 0.0, later).astype(BF)

    started = set()
    for dl in range(2):
        for dx in range(2):
            for dt in range(2):
                pars, rows = [], []
                for p in range(2):
                    for q in range(2):
                        for r in range(2):
                            for kl, ol in TAPS[p]:
                                for kx, ox in TAPS[q]:
                                    for kt, ot in TAPS[r]:
                                        if (ol, ox, ot) == (dl, dx, dt):
                                            tap = kl * 9 + kx * 3 + kt
                                            pars.append(4 * p + 2 * q + r)
                                            rows.append(weight_ref[32 * tap : 32 * tap + 32, :])
                source = (normed, shifted)[dt]
                field = jnp.concatenate([source[dl, dx + x] for x in range(4)], axis=1)
                got = jnp.dot(jnp.concatenate(rows, axis=0), field, preferred_element_type=F32)
                for i, par in enumerate(pars):
                    piece = got[32 * i : 32 * i + 32]
                    if par in started:
                        totals[par] += piece
                    else:
                        totals[par] = piece
                        started.add(par)
    source = lax.broadcasted_iota(jnp.int32, (2 * LAT, 2 * LAT), 0)
    target = lax.broadcasted_iota(jnp.int32, (2 * LAT, 2 * LAT), 1)
    mixing = (target == jnp.where(source < LAT, 2 * source, 2 * source - 2 * LAT + 1)).astype(F32).astype(BF)
    for p in range(2):
        rows = []
        for x in range(4):
            for q in range(2):
                even = totals[4 * p + 2 * q, :, LAT * x : LAT * x + LAT]
                odd = totals[4 * p + 2 * q + 1, :, LAT * x : LAT * x + LAT]
                rows.append(jnp.concatenate([even, odd], axis=1))
        mixed = jnp.dot(jnp.concatenate(rows, axis=0).astype(BF), mixing, preferred_element_type=F32)
        mixed = mixed.reshape(8, 4, 8, 2 * LAT)
        for relative, out_ref in enumerate((out0, out1, out2, out3)):
            out_ref[:, p] = jnp.transpose(mixed[:, relative], (1, 0, 2)).astype(BF)


def upsample(slice_order, beta, gamma, weight, own, up):
    shape = jax.ShapeDtypeStruct((8, 2, 8, 2 * LAT), BF)
    return pl.pallas_call(
        upsample_kernel,
        out_shape=[shape] * 4,
        in_specs=[SMEM] + [VMEM] * 9,
        out_specs=[VMEM] * 4,
        scratch_shapes=[
            pltpu.VMEM((2, 5, 320, LAT), F32),
            pltpu.VMEM((2, 5, 320, LAT), BF),
            pltpu.VMEM((2, 5, 320, LAT), BF),
            pltpu.VMEM((8, 32, 4 * LAT), F32),
        ],
        compiler_params=PARAMS,
        cost_estimate=COST,
        name="upsample",
    )(slice_order, beta, gamma, weight, *own, *up)


def place_kernel(in0, in1, in2, in3, out_ref):
    y_id = lax.axis_index("chan") % 4
    for relative, in_ref in enumerate((in0, in1, in2, in3)):
        level = (y_id + 4 - relative) % 4
        for o in range(8):
            for p in range(2):
                out_ref[o, 2 * level + p] = in_ref[o, p]


def place(pieces):
    return pl.pallas_call(
        place_kernel,
        out_shape=jax.ShapeDtypeStruct((8, 8, 8, 2 * LAT), BF),
        in_specs=[VMEM] * 4,
        out_specs=VMEM,
        compiler_params=PARAMS,
        cost_estimate=COST,
        name="place",
    )(*pieces)


def local(
    symbols,
    hyper_mean,
    slice_order,
    hyper_weight,
    ctx_weight,
    ctx_bias,
    out_weight,
    gdn_beta,
    gdn_gamma,
    tconv_weight,
):
    both = jnp.stack([symbols.astype(BF), hyper_mean])
    send = jnp.transpose(both, (2, 0, 3, 1, 4))
    recv = lax.all_to_all(jnp.concatenate([send, send]), "chan", 0, 0)
    chunks, tconv = spread(
        *pack(slice_order, hyper_weight, ctx_weight, ctx_bias, out_weight, tconv_weight)
    )
    ranked, far = to_ranks(slice_order, recv)
    halos = (from_lon(far, -2), from_lon(ranked, -1), ranked, from_lon(ranked, 1), from_lon(far, 2))

    def centre(value, count):
        start = value.shape[0] // 2 - 2
        return value[start : start + count]

    def around(value):
        return [from_lon(value, d) if d else value for d in (-2, -1, 0, 1, 2)]

    values, stacks, part = [], [], None
    for k in range(8):
        if k == 4:
            stacks = [(-8, stack) for stack in widen(wide_first)]
            acc, outs, last = early(k, slice_order, chunks, halos, stacks, 2)
            part, *more = finish("widened", acc, outs, last, *wide_second)
            stacks += [(-8, stack) for stack in more]
        elif k == 0:
            acc, outs = early(k, slice_order, chunks, halos, [], 0)
            (part,) = finish("plain", acc, outs)
        else:
            acc, outs, last = early(k, slice_order, chunks, halos, stacks, 1)
            part, value, stack = finish(
                "newest", acc, outs, last, part, x_swap(part), rank=k - 1, halos=halos
            )
            values.append(value)
            stacks.append((-2 * (3 - (k - 1) % 4), stack))
        if k == 2:
            wide_first = around(jnp.stack([centre(value, 4) for value in values]))
        if k == 3:
            mean = part.astype(F32) + x_swap(part).astype(F32)
            newest = (ranked[k, 0].astype(F32) + mean).astype(BF)
            wide_second = around(jnp.stack([centre(values[2], 4), newest]))
    blocks = [jnp.concatenate([w[2], w[3][:, :1]], axis=1) for w in (wide_first, wide_second)]
    blocks.append(jnp.stack([centre(value, 5) for value in values[3:]]))
    own_a = jnp.concatenate(blocks)
    mean = part.astype(F32) + x_swap(part).astype(F32)
    own_b = (ranked[7, 0].astype(F32) + mean).astype(BF)
    edge = own_b[:1]
    down = [(i + 1, i) for i in range(8) if i % 4 < 3]
    corner = [(i * 32 + (j + 1) % 32, (i - 1) * 32 + j) for i in range(8) if i % 4 > 0 for j in range(32)]
    own = [own_a, own_b, from_lon(edge, 1)]
    up = [lax.ppermute(v, "chan", down) for v in own[:2]] + [lax.ppermute(edge, ("chan", "lon"), corner)]
    pieces = upsample(slice_order, gdn_beta[:, None], gdn_gamma, tconv, own, up)
    return place([from_y(v, -r) if r else v for r, v in enumerate(pieces)])


def solution(mesh):
    placed = (
        P("chan", None, "lon", None),
        P("chan", None, "lon", None),
        P(),
        P("chan", None, None, None),
        P("chan", None, None, None),
        P("chan", None),
        P("chan", None, None),
        P(),
        P(),
        P(None, "chan", None),
    )
    return jax.shard_map(
        local, mesh=mesh, in_specs=placed, out_specs=P("chan", None, "lon", None), check_vma=False
    )
```

```python
import functools
import jax
import jax.numpy as jnp
from jax import lax
from jax.experimental import pallas as pl
from jax.experimental.pallas import tpu as pltpu
from jax.sharding import PartitionSpec as P

BF = jnp.bfloat16
F32 = jnp.float32
SW = 40
HALF = 112
LAT = 128
UNIT = 640
LANES = 5376
NEAR = LANES // 2
KEEP = 144
ANY = pl.BlockSpec(memory_space=pl.ANY)
VMEM = pl.BlockSpec(memory_space=pltpu.VMEM)
HBM = pl.BlockSpec(memory_space=pltpu.HBM)
SMEM = pl.BlockSpec(memory_space=pltpu.SMEM)
COST = pl.CostEstimate(flops=200_000_000, bytes_accessed=1 << 20, transcendentals=0)
PARAMS = pltpu.CompilerParams(vmem_limit_bytes=16 << 20)


def x_swap(value):
    return lax.ppermute(value, "chan", [(i, i ^ 4) for i in range(8)])


def core_swap(value):
    return lax.ppermute(value, "lon", [(i, i ^ 1) for i in range(32)])


def from_y(value, distance):
    return lax.ppermute(
        value, "chan", [(i, (i // 4) * 4 + (i - distance) % 4) for i in range(8)]
    )


def from_lon(value, distance):
    return lax.ppermute(value, "lon", [(i, (i - distance) % 32) for i in range(32)])


def pack_kernel(order_ref, bias_ref, hyper_hbm, ctx_hbm, out_hbm, tconv_hbm, keep, keep_other, give, hyper_ref, out_ref, blocks, packed, sem):
    x_id = lax.axis_index("chan") // 4
    core = lax.axis_index("lon") % 2
    first = [
        pltpu.make_async_copy(hyper_hbm, hyper_ref, sem.at[7]),
        pltpu.make_async_copy(out_hbm, out_ref, sem.at[8]),
        pltpu.make_async_copy(tconv_hbm, keep.at[HALF:], sem.at[9]),
    ]
    for copy in first:
        copy.start()
    copies = []
    for j in range(7):
        rows = pl.ds(pl.multiple_of(order_ref[j] * SW, 8), SW)
        copies.append(pltpu.make_async_copy(ctx_hbm.at[:, rows, :], blocks.at[j], sem.at[j]))
        copies[-1].start()
    bias = bias_ref[...]
    high = bias.astype(BF).astype(F32)
    mid = (bias - high).astype(BF).astype(F32)
    low = (bias - high - mid).astype(BF).astype(F32)
    parts = jnp.concatenate([high, mid, low, jnp.zeros((5, 224), F32)], axis=0)

    def put(u, taps):
        for a in range(5):
            tail = parts if u == 0 and a == 2 else jnp.zeros((8, 224), F32)
            block = jnp.concatenate([taps[3 * a + b].astype(F32) for b in range(3)] + [tail], axis=0)
            block = jnp.concatenate([block, jnp.zeros((128, 32), F32)], axis=1)
            lanes = UNIT * u + 128 * a
            packed[:, lanes : lanes + 128] = block.T[:224].astype(BF)

    packed[:, 8 * UNIT + 128 :] = jnp.zeros((224, 128), BF)
    first[0].wait()
    put(0, hyper_ref)
    first[1].wait()
    outs = jnp.concatenate([out_ref[...].astype(F32), jnp.zeros((88, 224), F32)], axis=0)
    outs = jnp.concatenate([outs, jnp.zeros((128, 32), F32)], axis=1)
    packed[:, 8 * UNIT : 8 * UNIT + 128] = outs.T[:224].astype(BF)
    for j in range(7):
        copies[j].wait()
        put(j + 1, blocks.at[j])
    near = pl.ds(pl.multiple_of(core * NEAR, 128), NEAR)
    away = pl.ds(pl.multiple_of((1 - core) * NEAR, 128), NEAR)
    own = pl.ds(pl.multiple_of(HALF * x_id, 16), HALF)
    theirs = pl.ds(pl.multiple_of(HALF * (1 - x_id), 16), HALF)
    keep[:HALF] = packed[own, near]
    keep_other[...] = packed[own, away]
    give[...] = packed[theirs, near]
    first[2].wait()


def pack(slice_order, hyper_weight, ctx_weight, ctx_bias, out_weight, tconv_weight):
    ctx = jnp.transpose(ctx_weight[0], (0, 2, 1))
    hyper = jnp.transpose(hyper_weight[0], (0, 2, 1))
    tconv = jnp.pad(tconv_weight.reshape(27, 2560), ((0, 5), (0, NEAR - 2560)))
    return pl.pallas_call(
        pack_kernel,
        out_shape=[jax.ShapeDtypeStruct((rows, NEAR), BF) for rows in (KEEP, HALF, HALF)],
        in_specs=[SMEM, VMEM, HBM, HBM, HBM, HBM],
        out_specs=[VMEM] * 3,
        scratch_shapes=[
            pltpu.VMEM((15, SW, 224), BF),
            pltpu.VMEM((SW, 224), BF),
            pltpu.VMEM((7, 15, SW, 224), BF),
            pltpu.VMEM((224, LANES), BF),
            pltpu.SemaphoreType.DMA((10,)),
        ],
        compiler_params=pltpu.CompilerParams(vmem_limit_bytes=60 << 20),
        cost_estimate=COST,
        name="pack",
    )(slice_order, ctx_bias, hyper, ctx, out_weight[0], tconv)


def tie(*values):
    return lax.optimization_barrier(values)


def spread(keep, keep_other, give, recv, slice_order):
    up_k, down_k = from_y(keep, -1), from_y(keep, 1)
    got = x_swap(give)
    ranked, far = to_ranks(slice_order, recv)
    halos = [from_lon(far, -2), from_lon(ranked, -1), ranked, from_lon(ranked, 1), from_lon(far, 2)]
    got, ranked = tie(got, ranked)
    far_k = from_y(up_k, -1)
    up_g, down_g = from_y(got, -1), from_y(got, 1)
    got_o = core_swap(got)
    near_k_o = core_swap(jnp.concatenate([up_k, down_k]))
    rows = [v[HALF : HALF + 27, :2560].reshape(27, 8, 320) for v in (keep, down_k, far_k, up_k)]
    tconv = jnp.stack(rows, axis=1).reshape(27 * 32, 320)
    up_g, down_g, got_o, near_k_o, tconv, *halos = tie(up_g, down_g, got_o, near_k_o, tconv, *halos)
    far_g = from_y(down_g, 1)
    near_g_o = core_swap(jnp.concatenate([up_g, down_g]))
    far_o = core_swap(jnp.concatenate([far_k, far_g]))
    mine = [keep, got, down_k, down_g, up_k, up_g, far_k, far_g]
    return mine + [keep_other, got_o, near_k_o, near_g_o, far_o], tconv, halos


def fetch_weights(refs, slice_id, dest, sem):
    keep, got, down_k, down_g, up_k, up_g, far_k, far_g, keep_o, got_o, near_k_o, near_g_o, far_o = refs
    chan = lax.axis_index("chan")
    core = lax.axis_index("lon") % 2
    relative = (slice_id + 4 - chan % 4) % 4
    side = (slice_id // 4 + chan // 4) % 2
    mine = dest.at[:, pl.ds(pl.multiple_of(core * NEAR, 128), NEAR)]
    other = dest.at[:, pl.ds(pl.multiple_of((1 - core) * NEAR, 128), NEAR)]

    def rows(ref, start):
        return ref.at[pl.ds(start, HALF)]

    choices = {
        (0, 0): (rows(keep, 0), keep_o),
        (0, 1): (got, got_o),
        (1, 0): (rows(down_k, 0), rows(near_k_o, KEEP)),
        (1, 1): (down_g, rows(near_g_o, HALF)),
        (2, 0): (rows(far_k, 0), rows(far_o, 0)),
        (2, 1): (far_g, rows(far_o, KEEP)),
        (3, 0): (rows(up_k, 0), rows(near_k_o, 0)),
        (3, 1): (up_g, rows(near_g_o, 0)),
    }
    for (r, i), (first, second) in choices.items():

        @pl.when((relative == r) & (side == i))
        def _(first=first, second=second):
            pltpu.make_async_copy(first, mine, sem.at[0]).start()
            pltpu.make_async_copy(second, other, sem.at[1]).start()

    def wait():
        pltpu.make_async_copy(got, mine, sem.at[0]).wait()
        pltpu.make_async_copy(got_o, other, sem.at[1]).wait()

    return wait


def rank_kernel(order_ref, recv_ref, ranked_ref, far_ref):
    for k in range(8):
        s = order_ref[k]

        @pl.loop(0, 8)
        def _(i, s=s, k=k):
            plane = recv_ref[s * 8 + i]
            ranked_ref[k * 8 + i] = plane
            if k % 4 < 2:
                far_ref[(k // 4 * 2 + k % 4) * 8 + i] = plane


def to_ranks(slice_order, recv):
    ranked, far = pl.pallas_call(
        rank_kernel,
        out_shape=[jax.ShapeDtypeStruct((64, SW, LAT), BF), jax.ShapeDtypeStruct((32, SW, LAT), BF)],
        in_specs=[SMEM, VMEM],
        out_specs=[VMEM] * 2,
        compiler_params=PARAMS,
        cost_estimate=COST,
        name="rank",
    )(slice_order, recv.reshape(64, SW, LAT))
    return ranked.reshape(8, 2, 4, SW, LAT), far.reshape(4, 2, 4, SW, LAT)


def stack_taps(plane, fill):
    lane = lax.broadcasted_iota(jnp.int32, plane.shape, 1)
    before = jnp.where(lane == 0, 0.0, pltpu.roll(plane, 1, 1))
    after = jnp.where(lane == LAT - 1, 0.0, pltpu.roll(plane, LAT - 1, 1))
    tail = jnp.full((8, LAT), fill, F32)
    return jnp.concatenate([before, plane, after, tail], axis=0).astype(BF)


def tap_group(stack_ref, start):
    longitudes = [stack_ref[pl.ds(start + i, 5)].reshape(UNIT, LAT) for i in range(4)]
    return jnp.concatenate(longitudes, axis=1)


def bands_of(k, halos):
    left2, left1, ranked, right1, right2 = halos
    if k % 4 < 2:
        j = k // 4 * 2 + k % 4
        return [(left2, j), (left1, k), (ranked, k), (right1, k), (right2, j)], -8
    return [(left1, k), (ranked, k), (right1, k)], -4


def band_spec(rank, kind):
    return pl.BlockSpec((1, 1, 4, SW, LAT), lambda i: (rank, kind, 0, 0, 0))


def whole(value):
    return pl.BlockSpec(value.shape, lambda i: (0,) * value.ndim)


def over_planes(bands, base, low, count, body):
    for b, band in enumerate(bands):
        for i in range(4):
            spot = base + 4 * b + i - low
            if 0 <= spot < count:
                body(spot, band, i)


def early_kernel(rank, n_bands, base, low, n_prior, offsets, n_last, *refs):
    order_ref = refs[0]
    chunks = refs[1:14]
    bands = refs[14 : 14 + n_bands]
    at = 14 + n_bands
    prior_hbm = refs[at : at + n_prior]
    at += n_prior
    acc_ref, out_ref = refs[at : at + 2]
    at += 2
    if n_last:
        last_ref = refs[at]
        at += 1
    hyper_stack, weights = refs[at : at + 2]
    priors, sem = refs[at + 2 : at + 2 + n_prior], refs[at + 2 + n_prior]
    wait = fetch_weights(chunks, order_ref[rank], weights, sem)
    planes = hyper_stack.shape[0]
    copies = []
    for j in range(n_prior):
        copies.append(
            pltpu.make_async_copy(prior_hbm[j].at[pl.ds(offsets[j], planes)], priors[j], sem.at[2 + j])
        )
        copies[-1].start()

    def stack_hyper(place, band, i):
        hyper_stack[place] = stack_taps(band[0, 0, i].astype(F32), 1.0)

    over_planes(bands, base, low, planes, stack_hyper)
    wait()
    outs = weights[:, 8 * UNIT : 8 * UNIT + 128].astype(F32)
    outs = jnp.concatenate([outs, jnp.zeros((16, 128), F32)], axis=0)
    out_ref[...] = outs.T.astype(BF)
    if n_last:
        last_ref[...] = weights[:, UNIT * (n_prior + 1) : UNIT * (n_prior + 1 + n_last)]
    for copy in copies:
        copy.wait()

    @pl.loop(0, acc_ref.shape[0])
    def _(p):
        total = jnp.dot(weights[:, :UNIT], tap_group(hyper_stack, 4 * p), preferred_element_type=F32)
        for j in range(n_prior):
            total = total + jnp.dot(
                weights[:, UNIT * (j + 1) : UNIT * (j + 2)],
                tap_group(priors[j], 4 * p),
                preferred_element_type=F32,
            )
        acc_ref[p] = total


def early(rank, slice_order, chunks, halos, stacks, n_last):
    reach = 2 * (3 - rank % 4)
    bands, base = bands_of(rank, halos)
    low, planes = -reach - 2, 8 + 2 * reach
    groups = (planes - 4) // 4
    shapes = [jax.ShapeDtypeStruct((groups, HALF, 4 * LAT), F32), jax.ShapeDtypeStruct((128, 128), BF)]
    if n_last:
        shapes.append(jax.ShapeDtypeStruct((HALF, UNIT * n_last), BF))
    offsets = [low - start for start, _ in stacks]
    priors = [stack for _, stack in stacks]
    return pl.pallas_call(
        functools.partial(early_kernel, rank, len(bands), base, low, len(priors), offsets, n_last),
        grid=(1,),
        out_shape=shapes,
        in_specs=[SMEM] + [ANY] * 13 + [band_spec(j, 1) for _, j in bands] + [HBM] * len(priors),
        out_specs=[whole(shape) for shape in shapes],
        scratch_shapes=[pltpu.VMEM((planes, 128, LAT), BF), pltpu.VMEM((HALF, LANES), BF)]
        + [pltpu.VMEM((planes, 128, LAT), BF)] * len(priors)
        + [pltpu.SemaphoreType.DMA((2 + len(priors),))],
        compiler_params=PARAMS,
        cost_estimate=COST,
        name="early",
    )(slice_order, *chunks, *[band for band, _ in bands], *priors)


ERF_TOP = (0.00022905065861350646, 0.0034082910107109506, 0.050955695062380861, 0.18520832239976145, 1.128379143519084)
ERF_LOW = (-1.1791602954361697e-7, 0.000023547966471313185, 0.0010179625278914885, 0.014070470171167667, 0.11098505178285362, 0.49746925110067538, 1.0)


def gelu(v):
    z = jnp.clip(v * 0.7071067811865476, -3.7439211627767994, 3.7439211627767994)
    square = z * z
    top = jnp.full_like(z, ERF_TOP[0])
    for c in ERF_TOP[1:]:
        top = top * square + c
    low = jnp.full_like(z, ERF_LOW[0])
    for c in ERF_LOW[1:]:
        low = low * square + c
    half = 0.5 * v
    return half + half * (z * top / low)


def finish_kernel(kind, n_bands, base, low, *refs):
    acc_hbm, out_ref = refs[:2]
    acc_ref, sem = refs[-2:]
    refs = refs[2:-2]
    copy = pltpu.make_async_copy(acc_hbm, acc_ref, sem)
    copy.start()
    stacks = []
    if kind == "newest":
        last_ref, own_ref, got_ref = refs[:3]
        bands = refs[3 : 3 + n_bands]
        part_ref, value_ref, stack_ref = refs[3 + n_bands :]
        stacks = [stack_ref]

        def decode(place, band, i):
            mean = own_ref[place].astype(F32) + got_ref[place].astype(F32)
            value = (band[0, 0, i].astype(F32) + mean).astype(BF)
            value_ref[place] = value
            stack_ref[place] = stack_taps(value.astype(F32), 0.0)

        over_planes(bands, base, low, own_ref.shape[0], decode)
    elif kind == "widened":
        last_ref = refs[0]
        part_ref, *stacks = refs[6:]
        widen_bands(refs[1:6], stacks)
    else:
        part_ref = refs[0]
    copy.wait()

    @pl.loop(0, acc_ref.shape[0])
    def _(p):
        total = acc_ref[p]
        for j, stack_ref in enumerate(stacks):
            total = total + jnp.dot(
                last_ref[:, UNIT * j : UNIT * (j + 1)], tap_group(stack_ref, 4 * p), preferred_element_type=F32
            )
        for h in range(2):
            hidden = gelu(total[:, 2 * LAT * h : 2 * LAT * (h + 1)]).astype(BF)
            part = jnp.dot(out_ref[:SW, :HALF], hidden, preferred_element_type=F32).astype(BF)
            part_ref[4 * p + 2 * h] = part[:, :LAT]
            part_ref[4 * p + 2 * h + 1] = part[:, LAT:]


def finish(kind, acc, outs, *more, rank=None, halos=None):
    lons = 4 * acc.shape[0]
    shapes = [jax.ShapeDtypeStruct((lons, SW, LAT), BF)]
    operands = [acc, outs, *more]
    specs = [HBM] + [whole(value) for value in operands[1:]]
    bands, base, low = [], 0, 0
    if kind == "newest":
        bands, base = bands_of(rank, halos)
        low = -2 * (3 - rank % 4)
        operands += [band for band, _ in bands]
        specs += [band_spec(j, 0) for _, j in bands]
        shapes.append(jax.ShapeDtypeStruct(more[1].shape, BF))
        shapes.append(jax.ShapeDtypeStruct((more[1].shape[0], 128, LAT), BF))
    elif kind == "widened":
        shapes += [jax.ShapeDtypeStruct((20, 128, LAT), BF)] * 2
    return pl.pallas_call(
        functools.partial(finish_kernel, kind, len(bands), base, low),
        grid=(1,),
        out_shape=shapes,
        in_specs=specs,
        out_specs=[whole(shape) for shape in shapes],
        scratch_shapes=[pltpu.VMEM(acc.shape, F32), pltpu.SemaphoreType.DMA],
        compiler_params=PARAMS,
        cost_estimate=COST,
        name="finish",
    )(*operands)


def widen_bands(bands, stacks):
    for j, stack_ref in enumerate(stacks):

        def widen(place, band, i, j=j, stack_ref=stack_ref):
            stack_ref[place] = stack_taps(band[j, i].astype(F32), 0.0)

        over_planes(bands, 0, 0, 20, widen)


def widen_kernel(*refs):
    widen_bands(refs[:5], refs[5:])


def widen(bands):
    return pl.pallas_call(
        widen_kernel,
        out_shape=[jax.ShapeDtypeStruct((20, 128, LAT), BF)] * 2,
        in_specs=[VMEM] * 5,
        out_specs=[VMEM] * 2,
        compiler_params=PARAMS,
        cost_estimate=COST,
        name="widen",
    )(*bands)


TAPS = (((1, 0),), ((2, 0), (0, 1)))


def upsample_kernel(
    order_ref, beta_ref, gamma_ref, weight_ref,
    own_a, own_b, own_c, up_a, up_b, up_c,
    out0, out1, out2, out3, fields, normed, shifted, totals,
):
    for level, (first, second, third) in enumerate(((own_a, own_b, own_c), (up_a, up_b, up_c))):
        for k in range(8):
            rows = pl.ds(pl.multiple_of(order_ref[k] * SW, 8), SW)
            for x in range(5):
                if k < 7:
                    plane = first[k, x]
                elif x < 4:
                    plane = second[x]
                else:
                    plane = third[0]
                fields[level, x, rows, :] = plane.astype(F32)
    gamma = gamma_ref[...].astype(BF)
    lane = lax.broadcasted_iota(jnp.int32, (320, LAT), 1)

    for level in range(2):

        @pl.loop(0, 5)
        def _(x, level=level):
            value = fields[level, x]
            energy = jnp.dot(gamma, (value * value).astype(BF), preferred_element_type=F32)
            field = (value * jnp.sqrt(energy + beta_ref[...])).astype(BF)
            normed[level, x] = field
            later = pltpu.roll(field.astype(F32), LAT - 1, 1)
            shifted[level, x] = jnp.where(lane == LAT - 1, 0.0, later).astype(BF)

    started = set()
    for dl in range(2):
        for dx in range(2):
            for dt in range(2):
                pars, rows = [], []
                for p in range(2):
                    for q in range(2):
                        for r in range(2):
                            for kl, ol in TAPS[p]:
                                for kx, ox in TAPS[q]:
                                    for kt, ot in TAPS[r]:
                                        if (ol, ox, ot) == (dl, dx, dt):
                                            tap = kl * 9 + kx * 3 + kt
                                            pars.append(4 * p + 2 * q + r)
                                            rows.append(weight_ref[32 * tap : 32 * tap + 32, :])
                source = (normed, shifted)[dt]
                field = jnp.concatenate([source[dl, dx + x] for x in range(4)], axis=1)
                got = jnp.dot(jnp.concatenate(rows, axis=0), field, preferred_element_type=F32)
                for i, par in enumerate(pars):
                    piece = got[32 * i : 32 * i + 32]
                    if par in started:
                        totals[par] += piece
                    else:
                        totals[par] = piece
                        started.add(par)
    source = lax.broadcasted_iota(jnp.int32, (2 * LAT, 2 * LAT), 0)
    target = lax.broadcasted_iota(jnp.int32, (2 * LAT, 2 * LAT), 1)
    mixing = (target == jnp.where(source < LAT, 2 * source, 2 * source - 2 * LAT + 1)).astype(F32).astype(BF)
    for p in range(2):
        rows = []
        for x in range(4):
            for q in range(2):
                even = totals[4 * p + 2 * q, :, LAT * x : LAT * x + LAT]
                odd = totals[4 * p + 2 * q + 1, :, LAT * x : LAT * x + LAT]
                rows.append(jnp.concatenate([even, odd], axis=1))
        mixed = jnp.dot(jnp.concatenate(rows, axis=0).astype(BF), mixing, preferred_element_type=F32)
        mixed = mixed.reshape(8, 4, 8, 2 * LAT)
        for relative, out_ref in enumerate((out0, out1, out2, out3)):
            out_ref[:, p] = jnp.transpose(mixed[:, relative], (1, 0, 2)).astype(BF)


def upsample(slice_order, beta, gamma, weight, own, up):
    shape = jax.ShapeDtypeStruct((8, 2, 8, 2 * LAT), BF)
    return pl.pallas_call(
        upsample_kernel,
        out_shape=[shape] * 4,
        in_specs=[SMEM] + [VMEM] * 9,
        out_specs=[VMEM] * 4,
        scratch_shapes=[
            pltpu.VMEM((2, 5, 320, LAT), F32),
            pltpu.VMEM((2, 5, 320, LAT), BF),
            pltpu.VMEM((2, 5, 320, LAT), BF),
            pltpu.VMEM((8, 32, 4 * LAT), F32),
        ],
        compiler_params=PARAMS,
        cost_estimate=COST,
        name="upsample",
    )(slice_order, beta, gamma, weight, *own, *up)


def place_kernel(in0, in1, in2, in3, out_ref):
    y_id = lax.axis_index("chan") % 4
    for relative, in_ref in enumerate((in0, in1, in2, in3)):
        level = (y_id + 4 - relative) % 4
        for o in range(8):
            for p in range(2):
                out_ref[o, 2 * level + p] = in_ref[o, p]


def place(pieces):
    return pl.pallas_call(
        place_kernel,
        out_shape=jax.ShapeDtypeStruct((8, 8, 8, 2 * LAT), BF),
        in_specs=[VMEM] * 4,
        out_specs=VMEM,
        compiler_params=PARAMS,
        cost_estimate=COST,
        name="place",
    )(*pieces)


def local(
    symbols,
    hyper_mean,
    slice_order,
    hyper_weight,
    ctx_weight,
    ctx_bias,
    out_weight,
    gdn_beta,
    gdn_gamma,
    tconv_weight,
):
    both = jnp.stack([symbols.astype(BF), hyper_mean])
    send = jnp.transpose(both, (2, 0, 3, 1, 4))
    send, pack_order = tie(jnp.concatenate([send, send]), slice_order)
    recv = lax.all_to_all(send, "chan", 0, 0)
    packed = pack(pack_order, hyper_weight, ctx_weight, ctx_bias, out_weight, tconv_weight)
    chunks, tconv, halos = spread(*packed, recv, slice_order)
    ranked = halos[2]

    def centre(value, count):
        start = value.shape[0] // 2 - 2
        return value[start : start + count]

    def around(value):
        return [from_lon(value, d) if d else value for d in (-2, -1, 0, 1, 2)]

    values, stacks, part = [], [], None
    for k in range(8):
        if k == 4:
            stacks = [(-8, stack) for stack in widen(wide_first)]
            acc, outs, last = early(k, slice_order, chunks, halos, stacks, 2)
            part, *more = finish("widened", acc, outs, last, *wide_second)
            stacks += [(-8, stack) for stack in more]
        elif k == 0:
            acc, outs = early(k, slice_order, chunks, halos, [], 0)
            (part,) = finish("plain", acc, outs)
        else:
            acc, outs, last = early(k, slice_order, chunks, halos, stacks, 1)
            part, value, stack = finish(
                "newest", acc, outs, last, part, x_swap(part), rank=k - 1, halos=halos
            )
            values.append(value)
            stacks.append((-2 * (3 - (k - 1) % 4), stack))
        if k == 2:
            wide_first = around(jnp.stack([centre(value, 4) for value in values]))
        if k == 3:
            mean = part.astype(F32) + x_swap(part).astype(F32)
            newest = (ranked[k, 0].astype(F32) + mean).astype(BF)
            wide_second = around(jnp.stack([centre(values[2], 4), newest]))
    blocks = [jnp.concatenate([w[2], w[3][:, :1]], axis=1) for w in (wide_first, wide_second)]
    blocks.append(jnp.stack([centre(value, 5) for value in values[3:]]))
    own_a = jnp.concatenate(blocks)
    mean = part.astype(F32) + x_swap(part).astype(F32)
    own_b = (ranked[7, 0].astype(F32) + mean).astype(BF)
    edge = own_b[:1]
    down = [(i + 1, i) for i in range(8) if i % 4 < 3]
    corner = [(i * 32 + (j + 1) % 32, (i - 1) * 32 + j) for i in range(8) if i % 4 > 0 for j in range(32)]
    own = [own_a, own_b, from_lon(edge, 1)]
    up = [lax.ppermute(v, "chan", down) for v in own[:2]] + [lax.ppermute(edge, ("chan", "lon"), corner)]
    pieces = upsample(slice_order, gdn_beta[:, None], gdn_gamma, tconv, own, up)
    return place([from_y(v, -r) if r else v for r, v in enumerate(pieces)])


def solution(mesh):
    placed = (
        P("chan", None, "lon", None),
        P("chan", None, "lon", None),
        P(),
        P("chan", None, None, None),
        P("chan", None, None, None),
        P("chan", None),
        P("chan", None, None),
        P(),
        P(),
        P(None, "chan", None),
    )
    return jax.shard_map(
        local, mesh=mesh, in_specs=placed, out_specs=P("chan", None, "lon", None), check_vma=False
    )
```

```python
import functools
import jax
import jax.numpy as jnp
from jax import lax
from jax.experimental import pallas as pl
from jax.experimental.pallas import tpu as pltpu
from jax.sharding import PartitionSpec as P

BF = jnp.bfloat16
F32 = jnp.float32
SW = 40
HALF = 112
LAT = 128
UNIT = 640
LANES = (2816, 2560)
ANY = pl.BlockSpec(memory_space=pl.ANY)
VMEM = pl.BlockSpec(memory_space=pltpu.VMEM)
HBM = pl.BlockSpec(memory_space=pltpu.HBM)
SMEM = pl.BlockSpec(memory_space=pltpu.SMEM)
COST = pl.CostEstimate(flops=200_000_000, bytes_accessed=1 << 20, transcendentals=0)
PARAMS = pltpu.CompilerParams(vmem_limit_bytes=16 << 20)


def x_swap(value):
    return lax.ppermute(value, "chan", [(i, i ^ 4) for i in range(8)])


def core_swap(value):
    return lax.ppermute(value, "lon", [(i, i ^ 1) for i in range(32)])


def from_y(value, distance):
    return lax.ppermute(
        value, "chan", [(i, (i // 4) * 4 + (i - distance) % 4) for i in range(8)]
    )


def from_lon(value, distance):
    return lax.ppermute(value, "lon", [(i, (i - distance) % 32) for i in range(32)])


def pack_kernel(chunk, order_ref, bias_ref, hyper_hbm, ctx_hbm, out_hbm, keep, keep_other, give, hyper_ref, out_ref, blocks, packed, sem):
    x_id = lax.axis_index("chan") // 4
    core = lax.axis_index("lon") % 2
    copies = []
    if chunk == 0:
        copies += [
            pltpu.make_async_copy(hyper_hbm, hyper_ref, sem.at[4]),
            pltpu.make_async_copy(out_hbm, out_ref, sem.at[5]),
        ]
    for j in range(3 + chunk):
        rows = pl.ds(pl.multiple_of(order_ref[3 * chunk + j] * SW, 8), SW)
        copies.append(pltpu.make_async_copy(ctx_hbm.at[:, rows, :], blocks.at[j], sem.at[j]))
    for copy in copies:
        copy.start()

    def put(u, taps, parts=None):
        for a in range(5):
            tail = jnp.zeros((8, 224), F32) if parts is None or a != 2 else parts
            block = jnp.concatenate([taps[3 * a + b].astype(F32) for b in range(3)] + [tail], axis=0)
            block = jnp.concatenate([block, jnp.zeros((128, 32), F32)], axis=1)
            lanes = UNIT * u + 128 * a
            packed[:, lanes : lanes + 128] = block.T[:224].astype(BF)

    if chunk == 0:
        bias = bias_ref[...]
        high = bias.astype(BF).astype(F32)
        mid = (bias - high).astype(BF).astype(F32)
        low = (bias - high - mid).astype(BF).astype(F32)
        copies.pop(0).wait()
        put(0, hyper_ref, jnp.concatenate([high, mid, low, jnp.zeros((5, 224), F32)], axis=0))
        copies.pop(0).wait()
        outs = jnp.concatenate([out_ref[...].astype(F32), jnp.zeros((88, 224), F32)], axis=0)
        outs = jnp.concatenate([outs, jnp.zeros((128, 32), F32)], axis=1)
        packed[:, 4 * UNIT : 4 * UNIT + 128] = outs.T[:224].astype(BF)
        packed[:, 4 * UNIT + 128 :] = jnp.zeros((224, 128), BF)
    for j, copy in enumerate(copies):
        copy.wait()
        put(1 - chunk + j, blocks.at[j])
    lanes = LANES[chunk] // 2
    near = pl.ds(pl.multiple_of(core * lanes, 128), lanes)
    away = pl.ds(pl.multiple_of((1 - core) * lanes, 128), lanes)
    own = pl.ds(pl.multiple_of(HALF * x_id, 16), HALF)
    theirs = pl.ds(pl.multiple_of(HALF * (1 - x_id), 16), HALF)
    keep[...] = packed[own, near]
    keep_other[...] = packed[own, away]
    give[...] = packed[theirs, near]


def pack(chunk, slice_order, hyper_weight, ctx_weight, ctx_bias, out_weight):
    ctx = jnp.transpose(ctx_weight[0], (0, 2, 1))
    hyper = jnp.transpose(hyper_weight[0], (0, 2, 1))
    return pl.pallas_call(
        functools.partial(pack_kernel, chunk),
        out_shape=[jax.ShapeDtypeStruct((HALF, LANES[chunk] // 2), BF)] * 3,
        in_specs=[SMEM, VMEM, HBM, HBM, HBM],
        out_specs=[VMEM] * 3,
        scratch_shapes=[
            pltpu.VMEM((15, SW, 224), BF),
            pltpu.VMEM((SW, 224), BF),
            pltpu.VMEM((4, 15, SW, 224), BF),
            pltpu.VMEM((224, LANES[chunk]), BF),
            pltpu.SemaphoreType.DMA((6,)),
        ],
        compiler_params=pltpu.CompilerParams(vmem_limit_bytes=(60, 16)[chunk] << 20),
        cost_estimate=COST,
        name="pack",
    )(slice_order, ctx_bias, hyper, ctx, out_weight[0])


def tie(*values):
    return lax.optimization_barrier(values)


def first_spread(keep, keep_other, give, recv, slice_order):
    up_k, down_k = from_y(keep, -1), from_y(keep, 1)
    got = x_swap(give)
    ranked, far = to_ranks(slice_order, recv)
    up_k, down_k, got, ranked, far = tie(up_k, down_k, got, ranked, far)
    up_g, down_g = from_y(got, -1), from_y(got, 1)
    far_k = from_y(up_k, -1)
    left2, right2 = from_lon(far, -2), from_lon(far, 2)
    up_g, down_g, far_k, left2, right2 = tie(up_g, down_g, far_k, left2, right2)
    far_g = from_y(down_g, 1)
    left1, right1 = from_lon(ranked, -1), from_lon(ranked, 1)
    near_o = core_swap(jnp.concatenate([up_k, up_g, down_k, down_g, got]))
    far_o = core_swap(jnp.concatenate([far_k, far_g]))
    chunk = [keep, got, up_k, up_g, down_k, down_g, far_k, far_g, keep_other, near_o, far_o]
    return chunk, (left2, left1, ranked, right1, right2)


def chunk_views(chunk, refs):
    def rows(ref, i):
        return ref.at[pl.ds(HALF * i, HALF)]

    if chunk == 0:
        views = refs[:8]
        keep_o, near_o, far_o = refs[8:]
    else:
        pair, up, down, far_k, far_g, keep_o, near_o, far_o = refs
        views = [rows(ref, i) for ref in (pair, up, down) for i in range(2)] + [far_k, far_g]
    keep, got, up_k, up_g, down_k, down_g, far_k, far_g = views
    return {
        (0, 0): (keep, keep_o),
        (0, 1): (got, rows(near_o, 4)),
        (1, 0): (down_k, rows(near_o, 2)),
        (1, 1): (down_g, rows(near_o, 3)),
        (2, 0): (far_k, rows(far_o, 0)),
        (2, 1): (far_g, rows(far_o, 1)),
        (3, 0): (up_k, rows(near_o, 0)),
        (3, 1): (up_g, rows(near_o, 1)),
    }


def fetch_weights(chunk_id, refs, slice_id, dest, sem):
    chan = lax.axis_index("chan")
    core = lax.axis_index("lon") % 2
    relative = (slice_id + 4 - chan % 4) % 4
    side = (slice_id // 4 + chan // 4) % 2
    lanes = LANES[chunk_id] // 2
    mine = dest.at[:, pl.ds(pl.multiple_of(core * lanes, 128), lanes)]
    other = dest.at[:, pl.ds(pl.multiple_of((1 - core) * lanes, 128), lanes)]
    choices = chunk_views(chunk_id, refs)
    for (r, i), (first, second) in choices.items():

        @pl.when((relative == r) & (side == i))
        def _(first=first, second=second):
            pltpu.make_async_copy(first, mine, sem.at[0]).start()
            pltpu.make_async_copy(second, other, sem.at[1]).start()

    def wait():
        pltpu.make_async_copy(choices[2, 0][0], mine, sem.at[0]).wait()
        pltpu.make_async_copy(choices[0, 0][1], other, sem.at[1]).wait()

    return wait


def rank_kernel(order_ref, recv_ref, ranked_ref, far_ref):
    for k in range(8):
        s = order_ref[k]

        @pl.loop(0, 8)
        def _(i, s=s, k=k):
            plane = recv_ref[s * 8 + i]
            ranked_ref[k * 8 + i] = plane
            if k % 4 < 2:
                far_ref[(k // 4 * 2 + k % 4) * 8 + i] = plane


def to_ranks(slice_order, recv):
    ranked, far = pl.pallas_call(
        rank_kernel,
        out_shape=[jax.ShapeDtypeStruct((64, SW, LAT), BF), jax.ShapeDtypeStruct((32, SW, LAT), BF)],
        in_specs=[SMEM, VMEM],
        out_specs=[VMEM] * 2,
        compiler_params=PARAMS,
        cost_estimate=COST,
        name="rank",
    )(slice_order, recv.reshape(64, SW, LAT))
    return ranked.reshape(8, 2, 4, SW, LAT), far.reshape(4, 2, 4, SW, LAT)


def stack_taps(plane, fill):
    lane = lax.broadcasted_iota(jnp.int32, plane.shape, 1)
    before = jnp.where(lane == 0, 0.0, pltpu.roll(plane, 1, 1))
    after = jnp.where(lane == LAT - 1, 0.0, pltpu.roll(plane, LAT - 1, 1))
    tail = jnp.full((8, LAT), fill, F32)
    return jnp.concatenate([before, plane, after, tail], axis=0).astype(BF)


def tap_group(stack_ref, start):
    longitudes = [stack_ref[pl.ds(start + i, 5)].reshape(UNIT, LAT) for i in range(4)]
    return jnp.concatenate(longitudes, axis=1)


def bands_of(k, halos):
    left2, left1, ranked, right1, right2 = halos
    if k % 4 < 2:
        j = k // 4 * 2 + k % 4
        return [(left2, j), (left1, k), (ranked, k), (right1, k), (right2, j)], -8
    return [(left1, k), (ranked, k), (right1, k)], -4


def band_spec(rank, kind):
    return pl.BlockSpec((1, 1, 4, SW, LAT), lambda i: (rank, kind, 0, 0, 0))


def whole(value):
    return pl.BlockSpec(value.shape, lambda i: (0,) * value.ndim)


def over_planes(bands, base, low, count, body):
    for b, band in enumerate(bands):
        for i in range(4):
            spot = base + 4 * b + i - low
            if 0 <= spot < count:
                body(spot, band, i)


COUNTS = (11, 8)


def early_kernel(rank, n_bands, base, low, n_chunks, n_prior, offsets, n_last, *refs):
    order_ref = refs[0]
    chunks = [refs[1:12], refs[12:20]][:n_chunks]
    at = 1 + sum(COUNTS[:n_chunks])
    bands = refs[at : at + n_bands]
    at += n_bands
    prior_hbm = refs[at : at + n_prior]
    at += n_prior
    acc_ref, out_ref = refs[at : at + 2]
    at += 2
    if n_last:
        last_ref = refs[at]
        at += 1
    hyper_stack = refs[at]
    weights = refs[at + 1 : at + 1 + n_chunks]
    at += 1 + n_chunks
    priors, sem = refs[at : at + n_prior], refs[at + n_prior]
    waits = [
        fetch_weights(i, chunks[i], order_ref[rank], weights[i], sem.at[pl.ds(2 * i, 2)])
        for i in range(n_chunks)
    ]
    planes = hyper_stack.shape[0]
    copies = []
    for j in range(n_prior):
        copies.append(
            pltpu.make_async_copy(prior_hbm[j].at[pl.ds(offsets[j], planes)], priors[j], sem.at[4 + j])
        )
        copies[-1].start()

    def stack_hyper(place, band, i):
        hyper_stack[place] = stack_taps(band[0, 0, i].astype(F32), 1.0)

    over_planes(bands, base, low, planes, stack_hyper)
    for wait in waits:
        wait()

    def weight(u):
        return weights[u // 4][:, UNIT * (u % 4) : UNIT * (u % 4 + 1)]

    outs = weights[0][:, 4 * UNIT : 4 * UNIT + 128].astype(F32)
    outs = jnp.concatenate([outs, jnp.zeros((16, 128), F32)], axis=0)
    out_ref[...] = outs.T.astype(BF)
    for j in range(n_last):
        last_ref[:, UNIT * j : UNIT * (j + 1)] = weight(n_prior + 1 + j)
    for copy in copies:
        copy.wait()

    @pl.loop(0, acc_ref.shape[0])
    def _(p):
        total = jnp.dot(weight(0), tap_group(hyper_stack, 4 * p), preferred_element_type=F32)
        for j in range(n_prior):
            total = total + jnp.dot(
                weight(j + 1),
                tap_group(priors[j], 4 * p),
                preferred_element_type=F32,
            )
        acc_ref[p] = total


def early(rank, slice_order, chunks, halos, stacks, n_last):
    reach = 2 * (3 - rank % 4)
    bands, base = bands_of(rank, halos)
    low, planes = -reach - 2, 8 + 2 * reach
    groups = (planes - 4) // 4
    shapes = [jax.ShapeDtypeStruct((groups, HALF, 4 * LAT), F32), jax.ShapeDtypeStruct((128, 128), BF)]
    if n_last:
        shapes.append(jax.ShapeDtypeStruct((HALF, UNIT * n_last), BF))
    offsets = [low - start for start, _ in stacks]
    priors = [stack for _, stack in stacks]
    return pl.pallas_call(
        functools.partial(early_kernel, rank, len(bands), base, low, len(chunks), len(priors), offsets, n_last),
        grid=(1,),
        out_shape=shapes,
        in_specs=[SMEM] + [ANY] * sum(COUNTS[: len(chunks)]) + [band_spec(j, 1) for _, j in bands] + [HBM] * len(priors),
        out_specs=[whole(shape) for shape in shapes],
        scratch_shapes=[pltpu.VMEM((planes, 128, LAT), BF)]
        + [pltpu.VMEM((HALF, LANES[i]), BF) for i in range(len(chunks))]
        + [pltpu.VMEM((planes, 128, LAT), BF)] * len(priors)
        + [pltpu.SemaphoreType.DMA((4 + len(priors),))],
        compiler_params=PARAMS,
        cost_estimate=COST,
        name="early",
    )(slice_order, *[ref for chunk in chunks for ref in chunk], *[band for band, _ in bands], *priors)


ERF_TOP = (0.00022905065861350646, 0.0034082910107109506, 0.050955695062380861, 0.18520832239976145, 1.128379143519084)
ERF_LOW = (-1.1791602954361697e-7, 0.000023547966471313185, 0.0010179625278914885, 0.014070470171167667, 0.11098505178285362, 0.49746925110067538, 1.0)


def gelu(v):
    z = jnp.clip(v * 0.7071067811865476, -3.7439211627767994, 3.7439211627767994)
    square = z * z
    top = jnp.full_like(z, ERF_TOP[0])
    for c in ERF_TOP[1:]:
        top = top * square + c
    low = jnp.full_like(z, ERF_LOW[0])
    for c in ERF_LOW[1:]:
        low = low * square + c
    half = 0.5 * v
    return half + half * (z * top / low)


def finish_kernel(kind, n_bands, base, low, *refs):
    acc_hbm, out_ref = refs[:2]
    acc_ref, sem = refs[-2:]
    refs = refs[2:-2]
    copy = pltpu.make_async_copy(acc_hbm, acc_ref, sem)
    copy.start()
    stacks = []
    if kind == "newest":
        last_ref, own_ref, got_ref = refs[:3]
        bands = refs[3 : 3 + n_bands]
        part_ref, value_ref, stack_ref = refs[3 + n_bands :]
        stacks = [stack_ref]

        def decode(place, band, i):
            mean = own_ref[place].astype(F32) + got_ref[place].astype(F32)
            value = (band[0, 0, i].astype(F32) + mean).astype(BF)
            value_ref[place] = value
            stack_ref[place] = stack_taps(value.astype(F32), 0.0)

        over_planes(bands, base, low, own_ref.shape[0], decode)
    elif kind == "widened":
        last_ref = refs[0]
        part_ref, *stacks = refs[6:]
        widen_bands(refs[1:6], stacks)
    else:
        part_ref = refs[0]
    copy.wait()

    @pl.loop(0, acc_ref.shape[0])
    def _(p):
        total = acc_ref[p]
        for j, stack_ref in enumerate(stacks):
            total = total + jnp.dot(
                last_ref[:, UNIT * j : UNIT * (j + 1)], tap_group(stack_ref, 4 * p), preferred_element_type=F32
            )
        for h in range(2):
            hidden = gelu(total[:, 2 * LAT * h : 2 * LAT * (h + 1)]).astype(BF)
            part = jnp.dot(out_ref[:SW, :HALF], hidden, preferred_element_type=F32).astype(BF)
            part_ref[4 * p + 2 * h] = part[:, :LAT]
            part_ref[4 * p + 2 * h + 1] = part[:, LAT:]


def finish(kind, acc, outs, *more, rank=None, halos=None):
    lons = 4 * acc.shape[0]
    shapes = [jax.ShapeDtypeStruct((lons, SW, LAT), BF)]
    operands = [acc, outs, *more]
    specs = [HBM] + [whole(value) for value in operands[1:]]
    bands, base, low = [], 0, 0
    if kind == "newest":
        bands, base = bands_of(rank, halos)
        low = -2 * (3 - rank % 4)
        operands += [band for band, _ in bands]
        specs += [band_spec(j, 0) for _, j in bands]
        shapes.append(jax.ShapeDtypeStruct(more[1].shape, BF))
        shapes.append(jax.ShapeDtypeStruct((more[1].shape[0], 128, LAT), BF))
    elif kind == "widened":
        shapes += [jax.ShapeDtypeStruct((20, 128, LAT), BF)] * 2
    return pl.pallas_call(
        functools.partial(finish_kernel, kind, len(bands), base, low),
        grid=(1,),
        out_shape=shapes,
        in_specs=specs,
        out_specs=[whole(shape) for shape in shapes],
        scratch_shapes=[pltpu.VMEM(acc.shape, F32), pltpu.SemaphoreType.DMA],
        compiler_params=PARAMS,
        cost_estimate=COST,
        name="finish",
    )(*operands)


def widen_bands(bands, stacks):
    for j, stack_ref in enumerate(stacks):

        def widen(place, band, i, j=j, stack_ref=stack_ref):
            stack_ref[place] = stack_taps(band[j, i].astype(F32), 0.0)

        over_planes(bands, 0, 0, 20, widen)


def widen_kernel(*refs):
    widen_bands(refs[:5], refs[5:])


def widen(bands):
    return pl.pallas_call(
        widen_kernel,
        out_shape=[jax.ShapeDtypeStruct((20, 128, LAT), BF)] * 2,
        in_specs=[VMEM] * 5,
        out_specs=[VMEM] * 2,
        compiler_params=PARAMS,
        cost_estimate=COST,
        name="widen",
    )(*bands)


TAPS = (((1, 0),), ((2, 0), (0, 1)))


def upsample_kernel(
    order_ref, beta_ref, gamma_ref, weight_ref,
    own_a, own_b, own_c, up_a, up_b, up_c,
    out0, out1, out2, out3, fields, normed, shifted, totals,
):
    for level, (first, second, third) in enumerate(((own_a, own_b, own_c), (up_a, up_b, up_c))):
        for k in range(8):
            rows = pl.ds(pl.multiple_of(order_ref[k] * SW, 8), SW)
            for x in range(5):
                if k < 6:
                    plane = first[k, x]
                elif k == 6:
                    plane = second[x]
                elif x < 4:
                    plane = second[5 + x]
                else:
                    plane = third[0]
                fields[level, x, rows, :] = plane.astype(F32)
    gamma = gamma_ref[...].astype(BF)
    lane = lax.broadcasted_iota(jnp.int32, (320, LAT), 1)

    for level in range(2):

        @pl.loop(0, 5)
        def _(x, level=level):
            value = fields[level, x]
            energy = jnp.dot(gamma, (value * value).astype(BF), preferred_element_type=F32)
            field = (value * jnp.sqrt(energy + beta_ref[...])).astype(BF)
            normed[level, x] = field
            later = pltpu.roll(field.astype(F32), LAT - 1, 1)
            shifted[level, x] = jnp.where(lane == LAT - 1, 0.0, later).astype(BF)

    started = set()
    for dl in range(2):
        for dx in range(2):
            for dt in range(2):
                pars, rows = [], []
                for p in range(2):
                    for q in range(2):
                        for r in range(2):
                            for kl, ol in TAPS[p]:
                                for kx, ox in TAPS[q]:
                                    for kt, ot in TAPS[r]:
                                        if (ol, ox, ot) == (dl, dx, dt):
                                            tap = kl * 9 + kx * 3 + kt
                                            pars.append(4 * p + 2 * q + r)
                                            rows.append(weight_ref[32 * tap : 32 * tap + 32, :])
                source = (normed, shifted)[dt]
                field = jnp.concatenate([source[dl, dx + x] for x in range(4)], axis=1)
                got = jnp.dot(jnp.concatenate(rows, axis=0), field, preferred_element_type=F32)
                for i, par in enumerate(pars):
                    piece = got[32 * i : 32 * i + 32]
                    if par in started:
                        totals[par] += piece
                    else:
                        totals[par] = piece
                        started.add(par)
    source = lax.broadcasted_iota(jnp.int32, (2 * LAT, 2 * LAT), 0)
    target = lax.broadcasted_iota(jnp.int32, (2 * LAT, 2 * LAT), 1)
    mixing = (target == jnp.where(source < LAT, 2 * source, 2 * source - 2 * LAT + 1)).astype(F32).astype(BF)
    for p in range(2):
        rows = []
        for x in range(4):
            for q in range(2):
                even = totals[4 * p + 2 * q, :, LAT * x : LAT * x + LAT]
                odd = totals[4 * p + 2 * q + 1, :, LAT * x : LAT * x + LAT]
                rows.append(jnp.concatenate([even, odd], axis=1))
        mixed = jnp.dot(jnp.concatenate(rows, axis=0).astype(BF), mixing, preferred_element_type=F32)
        mixed = mixed.reshape(8, 4, 8, 2 * LAT)
        for relative, out_ref in enumerate((out0, out1, out2, out3)):
            out_ref[:, p] = jnp.transpose(mixed[:, relative], (1, 0, 2)).astype(BF)


def upsample(slice_order, beta, gamma, weight, own, up):
    shape = jax.ShapeDtypeStruct((8, 2, 8, 2 * LAT), BF)
    return pl.pallas_call(
        upsample_kernel,
        out_shape=[shape] * 4,
        in_specs=[SMEM] + [VMEM] * 9,
        out_specs=[VMEM] * 4,
        scratch_shapes=[
            pltpu.VMEM((2, 5, 320, LAT), F32),
            pltpu.VMEM((2, 5, 320, LAT), BF),
            pltpu.VMEM((2, 5, 320, LAT), BF),
            pltpu.VMEM((8, 32, 4 * LAT), F32),
        ],
        compiler_params=PARAMS,
        cost_estimate=COST,
        name="upsample",
    )(slice_order, beta, gamma, weight, *own, *up)


def place_kernel(in0, in1, in2, in3, out_ref):
    y_id = lax.axis_index("chan") % 4
    for relative, in_ref in enumerate((in0, in1, in2, in3)):
        level = (y_id + 4 - relative) % 4
        for o in range(8):
            for p in range(2):
                out_ref[o, 2 * level + p] = in_ref[o, p]


def place(pieces):
    return pl.pallas_call(
        place_kernel,
        out_shape=jax.ShapeDtypeStruct((8, 8, 8, 2 * LAT), BF),
        in_specs=[VMEM] * 4,
        out_specs=VMEM,
        compiler_params=PARAMS,
        cost_estimate=COST,
        name="place",
    )(*pieces)


def local(
    symbols,
    hyper_mean,
    slice_order,
    hyper_weight,
    ctx_weight,
    ctx_bias,
    out_weight,
    gdn_beta,
    gdn_gamma,
    tconv_weight,
):
    both = jnp.stack([symbols.astype(BF), hyper_mean])
    send = jnp.transpose(both, (2, 0, 3, 1, 4))
    send, pack_order = tie(jnp.concatenate([send, send]), slice_order)
    recv = lax.all_to_all(send, "chan", 0, 0)
    weights = (hyper_weight, ctx_weight, ctx_bias, out_weight)
    first, halos = first_spread(*pack(0, pack_order, *weights), recv, slice_order)
    ranked = halos[2]
    later_order, _ = tie(slice_order, ranked)
    keep, keep_other, give = pack(1, later_order, *weights)
    give, tconv_weight, _ = tie(give, tconv_weight, first[6])
    got = x_swap(give)
    tconv = [tconv_weight] + [from_y(tconv_weight, r) for r in range(1, 4)]
    chunks = [first]

    def centre(value, count):
        start = value.shape[0] // 2 - 2
        return value[start : start + count]

    def around(value):
        return [from_lon(value, d) if d else value for d in (-2, -1, 0, 1, 2)]

    values, stacks, part = [], [], None
    for k in range(8):
        if k == 4:
            stacks = [(-8, stack) for stack in widen(wide_first)]
            acc, outs, last = early(k, slice_order, chunks, halos, stacks, 2)
            part, *more = finish("widened", acc, outs, last, *wide_second)
            stacks += [(-8, stack) for stack in more]
        elif k == 0:
            acc, outs = early(k, slice_order, chunks, halos, [], 0)
            acc, got = tie(acc, got)
            pair = jnp.concatenate([keep, got])
            up, down = from_y(pair, -1), from_y(pair, 1)
            (part,) = finish("plain", acc, outs)
        else:
            acc, outs, last = early(k, slice_order, chunks, halos, stacks, 1)
            if k == 1:
                acc, *tconv = tie(acc, *tconv)
            elif k == 2:
                acc, up, down = tie(acc, up, down)
                far_k, far_g = from_y(up[:HALF], -1), from_y(down[HALF:], 1)
                near_o = core_swap(jnp.concatenate([up, down, got]))
            elif k == 3:
                acc, far_k, far_g, near_o = tie(acc, far_k, far_g, near_o)
                far_o = core_swap(jnp.concatenate([far_k, far_g]))
                chunks = [first, [pair, up, down, far_k, far_g, keep_other, near_o, far_o]]
            part, value, stack = finish(
                "newest", acc, outs, last, part, x_swap(part), rank=k - 1, halos=halos
            )
            values.append(value)
            stacks.append((-2 * (3 - (k - 1) % 4), stack))
        if k == 2:
            wide_first = around(jnp.stack([centre(value, 4) for value in values]))
        if k == 3:
            mean = part.astype(F32) + x_swap(part).astype(F32)
            newest = (ranked[k, 0].astype(F32) + mean).astype(BF)
            wide_second = around(jnp.stack([centre(values[2], 4), newest]))
        if k == 6:
            blocks = [jnp.concatenate([w[2], w[3][:, :1]], axis=1) for w in (wide_first, wide_second)]
            own_a = jnp.concatenate(blocks + [jnp.stack([centre(value, 5) for value in values[3:]])])
            down_one = [(i + 1, i) for i in range(8) if i % 4 < 3]
            up_a = lax.ppermute(own_a, "chan", down_one)
    mean = part.astype(F32) + x_swap(part).astype(F32)
    newest = (ranked[7, 0].astype(F32) + mean).astype(BF)
    own_b = jnp.concatenate([centre(values[-1], 5), newest])
    edge = newest[:1]
    corner = [(i * 32 + (j + 1) % 32, (i - 1) * 32 + j) for i in range(8) if i % 4 > 0 for j in range(32)]
    own = [own_a, own_b, from_lon(edge, 1)]
    up = [up_a, lax.ppermute(own_b, "chan", down_one), lax.ppermute(edge, ("chan", "lon"), corner)]
    rows = jnp.stack(tconv, axis=1).reshape(27 * 32, 320)
    pieces = upsample(slice_order, gdn_beta[:, None], gdn_gamma, rows, own, up)
    return place([from_y(v, -r) if r else v for r, v in enumerate(pieces)])


def solution(mesh):
    placed = (
        P("chan", None, "lon", None),
        P("chan", None, "lon", None),
        P(),
        P("chan", None, None, None),
        P("chan", None, None, None),
        P("chan", None),
        P("chan", None, None),
        P(),
        P(),
        P(None, "chan", None),
    )
    return jax.shard_map(
        local, mesh=mesh, in_specs=placed, out_specs=P("chan", None, "lon", None), check_vma=False
    )
```

```python
import functools
import jax
import jax.numpy as jnp
from jax import lax
from jax.experimental import pallas as pl
from jax.experimental.pallas import tpu as pltpu
from jax.sharding import PartitionSpec as P

BF = jnp.bfloat16
F32 = jnp.float32
SW = 40
HALF = 112
LAT = 128
UNIT = 640
LANES = (2816, 2560)
ANY = pl.BlockSpec(memory_space=pl.ANY)
VMEM = pl.BlockSpec(memory_space=pltpu.VMEM)
HBM = pl.BlockSpec(memory_space=pltpu.HBM)
SMEM = pl.BlockSpec(memory_space=pltpu.SMEM)
COST = pl.CostEstimate(flops=200_000_000, bytes_accessed=1 << 20, transcendentals=0)
PARAMS = pltpu.CompilerParams(vmem_limit_bytes=16 << 20)


def x_swap(value):
    return lax.ppermute(value, "chan", [(i, i ^ 4) for i in range(8)])


def core_swap(value):
    return lax.ppermute(value, "lon", [(i, i ^ 1) for i in range(32)])


def from_y(value, distance):
    return lax.ppermute(
        value, "chan", [(i, (i // 4) * 4 + (i - distance) % 4) for i in range(8)]
    )


def from_lon(value, distance):
    return lax.ppermute(value, "lon", [(i, (i - distance) % 32) for i in range(32)])


def pack_kernel(chunk, order_ref, bias_ref, hyper_hbm, ctx_hbm, out_hbm, keep, keep_other, give, hyper_ref, out_ref, blocks, packed, sem):
    x_id = lax.axis_index("chan") // 4
    core = lax.axis_index("lon") % 2
    copies = []
    if chunk == 0:
        copies += [
            pltpu.make_async_copy(hyper_hbm, hyper_ref, sem.at[4]),
            pltpu.make_async_copy(out_hbm, out_ref, sem.at[5]),
        ]
    for j in range(3 + chunk):
        rows = pl.ds(pl.multiple_of(order_ref[3 * chunk + j] * SW, 8), SW)
        copies.append(pltpu.make_async_copy(ctx_hbm.at[:, rows, :], blocks.at[j], sem.at[j]))
    for copy in copies:
        copy.start()

    def put(u, taps, parts=None):
        for a in range(5):
            tail = jnp.zeros((8, 224), F32) if parts is None or a != 2 else parts
            block = jnp.concatenate([taps[3 * a + b].astype(F32) for b in range(3)] + [tail], axis=0)
            block = jnp.concatenate([block, jnp.zeros((128, 32), F32)], axis=1)
            lanes = UNIT * u + 128 * a
            packed[:, lanes : lanes + 128] = block.T[:224].astype(BF)

    if chunk == 0:
        bias = bias_ref[...]
        high = bias.astype(BF).astype(F32)
        mid = (bias - high).astype(BF).astype(F32)
        low = (bias - high - mid).astype(BF).astype(F32)
        copies.pop(0).wait()
        put(0, hyper_ref, jnp.concatenate([high, mid, low, jnp.zeros((5, 224), F32)], axis=0))
        copies.pop(0).wait()
        outs = jnp.concatenate([out_ref[...].astype(F32), jnp.zeros((88, 224), F32)], axis=0)
        outs = jnp.concatenate([outs, jnp.zeros((128, 32), F32)], axis=1)
        packed[:, 4 * UNIT : 4 * UNIT + 128] = outs.T[:224].astype(BF)
        packed[:, 4 * UNIT + 128 :] = jnp.zeros((224, 128), BF)
    for j, copy in enumerate(copies):
        copy.wait()
        put(1 - chunk + j, blocks.at[j])
    lanes = LANES[chunk] // 2
    near = pl.ds(pl.multiple_of(core * lanes, 128), lanes)
    away = pl.ds(pl.multiple_of((1 - core) * lanes, 128), lanes)
    own = pl.ds(pl.multiple_of(HALF * x_id, 16), HALF)
    theirs = pl.ds(pl.multiple_of(HALF * (1 - x_id), 16), HALF)
    keep[...] = packed[own, near]
    keep_other[...] = packed[own, away]
    give[...] = packed[theirs, near]


def pack(chunk, slice_order, hyper_weight, ctx_weight, ctx_bias, out_weight):
    ctx = jnp.transpose(ctx_weight[0], (0, 2, 1))
    hyper = jnp.transpose(hyper_weight[0], (0, 2, 1))
    return pl.pallas_call(
        functools.partial(pack_kernel, chunk),
        out_shape=[jax.ShapeDtypeStruct((HALF, LANES[chunk] // 2), BF)] * 3,
        in_specs=[SMEM, VMEM, HBM, HBM, HBM],
        out_specs=[VMEM] * 3,
        scratch_shapes=[
            pltpu.VMEM((15, SW, 224), BF),
            pltpu.VMEM((SW, 224), BF),
            pltpu.VMEM((4, 15, SW, 224), BF),
            pltpu.VMEM((224, LANES[chunk]), BF),
            pltpu.SemaphoreType.DMA((6,)),
        ],
        compiler_params=pltpu.CompilerParams(vmem_limit_bytes=(60, 16)[chunk] << 20),
        cost_estimate=COST,
        name="pack",
    )(slice_order, ctx_bias, hyper, ctx, out_weight[0])


def tie(*values):
    return lax.optimization_barrier(values)


def first_spread(keep, keep_other, give, recv, slice_order, later):
    up_k, down_k = from_y(keep, -1), from_y(keep, 1)
    got = x_swap(give)
    ranked, far = to_ranks(slice_order, recv)
    up_k, down_k, got, *later = tie(up_k, down_k, got, *later)
    up_g, down_g = from_y(got, -1), from_y(got, 1)
    far_k = from_y(up_k, -1)
    left2, right2 = from_lon(far, -2), from_lon(far, 2)
    up_g, down_g, far_k, left2, right2, ranked, later_give = tie(
        up_g, down_g, far_k, left2, right2, ranked, later[2]
    )
    later_got = x_swap(later_give)
    far_g = from_y(down_g, 1)
    left1, right1 = from_lon(ranked, -1), from_lon(ranked, 1)
    near_o = core_swap(jnp.concatenate([up_k, up_g, down_k, down_g, got]))
    far_o = core_swap(jnp.concatenate([far_k, far_g]))
    chunk = [keep, got, up_k, up_g, down_k, down_g, far_k, far_g, keep_other, near_o, far_o]
    return chunk, (left2, left1, ranked, right1, right2), (later[0], later[1], later_got)


def chunk_views(chunk, refs):
    def rows(ref, i):
        return ref.at[pl.ds(HALF * i, HALF)]

    if chunk == 0:
        views = refs[:8]
        keep_o, near_o, far_o = refs[8:]
    else:
        pair, up, down, far_k, far_g, keep_o, near_o, far_o = refs
        views = [rows(ref, i) for ref in (pair, up, down) for i in range(2)] + [far_k, far_g]
    keep, got, up_k, up_g, down_k, down_g, far_k, far_g = views
    return {
        (0, 0): (keep, keep_o),
        (0, 1): (got, rows(near_o, 4)),
        (1, 0): (down_k, rows(near_o, 2)),
        (1, 1): (down_g, rows(near_o, 3)),
        (2, 0): (far_k, rows(far_o, 0)),
        (2, 1): (far_g, rows(far_o, 1)),
        (3, 0): (up_k, rows(near_o, 0)),
        (3, 1): (up_g, rows(near_o, 1)),
    }


def fetch_weights(chunk_id, refs, slice_id, dest, sem):
    chan = lax.axis_index("chan")
    core = lax.axis_index("lon") % 2
    relative = (slice_id + 4 - chan % 4) % 4
    side = (slice_id // 4 + chan // 4) % 2
    lanes = LANES[chunk_id] // 2
    mine = dest.at[:, pl.ds(pl.multiple_of(core * lanes, 128), lanes)]
    other = dest.at[:, pl.ds(pl.multiple_of((1 - core) * lanes, 128), lanes)]
    choices = chunk_views(chunk_id, refs)
    for (r, i), (first, second) in choices.items():

        @pl.when((relative == r) & (side == i))
        def _(first=first, second=second):
            pltpu.make_async_copy(first, mine, sem.at[0]).start()
            pltpu.make_async_copy(second, other, sem.at[1]).start()

    def wait():
        pltpu.make_async_copy(choices[2, 0][0], mine, sem.at[0]).wait()
        pltpu.make_async_copy(choices[0, 0][1], other, sem.at[1]).wait()

    return wait


def rank_kernel(order_ref, recv_ref, ranked_ref, far_ref):
    for k in range(8):
        s = order_ref[k]

        @pl.loop(0, 8)
        def _(i, s=s, k=k):
            plane = recv_ref[s * 8 + i]
            ranked_ref[k * 8 + i] = plane
            if k % 4 < 2:
                far_ref[(k // 4 * 2 + k % 4) * 8 + i] = plane


def to_ranks(slice_order, recv):
    ranked, far = pl.pallas_call(
        rank_kernel,
        out_shape=[jax.ShapeDtypeStruct((64, SW, LAT), BF), jax.ShapeDtypeStruct((32, SW, LAT), BF)],
        in_specs=[SMEM, VMEM],
        out_specs=[VMEM] * 2,
        compiler_params=PARAMS,
        cost_estimate=COST,
        name="rank",
    )(slice_order, recv.reshape(64, SW, LAT))
    return ranked.reshape(8, 2, 4, SW, LAT), far.reshape(4, 2, 4, SW, LAT)


def stack_taps(plane, fill):
    lane = lax.broadcasted_iota(jnp.int32, plane.shape, 1)
    before = jnp.where(lane == 0, 0.0, pltpu.roll(plane, 1, 1))
    after = jnp.where(lane == LAT - 1, 0.0, pltpu.roll(plane, LAT - 1, 1))
    tail = jnp.full((8, LAT), fill, F32)
    return jnp.concatenate([before, plane, after, tail], axis=0).astype(BF)


def tap_group(stack_ref, start):
    longitudes = [stack_ref[pl.ds(start + i, 5)].reshape(UNIT, LAT) for i in range(4)]
    return jnp.concatenate(longitudes, axis=1)


def bands_of(k, halos):
    left2, left1, ranked, right1, right2 = halos
    if k % 4 < 2:
        j = k // 4 * 2 + k % 4
        return [(left2, j), (left1, k), (ranked, k), (right1, k), (right2, j)], -8
    return [(left1, k), (ranked, k), (right1, k)], -4


def band_spec(rank, kind):
    return pl.BlockSpec((1, 1, 4, SW, LAT), lambda i: (rank, kind, 0, 0, 0))


def whole(value):
    return pl.BlockSpec(value.shape, lambda i: (0,) * value.ndim)


def over_planes(bands, base, low, count, body):
    for b, band in enumerate(bands):
        for i in range(4):
            spot = base + 4 * b + i - low
            if 0 <= spot < count:
                body(spot, band, i)


COUNTS = (11, 8)


def early_kernel(rank, n_bands, base, low, n_chunks, n_prior, offsets, n_last, *refs):
    order_ref = refs[0]
    chunks = [refs[1:12], refs[12:20]][:n_chunks]
    at = 1 + sum(COUNTS[:n_chunks])
    bands = refs[at : at + n_bands]
    at += n_bands
    prior_hbm = refs[at : at + n_prior]
    at += n_prior
    acc_ref, out_ref = refs[at : at + 2]
    at += 2
    if n_last:
        last_ref = refs[at]
        at += 1
    hyper_stack = refs[at]
    weights = refs[at + 1 : at + 1 + n_chunks]
    at += 1 + n_chunks
    priors, sem = refs[at : at + n_prior], refs[at + n_prior]
    waits = [
        fetch_weights(i, chunks[i], order_ref[rank], weights[i], sem.at[pl.ds(2 * i, 2)])
        for i in range(n_chunks)
    ]
    planes = hyper_stack.shape[0]
    copies = []
    for j in range(n_prior):
        copies.append(
            pltpu.make_async_copy(prior_hbm[j].at[pl.ds(offsets[j], planes)], priors[j], sem.at[4 + j])
        )
        copies[-1].start()

    def stack_hyper(place, band, i):
        hyper_stack[place] = stack_taps(band[0, 0, i].astype(F32), 1.0)

    over_planes(bands, base, low, planes, stack_hyper)
    for wait in waits:
        wait()

    def weight(u):
        return weights[u // 4][:, UNIT * (u % 4) : UNIT * (u % 4 + 1)]

    outs = weights[0][:, 4 * UNIT : 4 * UNIT + 128].astype(F32)
    outs = jnp.concatenate([outs, jnp.zeros((16, 128), F32)], axis=0)
    out_ref[...] = outs.T.astype(BF)
    for j in range(n_last):
        last_ref[:, UNIT * j : UNIT * (j + 1)] = weight(n_prior + 1 + j)
    for copy in copies:
        copy.wait()

    @pl.loop(0, acc_ref.shape[0])
    def _(p):
        total = jnp.dot(weight(0), tap_group(hyper_stack, 4 * p), preferred_element_type=F32)
        for j in range(n_prior):
            total = total + jnp.dot(
                weight(j + 1),
                tap_group(priors[j], 4 * p),
                preferred_element_type=F32,
            )
        acc_ref[p] = total


def early(rank, slice_order, chunks, halos, stacks, n_last):
    reach = 2 * (3 - rank % 4)
    bands, base = bands_of(rank, halos)
    low, planes = -reach - 2, 8 + 2 * reach
    groups = (planes - 4) // 4
    shapes = [jax.ShapeDtypeStruct((groups, HALF, 4 * LAT), F32), jax.ShapeDtypeStruct((128, 128), BF)]
    if n_last:
        shapes.append(jax.ShapeDtypeStruct((HALF, UNIT * n_last), BF))
    offsets = [low - start for start, _ in stacks]
    priors = [stack for _, stack in stacks]
    return pl.pallas_call(
        functools.partial(early_kernel, rank, len(bands), base, low, len(chunks), len(priors), offsets, n_last),
        grid=(1,),
        out_shape=shapes,
        in_specs=[SMEM] + [ANY] * sum(COUNTS[: len(chunks)]) + [band_spec(j, 1) for _, j in bands] + [HBM] * len(priors),
        out_specs=[whole(shape) for shape in shapes],
        scratch_shapes=[pltpu.VMEM((planes, 128, LAT), BF)]
        + [pltpu.VMEM((HALF, LANES[i]), BF) for i in range(len(chunks))]
        + [pltpu.VMEM((planes, 128, LAT), BF)] * len(priors)
        + [pltpu.SemaphoreType.DMA((4 + len(priors),))],
        compiler_params=PARAMS,
        cost_estimate=COST,
        name="early",
    )(slice_order, *[ref for chunk in chunks for ref in chunk], *[band for band, _ in bands], *priors)


ERF_TOP = (0.00022905065861350646, 0.0034082910107109506, 0.050955695062380861, 0.18520832239976145, 1.128379143519084)
ERF_LOW = (-1.1791602954361697e-7, 0.000023547966471313185, 0.0010179625278914885, 0.014070470171167667, 0.11098505178285362, 0.49746925110067538, 1.0)


def gelu(v):
    z = jnp.clip(v * 0.7071067811865476, -3.7439211627767994, 3.7439211627767994)
    square = z * z
    top = jnp.full_like(z, ERF_TOP[0])
    for c in ERF_TOP[1:]:
        top = top * square + c
    low = jnp.full_like(z, ERF_LOW[0])
    for c in ERF_LOW[1:]:
        low = low * square + c
    half = 0.5 * v
    return half + half * (z * top / low)


def finish_kernel(kind, n_bands, base, low, *refs):
    acc_hbm, out_ref = refs[:2]
    acc_ref, sem = refs[-2:]
    refs = refs[2:-2]
    copy = pltpu.make_async_copy(acc_hbm, acc_ref, sem)
    copy.start()
    stacks = []
    if kind == "newest":
        last_ref, own_ref, got_ref = refs[:3]
        bands = refs[3 : 3 + n_bands]
        part_ref, value_ref, stack_ref = refs[3 + n_bands :]
        stacks = [stack_ref]

        def decode(place, band, i):
            mean = own_ref[place].astype(F32) + got_ref[place].astype(F32)
            value = (band[0, 0, i].astype(F32) + mean).astype(BF)
            value_ref[place] = value
            stack_ref[place] = stack_taps(value.astype(F32), 0.0)

        over_planes(bands, base, low, own_ref.shape[0], decode)
    elif kind == "widened":
        last_ref = refs[0]
        part_ref, *stacks = refs[6:]
        widen_bands(refs[1:6], stacks)
    else:
        part_ref = refs[0]
    copy.wait()

    @pl.loop(0, acc_ref.shape[0])
    def _(p):
        total = acc_ref[p]
        for j, stack_ref in enumerate(stacks):
            total = total + jnp.dot(
                last_ref[:, UNIT * j : UNIT * (j + 1)], tap_group(stack_ref, 4 * p), preferred_element_type=F32
            )
        for h in range(2):
            hidden = gelu(total[:, 2 * LAT * h : 2 * LAT * (h + 1)]).astype(BF)
            part = jnp.dot(out_ref[:SW, :HALF], hidden, preferred_element_type=F32).astype(BF)
            part_ref[4 * p + 2 * h] = part[:, :LAT]
            part_ref[4 * p + 2 * h + 1] = part[:, LAT:]


def finish(kind, acc, outs, *more, rank=None, halos=None):
    lons = 4 * acc.shape[0]
    shapes = [jax.ShapeDtypeStruct((lons, SW, LAT), BF)]
    operands = [acc, outs, *more]
    specs = [HBM] + [whole(value) for value in operands[1:]]
    bands, base, low = [], 0, 0
    if kind == "newest":
        bands, base = bands_of(rank, halos)
        low = -2 * (3 - rank % 4)
        operands += [band for band, _ in bands]
        specs += [band_spec(j, 0) for _, j in bands]
        shapes.append(jax.ShapeDtypeStruct(more[1].shape, BF))
        shapes.append(jax.ShapeDtypeStruct((more[1].shape[0], 128, LAT), BF))
    elif kind == "widened":
        shapes += [jax.ShapeDtypeStruct((20, 128, LAT), BF)] * 2
    return pl.pallas_call(
        functools.partial(finish_kernel, kind, len(bands), base, low),
        grid=(1,),
        out_shape=shapes,
        in_specs=specs,
        out_specs=[whole(shape) for shape in shapes],
        scratch_shapes=[pltpu.VMEM(acc.shape, F32), pltpu.SemaphoreType.DMA],
        compiler_params=PARAMS,
        cost_estimate=COST,
        name="finish",
    )(*operands)


def widen_bands(bands, stacks):
    for j, stack_ref in enumerate(stacks):

        def widen(place, band, i, j=j, stack_ref=stack_ref):
            stack_ref[place] = stack_taps(band[j, i].astype(F32), 0.0)

        over_planes(bands, 0, 0, 20, widen)


def widen_kernel(*refs):
    widen_bands(refs[:5], refs[5:])


def widen(bands):
    return pl.pallas_call(
        widen_kernel,
        out_shape=[jax.ShapeDtypeStruct((20, 128, LAT), BF)] * 2,
        in_specs=[VMEM] * 5,
        out_specs=[VMEM] * 2,
        compiler_params=PARAMS,
        cost_estimate=COST,
        name="widen",
    )(*bands)


TAPS = (((1, 0),), ((2, 0), (0, 1)))


def upsample_kernel(
    order_ref, beta_ref, gamma_ref, weight_ref,
    own_a, own_b, own_c, up_a, up_b, up_c,
    out0, out1, out2, out3, fields, normed, shifted, totals,
):
    for level, (first, second, third) in enumerate(((own_a, own_b, own_c), (up_a, up_b, up_c))):
        for k in range(8):
            rows = pl.ds(pl.multiple_of(order_ref[k] * SW, 8), SW)
            for x in range(5):
                if k < 5:
                    plane = first[k, x]
                elif k < 7 or x < 4:
                    plane = second[5 * (k - 5) + x]
                else:
                    plane = third[0]
                fields[level, x, rows, :] = plane.astype(F32)
    gamma = gamma_ref[...].astype(BF)
    lane = lax.broadcasted_iota(jnp.int32, (320, LAT), 1)

    for level in range(2):

        @pl.loop(0, 5)
        def _(x, level=level):
            value = fields[level, x]
            energy = jnp.dot(gamma, (value * value).astype(BF), preferred_element_type=F32)
            field = (value * jnp.sqrt(energy + beta_ref[...])).astype(BF)
            normed[level, x] = field
            later = pltpu.roll(field.astype(F32), LAT - 1, 1)
            shifted[level, x] = jnp.where(lane == LAT - 1, 0.0, later).astype(BF)

    started = set()
    for dl in range(2):
        for dx in range(2):
            for dt in range(2):
                pars, rows = [], []
                for p in range(2):
                    for q in range(2):
                        for r in range(2):
                            for kl, ol in TAPS[p]:
                                for kx, ox in TAPS[q]:
                                    for kt, ot in TAPS[r]:
                                        if (ol, ox, ot) == (dl, dx, dt):
                                            tap = kl * 9 + kx * 3 + kt
                                            pars.append(4 * p + 2 * q + r)
                                            rows.append(weight_ref[32 * tap : 32 * tap + 32, :])
                source = (normed, shifted)[dt]
                field = jnp.concatenate([source[dl, dx + x] for x in range(4)], axis=1)
                got = jnp.dot(jnp.concatenate(rows, axis=0), field, preferred_element_type=F32)
                for i, par in enumerate(pars):
                    piece = got[32 * i : 32 * i + 32]
                    if par in started:
                        totals[par] += piece
                    else:
                        totals[par] = piece
                        started.add(par)
    source = lax.broadcasted_iota(jnp.int32, (2 * LAT, 2 * LAT), 0)
    target = lax.broadcasted_iota(jnp.int32, (2 * LAT, 2 * LAT), 1)
    mixing = (target == jnp.where(source < LAT, 2 * source, 2 * source - 2 * LAT + 1)).astype(F32).astype(BF)
    for p in range(2):
        rows = []
        for x in range(4):
            for q in range(2):
                even = totals[4 * p + 2 * q, :, LAT * x : LAT * x + LAT]
                odd = totals[4 * p + 2 * q + 1, :, LAT * x : LAT * x + LAT]
                rows.append(jnp.concatenate([even, odd], axis=1))
        mixed = jnp.dot(jnp.concatenate(rows, axis=0).astype(BF), mixing, preferred_element_type=F32)
        mixed = mixed.reshape(8, 4, 8, 2 * LAT)
        for relative, out_ref in enumerate((out0, out1, out2, out3)):
            out_ref[:, p] = jnp.transpose(mixed[:, relative], (1, 0, 2)).astype(BF)


def upsample(slice_order, beta, gamma, weight, own, up):
    shape = jax.ShapeDtypeStruct((8, 2, 8, 2 * LAT), BF)
    return pl.pallas_call(
        upsample_kernel,
        out_shape=[shape] * 4,
        in_specs=[SMEM] + [VMEM] * 9,
        out_specs=[VMEM] * 4,
        scratch_shapes=[
            pltpu.VMEM((2, 5, 320, LAT), F32),
            pltpu.VMEM((2, 5, 320, LAT), BF),
            pltpu.VMEM((2, 5, 320, LAT), BF),
            pltpu.VMEM((8, 32, 4 * LAT), F32),
        ],
        compiler_params=PARAMS,
        cost_estimate=COST,
        name="upsample",
    )(slice_order, beta, gamma, weight, *own, *up)


def place_kernel(in0, in1, in2, in3, out_ref):
    y_id = lax.axis_index("chan") % 4
    for relative, in_ref in enumerate((in0, in1, in2, in3)):
        level = (y_id + 4 - relative) % 4
        for o in range(8):
            for p in range(2):
                out_ref[o, 2 * level + p] = in_ref[o, p]


def place(pieces):
    return pl.pallas_call(
        place_kernel,
        out_shape=jax.ShapeDtypeStruct((8, 8, 8, 2 * LAT), BF),
        in_specs=[VMEM] * 4,
        out_specs=VMEM,
        compiler_params=PARAMS,
        cost_estimate=COST,
        name="place",
    )(*pieces)


def local(
    symbols,
    hyper_mean,
    slice_order,
    hyper_weight,
    ctx_weight,
    ctx_bias,
    out_weight,
    gdn_beta,
    gdn_gamma,
    tconv_weight,
):
    both = jnp.stack([symbols.astype(BF), hyper_mean])
    send = jnp.transpose(both, (2, 0, 3, 1, 4))
    send, pack_order = tie(jnp.concatenate([send, send]), slice_order)
    recv = lax.all_to_all(send, "chan", 0, 0)
    weights = (hyper_weight, ctx_weight, ctx_bias, out_weight)
    packed = pack(0, pack_order, *weights)
    later_order, _ = tie(slice_order, packed[0])
    later = pack(1, later_order, *weights)
    first, halos, (keep, keep_other, got) = first_spread(*packed, recv, slice_order, later)
    ranked = halos[2]
    chunks = [first]

    def centre(value, count):
        start = value.shape[0] // 2 - 2
        return value[start : start + count]

    def around(value):
        return [from_lon(value, d) if d else value for d in (-2, -1, 0, 1, 2)]

    values, stacks, part = [], [], None
    for k in range(8):
        if k == 4:
            stacks = [(-8, stack) for stack in widen(wide_first)]
            acc, outs, last = early(k, slice_order, chunks, halos, stacks, 2)
            acc, tconv_weight = tie(acc, tconv_weight)
            tconv = [tconv_weight] + [from_y(tconv_weight, r) for r in range(1, 4)]
            part, *more = finish("widened", acc, outs, last, *wide_second)
            stacks += [(-8, stack) for stack in more]
        elif k == 0:
            acc, outs = early(k, slice_order, chunks, halos, [], 0)
            acc, got = tie(acc, got)
            pair = jnp.concatenate([keep, got])
            up, down = from_y(pair, -1), from_y(pair, 1)
            (part,) = finish("plain", acc, outs)
        else:
            acc, outs, last = early(k, slice_order, chunks, halos, stacks, 1)
            if k == 2:
                acc, up, down = tie(acc, up, down)
                far_k, far_g = from_y(up[:HALF], -1), from_y(down[HALF:], 1)
                near_o = core_swap(jnp.concatenate([up, down, got]))
            elif k == 3:
                acc, far_k, far_g, near_o = tie(acc, far_k, far_g, near_o)
                far_o = core_swap(jnp.concatenate([far_k, far_g]))
                chunks = [first, [pair, up, down, far_k, far_g, keep_other, near_o, far_o]]
            elif k == 5:
                acc, *tconv = tie(acc, *tconv)
            elif k == 7:
                acc, up_a = tie(acc, up_a)
            part, value, stack = finish(
                "newest", acc, outs, last, part, x_swap(part), rank=k - 1, halos=halos
            )
            values.append(value)
            stacks.append((-2 * (3 - (k - 1) % 4), stack))
        if k == 2:
            wide_first = around(jnp.stack([centre(value, 4) for value in values]))
        if k == 3:
            mean = part.astype(F32) + x_swap(part).astype(F32)
            newest = (ranked[k, 0].astype(F32) + mean).astype(BF)
            wide_second = around(jnp.stack([centre(values[2], 4), newest]))
        if k == 5:
            blocks = [jnp.concatenate([w[2], w[3][:, :1]], axis=1) for w in (wide_first, wide_second)]
            own_a = jnp.concatenate(blocks + [jnp.stack([centre(value, 5) for value in values[3:]])])
            down_one = [(i + 1, i) for i in range(8) if i % 4 < 3]
            up_a = lax.ppermute(own_a, "chan", down_one)
    mean = part.astype(F32) + x_swap(part).astype(F32)
    newest = (ranked[7, 0].astype(F32) + mean).astype(BF)
    own_b = jnp.concatenate([centre(values[-2], 5), centre(values[-1], 5), newest])
    edge = newest[:1]
    corner = [(i * 32 + (j + 1) % 32, (i - 1) * 32 + j) for i in range(8) if i % 4 > 0 for j in range(32)]
    own = [own_a, own_b, from_lon(edge, 1)]
    up = [up_a, lax.ppermute(own_b, "chan", down_one), lax.ppermute(edge, ("chan", "lon"), corner)]
    rows = jnp.stack(tconv, axis=1).reshape(27 * 32, 320)
    pieces = upsample(slice_order, gdn_beta[:, None], gdn_gamma, rows, own, up)
    return place([from_y(v, -r) if r else v for r, v in enumerate(pieces)])


def solution(mesh):
    placed = (
        P("chan", None, "lon", None),
        P("chan", None, "lon", None),
        P(),
        P("chan", None, None, None),
        P("chan", None, None, None),
        P("chan", None),
        P("chan", None, None),
        P(),
        P(),
        P(None, "chan", None),
    )
    return jax.shard_map(
        local, mesh=mesh, in_specs=placed, out_specs=P("chan", None, "lon", None), check_vma=False
    )
```

```python
import functools
import jax
import jax.numpy as jnp
from jax import lax
from jax.experimental import pallas as pl
from jax.experimental.pallas import tpu as pltpu
from jax.sharding import PartitionSpec as P

BF = jnp.bfloat16
F32 = jnp.float32
SW = 40
HALF = 112
LAT = 128
UNIT = 640
LANES = (2816, 2560)
ANY = pl.BlockSpec(memory_space=pl.ANY)
VMEM = pl.BlockSpec(memory_space=pltpu.VMEM)
HBM = pl.BlockSpec(memory_space=pltpu.HBM)
SMEM = pl.BlockSpec(memory_space=pltpu.SMEM)
COST = pl.CostEstimate(flops=200_000_000, bytes_accessed=1 << 20, transcendentals=0)
PARAMS = pltpu.CompilerParams(vmem_limit_bytes=16 << 20)


def x_swap(value):
    return lax.ppermute(value, "chan", [(i, i ^ 4) for i in range(8)])


def core_swap(value):
    return lax.ppermute(value, "lon", [(i, i ^ 1) for i in range(32)])


def from_y(value, distance):
    return lax.ppermute(
        value, "chan", [(i, (i // 4) * 4 + (i - distance) % 4) for i in range(8)]
    )


def from_lon(value, distance):
    return lax.ppermute(value, "lon", [(i, (i - distance) % 32) for i in range(32)])


def pack_kernel(chunk, order_ref, bias_ref, hyper_hbm, ctx_hbm, out_hbm, keep, keep_other, give, hyper_ref, out_ref, blocks, packed, sem):
    x_id = lax.axis_index("chan") // 4
    core = lax.axis_index("lon") % 2
    copies = []
    if chunk == 0:
        copies += [
            pltpu.make_async_copy(hyper_hbm, hyper_ref, sem.at[4]),
            pltpu.make_async_copy(out_hbm, out_ref, sem.at[5]),
        ]
    for j in range(3 + chunk):
        rows = pl.ds(pl.multiple_of(order_ref[3 * chunk + j] * SW, 8), SW)
        copies.append(pltpu.make_async_copy(ctx_hbm.at[:, rows, :], blocks.at[j], sem.at[j]))
    for copy in copies:
        copy.start()

    def put(u, taps, parts=None):
        for a in range(5):
            tail = jnp.zeros((8, 224), F32) if parts is None or a != 2 else parts
            block = jnp.concatenate([taps[3 * a + b].astype(F32) for b in range(3)] + [tail], axis=0)
            block = jnp.concatenate([block, jnp.zeros((128, 32), F32)], axis=1)
            lanes = UNIT * u + 128 * a
            packed[:, lanes : lanes + 128] = block.T[:224].astype(BF)

    if chunk == 0:
        bias = bias_ref[...]
        high = bias.astype(BF).astype(F32)
        mid = (bias - high).astype(BF).astype(F32)
        low = (bias - high - mid).astype(BF).astype(F32)
        copies.pop(0).wait()
        put(0, hyper_ref, jnp.concatenate([high, mid, low, jnp.zeros((5, 224), F32)], axis=0))
        copies.pop(0).wait()
        outs = jnp.concatenate([out_ref[...].astype(F32), jnp.zeros((88, 224), F32)], axis=0)
        outs = jnp.concatenate([outs, jnp.zeros((128, 32), F32)], axis=1)
        packed[:, 4 * UNIT : 4 * UNIT + 128] = outs.T[:224].astype(BF)
        packed[:, 4 * UNIT + 128 :] = jnp.zeros((224, 128), BF)
    for j, copy in enumerate(copies):
        copy.wait()
        put(1 - chunk + j, blocks.at[j])
    lanes = LANES[chunk] // 2
    near = pl.ds(pl.multiple_of(core * lanes, 128), lanes)
    away = pl.ds(pl.multiple_of((1 - core) * lanes, 128), lanes)
    own = pl.ds(pl.multiple_of(HALF * x_id, 16), HALF)
    theirs = pl.ds(pl.multiple_of(HALF * (1 - x_id), 16), HALF)
    keep[...] = packed[own, near]
    keep_other[...] = packed[own, away]
    give[...] = packed[theirs, near]


def pack(chunk, slice_order, hyper_weight, ctx_weight, ctx_bias, out_weight):
    ctx = jnp.transpose(ctx_weight[0], (0, 2, 1))
    hyper = jnp.transpose(hyper_weight[0], (0, 2, 1))
    return pl.pallas_call(
        functools.partial(pack_kernel, chunk),
        out_shape=[jax.ShapeDtypeStruct((HALF, LANES[chunk] // 2), BF)] * 3,
        in_specs=[SMEM, VMEM, HBM, HBM, HBM],
        out_specs=[VMEM] * 3,
        scratch_shapes=[
            pltpu.VMEM((15, SW, 224), BF),
            pltpu.VMEM((SW, 224), BF),
            pltpu.VMEM((4, 15, SW, 224), BF),
            pltpu.VMEM((224, LANES[chunk]), BF),
            pltpu.SemaphoreType.DMA((6,)),
        ],
        compiler_params=pltpu.CompilerParams(vmem_limit_bytes=(60, 16)[chunk] << 20),
        cost_estimate=COST,
        name="pack",
    )(slice_order, ctx_bias, hyper, ctx, out_weight[0])


def tie(*values):
    return lax.optimization_barrier(values)


def first_spread(keep, keep_other, give, recv, slice_order, later):
    up_k, down_k = from_y(keep, -1), from_y(keep, 1)
    got = x_swap(give)
    ranked, far = to_ranks(slice_order, recv)
    up_k, down_k, got, *later = tie(up_k, down_k, got, *later)
    up_g, down_g = from_y(got, -1), from_y(got, 1)
    far_k = from_y(up_k, -1)
    left2, right2 = from_lon(far, -2), from_lon(far, 2)
    up_g, down_g, far_k, left2, right2, ranked, later_give = tie(
        up_g, down_g, far_k, left2, right2, ranked, later[2]
    )
    later_got = x_swap(later_give)
    far_g = from_y(down_g, 1)
    left1, right1 = from_lon(ranked, -1), from_lon(ranked, 1)
    near_o = core_swap(jnp.concatenate([up_k, up_g, down_k, down_g, got]))
    far_o = core_swap(jnp.concatenate([far_k, far_g]))
    chunk = [keep, got, up_k, up_g, down_k, down_g, far_k, far_g, keep_other, near_o, far_o]
    return chunk, (left2, left1, ranked, right1, right2), (later[0], later[1], later_got)


def chunk_views(chunk, refs):
    def rows(ref, i):
        return ref.at[pl.ds(HALF * i, HALF)]

    if chunk == 0:
        views = refs[:8]
        keep_o, near_o, far_o = refs[8:]
    else:
        pair, up, down, far_k, far_g, keep_o, near_o, far_o = refs
        views = [rows(ref, i) for ref in (pair, up, down) for i in range(2)] + [far_k, far_g]
    keep, got, up_k, up_g, down_k, down_g, far_k, far_g = views
    return {
        (0, 0): (keep, keep_o),
        (0, 1): (got, rows(near_o, 4)),
        (1, 0): (down_k, rows(near_o, 2)),
        (1, 1): (down_g, rows(near_o, 3)),
        (2, 0): (far_k, rows(far_o, 0)),
        (2, 1): (far_g, rows(far_o, 1)),
        (3, 0): (up_k, rows(near_o, 0)),
        (3, 1): (up_g, rows(near_o, 1)),
    }


def fetch_weights(chunk_id, refs, slice_id, dest, sem):
    chan = lax.axis_index("chan")
    core = lax.axis_index("lon") % 2
    relative = (slice_id + 4 - chan % 4) % 4
    side = (slice_id // 4 + chan // 4) % 2
    lanes = LANES[chunk_id] // 2
    mine = dest.at[:, pl.ds(pl.multiple_of(core * lanes, 128), lanes)]
    other = dest.at[:, pl.ds(pl.multiple_of((1 - core) * lanes, 128), lanes)]
    choices = chunk_views(chunk_id, refs)
    for (r, i), (first, second) in choices.items():

        @pl.when((relative == r) & (side == i))
        def _(first=first, second=second):
            pltpu.make_async_copy(first, mine, sem.at[0]).start()
            pltpu.make_async_copy(second, other, sem.at[1]).start()

    def wait():
        pltpu.make_async_copy(choices[2, 0][0], mine, sem.at[0]).wait()
        pltpu.make_async_copy(choices[0, 0][1], other, sem.at[1]).wait()

    return wait


def rank_kernel(order_ref, recv_ref, ranked_ref, far_ref):
    for k in range(8):
        s = order_ref[k]

        @pl.loop(0, 8)
        def _(i, s=s, k=k):
            plane = recv_ref[s * 8 + i]
            ranked_ref[k * 8 + i] = plane
            if k % 4 < 2:
                far_ref[(k // 4 * 2 + k % 4) * 8 + i] = plane


def to_ranks(slice_order, recv):
    ranked, far = pl.pallas_call(
        rank_kernel,
        out_shape=[jax.ShapeDtypeStruct((64, SW, LAT), BF), jax.ShapeDtypeStruct((32, SW, LAT), BF)],
        in_specs=[SMEM, VMEM],
        out_specs=[VMEM] * 2,
        compiler_params=PARAMS,
        cost_estimate=COST,
        name="rank",
    )(slice_order, recv.reshape(64, SW, LAT))
    return ranked.reshape(8, 2, 4, SW, LAT), far.reshape(4, 2, 4, SW, LAT)


def stack_taps(plane, fill):
    lane = lax.broadcasted_iota(jnp.int32, plane.shape, 1)
    before = jnp.where(lane == 0, 0.0, pltpu.roll(plane, 1, 1))
    after = jnp.where(lane == LAT - 1, 0.0, pltpu.roll(plane, LAT - 1, 1))
    tail = jnp.full((8, LAT), fill, F32)
    return jnp.concatenate([before, plane, after, tail], axis=0).astype(BF)


def tap_group(stack_ref, start):
    longitudes = [stack_ref[pl.ds(start + i, 5)].reshape(UNIT, LAT) for i in range(4)]
    return jnp.concatenate(longitudes, axis=1)


def bands_of(k, halos):
    left2, left1, ranked, right1, right2 = halos
    if k % 4 < 2:
        j = k // 4 * 2 + k % 4
        return [(left2, j), (left1, k), (ranked, k), (right1, k), (right2, j)], -8
    return [(left1, k), (ranked, k), (right1, k)], -4


def band_spec(rank, kind):
    return pl.BlockSpec((1, 1, 4, SW, LAT), lambda i: (rank, kind, 0, 0, 0))


def whole(value):
    return pl.BlockSpec(value.shape, lambda i: (0,) * value.ndim)


def over_planes(bands, base, low, count, body):
    for b, band in enumerate(bands):
        for i in range(4):
            spot = base + 4 * b + i - low
            if 0 <= spot < count:
                body(spot, band, i)


COUNTS = (11, 8)


def early_kernel(rank, n_bands, base, low, n_chunks, n_prior, offsets, n_last, *refs):
    order_ref = refs[0]
    chunks = [refs[1:12], refs[12:20]][:n_chunks]
    at = 1 + sum(COUNTS[:n_chunks])
    bands = refs[at : at + n_bands]
    at += n_bands
    prior_hbm = refs[at : at + n_prior]
    at += n_prior
    acc_ref, out_ref = refs[at : at + 2]
    at += 2
    if n_last:
        last_ref = refs[at]
        at += 1
    hyper_stack = refs[at]
    weights = refs[at + 1 : at + 1 + n_chunks]
    at += 1 + n_chunks
    priors, sem = refs[at : at + n_prior], refs[at + n_prior]
    waits = [
        fetch_weights(i, chunks[i], order_ref[rank], weights[i], sem.at[pl.ds(2 * i, 2)])
        for i in range(n_chunks)
    ]
    planes = hyper_stack.shape[0]
    copies = []
    for j in range(n_prior):
        copies.append(
            pltpu.make_async_copy(prior_hbm[j].at[pl.ds(offsets[j], planes)], priors[j], sem.at[4 + j])
        )
        copies[-1].start()

    def stack_hyper(place, band, i):
        hyper_stack[place] = stack_taps(band[0, 0, i].astype(F32), 1.0)

    over_planes(bands, base, low, planes, stack_hyper)
    for wait in waits:
        wait()

    def weight(u):
        return weights[u // 4][:, UNIT * (u % 4) : UNIT * (u % 4 + 1)]

    outs = weights[0][:, 4 * UNIT : 4 * UNIT + 128].astype(F32)
    outs = jnp.concatenate([outs, jnp.zeros((16, 128), F32)], axis=0)
    out_ref[...] = outs.T.astype(BF)
    for j in range(n_last):
        last_ref[:, UNIT * j : UNIT * (j + 1)] = weight(n_prior + 1 + j)
    for copy in copies:
        copy.wait()

    @pl.loop(0, acc_ref.shape[0])
    def _(p):
        total = jnp.dot(weight(0), tap_group(hyper_stack, 4 * p), preferred_element_type=F32)
        for j in range(n_prior):
            total = total + jnp.dot(
                weight(j + 1),
                tap_group(priors[j], 4 * p),
                preferred_element_type=F32,
            )
        acc_ref[p] = total


def early(rank, slice_order, chunks, halos, stacks, n_last):
    reach = 2 * (3 - rank % 4)
    bands, base = bands_of(rank, halos)
    low, planes = -reach - 2, 8 + 2 * reach
    groups = (planes - 4) // 4
    shapes = [jax.ShapeDtypeStruct((groups, HALF, 4 * LAT), F32), jax.ShapeDtypeStruct((128, 128), BF)]
    if n_last:
        shapes.append(jax.ShapeDtypeStruct((HALF, UNIT * n_last), BF))
    offsets = [low - start for start, _ in stacks]
    priors = [stack for _, stack in stacks]
    return pl.pallas_call(
        functools.partial(early_kernel, rank, len(bands), base, low, len(chunks), len(priors), offsets, n_last),
        grid=(1,),
        out_shape=shapes,
        in_specs=[SMEM] + [ANY] * sum(COUNTS[: len(chunks)]) + [band_spec(j, 1) for _, j in bands] + [HBM] * len(priors),
        out_specs=[whole(shape) for shape in shapes],
        scratch_shapes=[pltpu.VMEM((planes, 128, LAT), BF)]
        + [pltpu.VMEM((HALF, LANES[i]), BF) for i in range(len(chunks))]
        + [pltpu.VMEM((planes, 128, LAT), BF)] * len(priors)
        + [pltpu.SemaphoreType.DMA((4 + len(priors),))],
        compiler_params=PARAMS,
        cost_estimate=COST,
        name="early",
    )(slice_order, *[ref for chunk in chunks for ref in chunk], *[band for band, _ in bands], *priors)


ERF_TOP = (0.00022905065861350646, 0.0034082910107109506, 0.050955695062380861, 0.18520832239976145, 1.128379143519084)
ERF_LOW = (-1.1791602954361697e-7, 0.000023547966471313185, 0.0010179625278914885, 0.014070470171167667, 0.11098505178285362, 0.49746925110067538, 1.0)


def gelu(v):
    z = jnp.clip(v * 0.7071067811865476, -3.7439211627767994, 3.7439211627767994)
    square = z * z
    top = jnp.full_like(z, ERF_TOP[0])
    for c in ERF_TOP[1:]:
        top = top * square + c
    low = jnp.full_like(z, ERF_LOW[0])
    for c in ERF_LOW[1:]:
        low = low * square + c
    half = 0.5 * v
    return half + half * (z * top / low)


def finish_kernel(kind, n_bands, base, low, *refs):
    acc_hbm, out_ref = refs[:2]
    acc_ref, sem = refs[-2:]
    refs = refs[2:-2]
    copy = pltpu.make_async_copy(acc_hbm, acc_ref, sem)
    copy.start()
    stacks = []
    if kind == "newest":
        last_ref, own_ref, got_ref = refs[:3]
        bands = refs[3 : 3 + n_bands]
        part_ref, value_ref, stack_ref = refs[3 + n_bands :]
        stacks = [stack_ref]

        def decode(place, band, i):
            mean = own_ref[place].astype(F32) + got_ref[place].astype(F32)
            value = (band[0, 0, i].astype(F32) + mean).astype(BF)
            value_ref[place] = value
            stack_ref[place] = stack_taps(value.astype(F32), 0.0)

        over_planes(bands, base, low, own_ref.shape[0], decode)
    elif kind == "widened":
        last_ref = refs[0]
        part_ref, *stacks = refs[6:]
        widen_bands(refs[1:6], stacks)
    else:
        part_ref = refs[0]
    copy.wait()

    @pl.loop(0, acc_ref.shape[0])
    def _(p):
        total = acc_ref[p]
        for j, stack_ref in enumerate(stacks):
            total = total + jnp.dot(
                last_ref[:, UNIT * j : UNIT * (j + 1)], tap_group(stack_ref, 4 * p), preferred_element_type=F32
            )
        for h in range(2):
            hidden = gelu(total[:, 2 * LAT * h : 2 * LAT * (h + 1)]).astype(BF)
            part = jnp.dot(out_ref[:SW, :HALF], hidden, preferred_element_type=F32).astype(BF)
            part_ref[4 * p + 2 * h] = part[:, :LAT]
            part_ref[4 * p + 2 * h + 1] = part[:, LAT:]


def finish(kind, acc, outs, *more, rank=None, halos=None):
    lons = 4 * acc.shape[0]
    shapes = [jax.ShapeDtypeStruct((lons, SW, LAT), BF)]
    operands = [acc, outs, *more]
    specs = [HBM] + [whole(value) for value in operands[1:]]
    bands, base, low = [], 0, 0
    if kind == "newest":
        bands, base = bands_of(rank, halos)
        low = -2 * (3 - rank % 4)
        operands += [band for band, _ in bands]
        specs += [band_spec(j, 0) for _, j in bands]
        shapes.append(jax.ShapeDtypeStruct(more[1].shape, BF))
        shapes.append(jax.ShapeDtypeStruct((more[1].shape[0], 128, LAT), BF))
    elif kind == "widened":
        shapes += [jax.ShapeDtypeStruct((20, 128, LAT), BF)] * 4
    return pl.pallas_call(
        functools.partial(finish_kernel, kind, len(bands), base, low),
        grid=(1,),
        out_shape=shapes,
        in_specs=specs,
        out_specs=[whole(shape) for shape in shapes],
        scratch_shapes=[pltpu.VMEM(acc.shape, F32), pltpu.SemaphoreType.DMA],
        compiler_params=PARAMS,
        cost_estimate=COST,
        name="finish",
    )(*operands)


def widen_bands(bands, stacks):
    for j, stack_ref in enumerate(stacks):

        def widen(place, band, i, j=j, stack_ref=stack_ref):
            stack_ref[place] = stack_taps(band[j, i].astype(F32), 0.0)

        over_planes(bands, 0, 0, 20, widen)


TAPS = (((1, 0),), ((2, 0), (0, 1)))


def upsample_kernel(
    order_ref, beta_ref, gamma_ref, weight_ref,
    own_a, own_b, own_c, up_a, up_b, up_c,
    out0, out1, out2, out3, fields, normed, shifted, totals,
):
    for level, (first, second, third) in enumerate(((own_a, own_b, own_c), (up_a, up_b, up_c))):
        for k in range(8):
            rows = pl.ds(pl.multiple_of(order_ref[k] * SW, 8), SW)
            for x in range(5):
                if k < 5:
                    plane = first[k, x]
                elif k < 7 or x < 4:
                    plane = second[5 * (k - 5) + x]
                else:
                    plane = third[0]
                fields[level, x, rows, :] = plane.astype(F32)
    gamma = gamma_ref[...].astype(BF)
    lane = lax.broadcasted_iota(jnp.int32, (320, LAT), 1)

    for level in range(2):

        @pl.loop(0, 5)
        def _(x, level=level):
            value = fields[level, x]
            energy = jnp.dot(gamma, (value * value).astype(BF), preferred_element_type=F32)
            field = (value * jnp.sqrt(energy + beta_ref[...])).astype(BF)
            normed[level, x] = field
            later = pltpu.roll(field.astype(F32), LAT - 1, 1)
            shifted[level, x] = jnp.where(lane == LAT - 1, 0.0, later).astype(BF)

    started = set()
    for dl in range(2):
        for dx in range(2):
            for dt in range(2):
                pars, rows = [], []
                for p in range(2):
                    for q in range(2):
                        for r in range(2):
                            for kl, ol in TAPS[p]:
                                for kx, ox in TAPS[q]:
                                    for kt, ot in TAPS[r]:
                                        if (ol, ox, ot) == (dl, dx, dt):
                                            tap = kl * 9 + kx * 3 + kt
                                            pars.append(4 * p + 2 * q + r)
                                            rows.append(weight_ref[32 * tap : 32 * tap + 32, :])
                source = (normed, shifted)[dt]
                field = jnp.concatenate([source[dl, dx + x] for x in range(4)], axis=1)
                got = jnp.dot(jnp.concatenate(rows, axis=0), field, preferred_element_type=F32)
                for i, par in enumerate(pars):
                    piece = got[32 * i : 32 * i + 32]
                    if par in started:
                        totals[par] += piece
                    else:
                        totals[par] = piece
                        started.add(par)
    source = lax.broadcasted_iota(jnp.int32, (2 * LAT, 2 * LAT), 0)
    target = lax.broadcasted_iota(jnp.int32, (2 * LAT, 2 * LAT), 1)
    mixing = (target == jnp.where(source < LAT, 2 * source, 2 * source - 2 * LAT + 1)).astype(F32).astype(BF)
    for p in range(2):
        rows = []
        for x in range(4):
            for q in range(2):
                even = totals[4 * p + 2 * q, :, LAT * x : LAT * x + LAT]
                odd = totals[4 * p + 2 * q + 1, :, LAT * x : LAT * x + LAT]
                rows.append(jnp.concatenate([even, odd], axis=1))
        mixed = jnp.dot(jnp.concatenate(rows, axis=0).astype(BF), mixing, preferred_element_type=F32)
        mixed = mixed.reshape(8, 4, 8, 2 * LAT)
        for relative, out_ref in enumerate((out0, out1, out2, out3)):
            out_ref[:, p] = jnp.transpose(mixed[:, relative], (1, 0, 2)).astype(BF)


def upsample(slice_order, beta, gamma, weight, own, up):
    shape = jax.ShapeDtypeStruct((8, 2, 8, 2 * LAT), BF)
    return pl.pallas_call(
        upsample_kernel,
        out_shape=[shape] * 4,
        in_specs=[SMEM] + [VMEM] * 9,
        out_specs=[VMEM] * 4,
        scratch_shapes=[
            pltpu.VMEM((2, 5, 320, LAT), F32),
            pltpu.VMEM((2, 5, 320, LAT), BF),
            pltpu.VMEM((2, 5, 320, LAT), BF),
            pltpu.VMEM((8, 32, 4 * LAT), F32),
        ],
        compiler_params=PARAMS,
        cost_estimate=COST,
        name="upsample",
    )(slice_order, beta, gamma, weight, *own, *up)


def place_kernel(in0, in1, in2, in3, out_ref):
    y_id = lax.axis_index("chan") % 4
    for relative, in_ref in enumerate((in0, in1, in2, in3)):
        level = (y_id + 4 - relative) % 4
        for o in range(8):
            for p in range(2):
                out_ref[o, 2 * level + p] = in_ref[o, p]


def place(pieces):
    return pl.pallas_call(
        place_kernel,
        out_shape=jax.ShapeDtypeStruct((8, 8, 8, 2 * LAT), BF),
        in_specs=[VMEM] * 4,
        out_specs=VMEM,
        compiler_params=PARAMS,
        cost_estimate=COST,
        name="place",
    )(*pieces)


def local(
    symbols,
    hyper_mean,
    slice_order,
    hyper_weight,
    ctx_weight,
    ctx_bias,
    out_weight,
    gdn_beta,
    gdn_gamma,
    tconv_weight,
):
    both = jnp.stack([symbols.astype(BF), hyper_mean])
    send = jnp.transpose(both, (2, 0, 3, 1, 4))
    send, pack_order = tie(jnp.concatenate([send, send]), slice_order)
    recv = lax.all_to_all(send, "chan", 0, 0)
    weights = (hyper_weight, ctx_weight, ctx_bias, out_weight)
    packed = pack(0, pack_order, *weights)
    later_order, _ = tie(slice_order, packed[0])
    later = pack(1, later_order, *weights)
    first, halos, (keep, keep_other, got) = first_spread(*packed, recv, slice_order, later)
    ranked = halos[2]
    chunks = [first]

    def centre(value, count):
        start = value.shape[0] // 2 - 2
        return value[start : start + count]

    def around(value):
        return [from_lon(value, d) if d else value for d in (-2, -1, 0, 1, 2)]

    values, stacks, part = [], [], None
    for k in range(8):
        if k == 4:
            acc, outs, last = early(k, slice_order, chunks, halos, [], 4)
            acc, tconv_weight = tie(acc, tconv_weight)
            tconv = [tconv_weight] + [from_y(tconv_weight, r) for r in range(1, 4)]
            part, *more = finish("widened", acc, outs, last, *wide)
            stacks = [(-8, stack) for stack in more]
        elif k == 0:
            acc, outs = early(k, slice_order, chunks, halos, [], 0)
            acc, got = tie(acc, got)
            pair = jnp.concatenate([keep, got])
            up, down = from_y(pair, -1), from_y(pair, 1)
            (part,) = finish("plain", acc, outs)
        else:
            acc, outs, last = early(k, slice_order, chunks, halos, stacks, 1)
            if k == 2:
                acc, up, down = tie(acc, up, down)
                far_k, far_g = from_y(up[:HALF], -1), from_y(down[HALF:], 1)
                near_o = core_swap(jnp.concatenate([up, down, got]))
            elif k == 3:
                acc, far_k, far_g, near_o = tie(acc, far_k, far_g, near_o)
                far_o = core_swap(jnp.concatenate([far_k, far_g]))
                chunks = [first, [pair, up, down, far_k, far_g, keep_other, near_o, far_o]]
            elif k == 5:
                acc, *tconv = tie(acc, *tconv)
            elif k == 7:
                acc, up_a = tie(acc, up_a)
            part, value, stack = finish(
                "newest", acc, outs, last, part, x_swap(part), rank=k - 1, halos=halos
            )
            values.append(value)
            stacks.append((-2 * (3 - (k - 1) % 4), stack))
        if k == 3:
            mean = part.astype(F32) + x_swap(part).astype(F32)
            newest = (ranked[k, 0].astype(F32) + mean).astype(BF)
            wide = around(jnp.stack([centre(value, 4) for value in values] + [newest]))
        if k == 5:
            block = jnp.concatenate([wide[2], wide[3][:, :1]], axis=1)
            own_a = jnp.concatenate([block] + [jnp.stack([centre(value, 5) for value in values[3:]])])
            down_one = [(i + 1, i) for i in range(8) if i % 4 < 3]
            up_a = lax.ppermute(own_a, "chan", down_one)
    mean = part.astype(F32) + x_swap(part).astype(F32)
    newest = (ranked[7, 0].astype(F32) + mean).astype(BF)
    own_b = jnp.concatenate([centre(values[-2], 5), centre(values[-1], 5), newest])
    edge = newest[:1]
    corner = [(i * 32 + (j + 1) % 32, (i - 1) * 32 + j) for i in range(8) if i % 4 > 0 for j in range(32)]
    own = [own_a, own_b, from_lon(edge, 1)]
    up = [up_a, lax.ppermute(own_b, "chan", down_one), lax.ppermute(edge, ("chan", "lon"), corner)]
    rows = jnp.stack(tconv, axis=1).reshape(27 * 32, 320)
    pieces = upsample(slice_order, gdn_beta[:, None], gdn_gamma, rows, own, up)
    return place([from_y(v, -r) if r else v for r, v in enumerate(pieces)])


def solution(mesh):
    placed = (
        P("chan", None, "lon", None),
        P("chan", None, "lon", None),
        P(),
        P("chan", None, None, None),
        P("chan", None, None, None),
        P("chan", None),
        P("chan", None, None),
        P(),
        P(),
        P(None, "chan", None),
    )
    return jax.shard_map(
        local, mesh=mesh, in_specs=placed, out_specs=P("chan", None, "lon", None), check_vma=False
    )
```

```python
import functools
import jax
import jax.numpy as jnp
from jax import lax
from jax.experimental import pallas as pl
from jax.experimental.pallas import tpu as pltpu
from jax.sharding import PartitionSpec as P

BF = jnp.bfloat16
F32 = jnp.float32
SW = 40
HALF = 112
LAT = 128
UNIT = 640
LANES = (2816, 2560)
ANY = pl.BlockSpec(memory_space=pl.ANY)
VMEM = pl.BlockSpec(memory_space=pltpu.VMEM)
HBM = pl.BlockSpec(memory_space=pltpu.HBM)
SMEM = pl.BlockSpec(memory_space=pltpu.SMEM)
COST = pl.CostEstimate(flops=200_000_000, bytes_accessed=1 << 20, transcendentals=0)
PARAMS = pltpu.CompilerParams(vmem_limit_bytes=16 << 20)


def x_swap(value):
    return lax.ppermute(value, "chan", [(i, i ^ 4) for i in range(8)])


def core_swap(value):
    return lax.ppermute(value, "lon", [(i, i ^ 1) for i in range(32)])


def from_y(value, distance):
    return lax.ppermute(
        value, "chan", [(i, (i // 4) * 4 + (i - distance) % 4) for i in range(8)]
    )


def from_lon(value, distance):
    return lax.ppermute(value, "lon", [(i, (i - distance) % 32) for i in range(32)])


def pack_kernel(chunk, order_ref, bias_ref, hyper_hbm, ctx_hbm, out_hbm, keep, keep_other, give, hyper_ref, out_ref, blocks, packed, sem):
    x_id = lax.axis_index("chan") // 4
    core = lax.axis_index("lon") % 2
    copies = []
    if chunk == 0:
        copies += [
            pltpu.make_async_copy(hyper_hbm, hyper_ref, sem.at[4]),
            pltpu.make_async_copy(out_hbm, out_ref, sem.at[5]),
        ]
    for j in range(3 + chunk):
        rows = pl.ds(pl.multiple_of(order_ref[3 * chunk + j] * SW, 8), SW)
        copies.append(pltpu.make_async_copy(ctx_hbm.at[:, rows, :], blocks.at[j], sem.at[j]))
    for copy in copies:
        copy.start()

    def put(u, taps, parts=None):
        for a in range(5):
            tail = jnp.zeros((8, 224), F32) if parts is None or a != 2 else parts
            block = jnp.concatenate([taps[3 * a + b].astype(F32) for b in range(3)] + [tail], axis=0)
            block = jnp.concatenate([block, jnp.zeros((128, 32), F32)], axis=1)
            lanes = UNIT * u + 128 * a
            packed[:, lanes : lanes + 128] = block.T[:224].astype(BF)

    if chunk == 0:
        bias = bias_ref[...]
        high = bias.astype(BF).astype(F32)
        mid = (bias - high).astype(BF).astype(F32)
        low = (bias - high - mid).astype(BF).astype(F32)
        copies.pop(0).wait()
        put(0, hyper_ref, jnp.concatenate([high, mid, low, jnp.zeros((5, 224), F32)], axis=0))
        copies.pop(0).wait()
        outs = jnp.concatenate([out_ref[...].astype(F32), jnp.zeros((88, 224), F32)], axis=0)
        outs = jnp.concatenate([outs, jnp.zeros((128, 32), F32)], axis=1)
        packed[:, 4 * UNIT : 4 * UNIT + 128] = outs.T[:224].astype(BF)
        packed[:, 4 * UNIT + 128 :] = jnp.zeros((224, 128), BF)
    for j, copy in enumerate(copies):
        copy.wait()
        put(1 - chunk + j, blocks.at[j])
    lanes = LANES[chunk] // 2
    near = pl.ds(pl.multiple_of(core * lanes, 128), lanes)
    away = pl.ds(pl.multiple_of((1 - core) * lanes, 128), lanes)
    own = pl.ds(pl.multiple_of(HALF * x_id, 16), HALF)
    theirs = pl.ds(pl.multiple_of(HALF * (1 - x_id), 16), HALF)
    keep[...] = packed[own, near]
    keep_other[...] = packed[own, away]
    give[...] = packed[theirs, near]


def pack(chunk, slice_order, hyper_weight, ctx_weight, ctx_bias, out_weight):
    ctx = jnp.transpose(ctx_weight[0], (0, 2, 1))
    hyper = jnp.transpose(hyper_weight[0], (0, 2, 1))
    return pl.pallas_call(
        functools.partial(pack_kernel, chunk),
        out_shape=[jax.ShapeDtypeStruct((HALF, LANES[chunk] // 2), BF)] * 3,
        in_specs=[SMEM, VMEM, HBM, HBM, HBM],
        out_specs=[VMEM] * 3,
        scratch_shapes=[
            pltpu.VMEM((15, SW, 224), BF),
            pltpu.VMEM((SW, 224), BF),
            pltpu.VMEM((4, 15, SW, 224), BF),
            pltpu.VMEM((224, LANES[chunk]), BF),
            pltpu.SemaphoreType.DMA((6,)),
        ],
        compiler_params=pltpu.CompilerParams(vmem_limit_bytes=(60, 16)[chunk] << 20),
        cost_estimate=COST,
        name="pack",
    )(slice_order, ctx_bias, hyper, ctx, out_weight[0])


def tie(*values):
    return lax.optimization_barrier(values)


def first_spread(keep, keep_other, give, recv, slice_order, later):
    up_k, down_k = from_y(keep, -1), from_y(keep, 1)
    got = x_swap(give)
    ranked, far = to_ranks(slice_order, recv)
    up_k, down_k, got, *later = tie(up_k, down_k, got, *later)
    up_g, down_g = from_y(got, -1), from_y(got, 1)
    far_k = from_y(up_k, -1)
    left2, right2 = from_lon(far, -2), from_lon(far, 2)
    up_g, down_g, far_k, left2, right2, ranked, later_give = tie(
        up_g, down_g, far_k, left2, right2, ranked, later[2]
    )
    later_got = x_swap(later_give)
    far_g = from_y(down_g, 1)
    left1, right1 = from_lon(ranked, -1), from_lon(ranked, 1)
    near_o = core_swap(jnp.concatenate([up_k, up_g, down_k, down_g, got]))
    far_o = core_swap(jnp.concatenate([far_k, far_g]))
    chunk = [keep, got, up_k, up_g, down_k, down_g, far_k, far_g, keep_other, near_o, far_o]
    return chunk, (left2, left1, ranked, right1, right2), (later[0], later[1], later_got)


def chunk_views(chunk, refs):
    def rows(ref, i):
        return ref.at[pl.ds(HALF * i, HALF)]

    if chunk == 0:
        views = refs[:8]
        keep_o, near_o, far_o = refs[8:]
    else:
        pair, up, down, far_k, far_g, keep_o, near_o, far_o = refs
        views = [rows(ref, i) for ref in (pair, up, down) for i in range(2)] + [far_k, far_g]
    keep, got, up_k, up_g, down_k, down_g, far_k, far_g = views
    return {
        (0, 0): (keep, keep_o),
        (0, 1): (got, rows(near_o, 4)),
        (1, 0): (down_k, rows(near_o, 2)),
        (1, 1): (down_g, rows(near_o, 3)),
        (2, 0): (far_k, rows(far_o, 0)),
        (2, 1): (far_g, rows(far_o, 1)),
        (3, 0): (up_k, rows(near_o, 0)),
        (3, 1): (up_g, rows(near_o, 1)),
    }


def fetch_weights(chunk_id, refs, slice_id, dest, sem):
    chan = lax.axis_index("chan")
    core = lax.axis_index("lon") % 2
    relative = (slice_id + 4 - chan % 4) % 4
    side = (slice_id // 4 + chan // 4) % 2
    lanes = LANES[chunk_id] // 2
    mine = dest.at[:, pl.ds(pl.multiple_of(core * lanes, 128), lanes)]
    other = dest.at[:, pl.ds(pl.multiple_of((1 - core) * lanes, 128), lanes)]
    choices = chunk_views(chunk_id, refs)
    for (r, i), (first, second) in choices.items():

        @pl.when((relative == r) & (side == i))
        def _(first=first, second=second):
            pltpu.make_async_copy(first, mine, sem.at[0]).start()
            pltpu.make_async_copy(second, other, sem.at[1]).start()

    def wait():
        pltpu.make_async_copy(choices[2, 0][0], mine, sem.at[0]).wait()
        pltpu.make_async_copy(choices[0, 0][1], other, sem.at[1]).wait()

    return wait


def rank_kernel(order_ref, recv_ref, ranked_ref, far_ref):
    for k in range(8):
        s = order_ref[k]

        @pl.loop(0, 8)
        def _(i, s=s, k=k):
            plane = recv_ref[s * 8 + i]
            ranked_ref[k * 8 + i] = plane
            if k % 4 < 2:
                far_ref[(k // 4 * 2 + k % 4) * 8 + i] = plane


def to_ranks(slice_order, recv):
    ranked, far = pl.pallas_call(
        rank_kernel,
        out_shape=[jax.ShapeDtypeStruct((64, SW, LAT), BF), jax.ShapeDtypeStruct((32, SW, LAT), BF)],
        in_specs=[SMEM, VMEM],
        out_specs=[VMEM] * 2,
        compiler_params=PARAMS,
        cost_estimate=COST,
        name="rank",
    )(slice_order, recv.reshape(64, SW, LAT))
    return ranked.reshape(8, 2, 4, SW, LAT), far.reshape(4, 2, 4, SW, LAT)


def stack_taps(plane, fill):
    lane = lax.broadcasted_iota(jnp.int32, plane.shape, 1)
    before = jnp.where(lane == 0, 0.0, pltpu.roll(plane, 1, 1))
    after = jnp.where(lane == LAT - 1, 0.0, pltpu.roll(plane, LAT - 1, 1))
    tail = jnp.full((8, LAT), fill, F32)
    return jnp.concatenate([before, plane, after, tail], axis=0).astype(BF)


def tap_group(stack_ref, start):
    longitudes = [stack_ref[pl.ds(start + i, 5)].reshape(UNIT, LAT) for i in range(4)]
    return jnp.concatenate(longitudes, axis=1)


def bands_of(k, halos):
    left2, left1, ranked, right1, right2 = halos
    if k % 4 < 2:
        j = k // 4 * 2 + k % 4
        return [(left2, j), (left1, k), (ranked, k), (right1, k), (right2, j)], -8
    return [(left1, k), (ranked, k), (right1, k)], -4


def band_spec(rank, kind):
    return pl.BlockSpec((1, 1, 4, SW, LAT), lambda i: (rank, kind, 0, 0, 0))


def whole(value):
    return pl.BlockSpec(value.shape, lambda i: (0,) * value.ndim)


def over_planes(bands, base, low, count, body):
    for b, band in enumerate(bands):
        for i in range(4):
            spot = base + 4 * b + i - low
            if 0 <= spot < count:
                body(spot, band, i)


COUNTS = (11, 8)


def early_kernel(rank, n_bands, base, low, n_chunks, n_prior, offsets, n_last, *refs):
    order_ref = refs[0]
    chunks = [refs[1:12], refs[12:20]][:n_chunks]
    at = 1 + sum(COUNTS[:n_chunks])
    bands = refs[at : at + n_bands]
    at += n_bands
    prior_hbm = refs[at : at + n_prior]
    at += n_prior
    acc_ref, out_ref = refs[at : at + 2]
    at += 2
    if n_last:
        last_ref = refs[at]
        at += 1
    hyper_stack = refs[at]
    weights = refs[at + 1 : at + 1 + n_chunks]
    at += 1 + n_chunks
    priors, sem = refs[at : at + n_prior], refs[at + n_prior]
    waits = [
        fetch_weights(i, chunks[i], order_ref[rank], weights[i], sem.at[pl.ds(2 * i, 2)])
        for i in range(n_chunks)
    ]
    planes = hyper_stack.shape[0]
    copies = []
    for j in range(n_prior):
        copies.append(
            pltpu.make_async_copy(prior_hbm[j].at[pl.ds(offsets[j], planes)], priors[j], sem.at[4 + j])
        )
        copies[-1].start()

    def stack_hyper(place, band, i):
        hyper_stack[place] = stack_taps(band[0, 0, i].astype(F32), 1.0)

    over_planes(bands, base, low, planes, stack_hyper)
    for wait in waits:
        wait()

    def weight(u):
        return weights[u // 4][:, UNIT * (u % 4) : UNIT * (u % 4 + 1)]

    outs = weights[0][:, 4 * UNIT : 4 * UNIT + 128].astype(F32)
    outs = jnp.concatenate([outs, jnp.zeros((16, 128), F32)], axis=0)
    out_ref[...] = outs.T.astype(BF)
    for j in range(n_last):
        last_ref[:, UNIT * j : UNIT * (j + 1)] = weight(n_prior + 1 + j)
    for copy in copies:
        copy.wait()

    @pl.loop(0, acc_ref.shape[0])
    def _(p):
        total = jnp.dot(weight(0), tap_group(hyper_stack, 4 * p), preferred_element_type=F32)
        for j in range(n_prior):
            total = total + jnp.dot(
                weight(j + 1),
                tap_group(priors[j], 4 * p),
                preferred_element_type=F32,
            )
        acc_ref[p] = total


def early(rank, slice_order, chunks, halos, stacks, n_last):
    reach = 2 * (3 - rank % 4)
    bands, base = bands_of(rank, halos)
    low, planes = -reach - 2, 8 + 2 * reach
    groups = (planes - 4) // 4
    shapes = [jax.ShapeDtypeStruct((groups, HALF, 4 * LAT), F32), jax.ShapeDtypeStruct((128, 128), BF)]
    if n_last:
        shapes.append(jax.ShapeDtypeStruct((HALF, UNIT * n_last), BF))
    offsets = [low - start for start, _ in stacks]
    priors = [stack for _, stack in stacks]
    return pl.pallas_call(
        functools.partial(early_kernel, rank, len(bands), base, low, len(chunks), len(priors), offsets, n_last),
        grid=(1,),
        out_shape=shapes,
        in_specs=[SMEM] + [ANY] * sum(COUNTS[: len(chunks)]) + [band_spec(j, 1) for _, j in bands] + [HBM] * len(priors),
        out_specs=[whole(shape) for shape in shapes],
        scratch_shapes=[pltpu.VMEM((planes, 128, LAT), BF)]
        + [pltpu.VMEM((HALF, LANES[i]), BF) for i in range(len(chunks))]
        + [pltpu.VMEM((planes, 128, LAT), BF)] * len(priors)
        + [pltpu.SemaphoreType.DMA((4 + len(priors),))],
        compiler_params=PARAMS,
        cost_estimate=COST,
        name="early",
    )(slice_order, *[ref for chunk in chunks for ref in chunk], *[band for band, _ in bands], *priors)


ERF_TOP = (0.00022905065861350646, 0.0034082910107109506, 0.050955695062380861, 0.18520832239976145, 1.128379143519084)
ERF_LOW = (-1.1791602954361697e-7, 0.000023547966471313185, 0.0010179625278914885, 0.014070470171167667, 0.11098505178285362, 0.49746925110067538, 1.0)


def gelu(v):
    z = jnp.clip(v * 0.7071067811865476, -3.7439211627767994, 3.7439211627767994)
    square = z * z
    top = jnp.full_like(z, ERF_TOP[0])
    for c in ERF_TOP[1:]:
        top = top * square + c
    low = jnp.full_like(z, ERF_LOW[0])
    for c in ERF_LOW[1:]:
        low = low * square + c
    half = 0.5 * v
    return half + half * (z * top / low)


def finish_kernel(kind, n_bands, base, low, *refs):
    acc_hbm, out_ref = refs[:2]
    acc_ref, sem = refs[-2:]
    refs = refs[2:-2]
    copy = pltpu.make_async_copy(acc_hbm, acc_ref, sem)
    copy.start()
    stacks = []
    if kind == "newest":
        last_ref, own_ref, got_ref = refs[:3]
        bands = refs[3 : 3 + n_bands]
        part_ref, value_ref, stack_ref = refs[3 + n_bands :]
        stacks = [stack_ref]

        def decode(place, band, i):
            mean = own_ref[place].astype(F32) + got_ref[place].astype(F32)
            value = (band[0, 0, i].astype(F32) + mean).astype(BF)
            value_ref[place] = value
            stack_ref[place] = stack_taps(value.astype(F32), 0.0)

        over_planes(bands, base, low, own_ref.shape[0], decode)
    elif kind == "widened":
        last_ref = refs[0]
        part_ref, *stacks = refs[6:]
        widen_bands(refs[1:6], stacks)
    else:
        part_ref = refs[0]
    copy.wait()

    @pl.loop(0, acc_ref.shape[0])
    def _(p):
        total = acc_ref[p]
        for j, stack_ref in enumerate(stacks):
            total = total + jnp.dot(
                last_ref[:, UNIT * j : UNIT * (j + 1)], tap_group(stack_ref, 4 * p), preferred_element_type=F32
            )
        for h in range(2):
            hidden = gelu(total[:, 2 * LAT * h : 2 * LAT * (h + 1)]).astype(BF)
            part = jnp.dot(out_ref[:SW, :HALF], hidden, preferred_element_type=F32).astype(BF)
            part_ref[4 * p + 2 * h] = part[:, :LAT]
            part_ref[4 * p + 2 * h + 1] = part[:, LAT:]


def finish(kind, acc, outs, *more, rank=None, halos=None):
    lons = 4 * acc.shape[0]
    shapes = [jax.ShapeDtypeStruct((lons, SW, LAT), BF)]
    operands = [acc, outs, *more]
    specs = [HBM] + [whole(value) for value in operands[1:]]
    bands, base, low = [], 0, 0
    if kind == "newest":
        bands, base = bands_of(rank, halos)
        low = -2 * (3 - rank % 4)
        operands += [band for band, _ in bands]
        specs += [band_spec(j, 0) for _, j in bands]
        shapes.append(jax.ShapeDtypeStruct(more[1].shape, BF))
        shapes.append(jax.ShapeDtypeStruct((more[1].shape[0], 128, LAT), BF))
    elif kind == "widened":
        shapes += [jax.ShapeDtypeStruct((20, 128, LAT), BF)] * 4
    return pl.pallas_call(
        functools.partial(finish_kernel, kind, len(bands), base, low),
        grid=(1,),
        out_shape=shapes,
        in_specs=specs,
        out_specs=[whole(shape) for shape in shapes],
        scratch_shapes=[pltpu.VMEM(acc.shape, F32), pltpu.SemaphoreType.DMA],
        compiler_params=PARAMS,
        cost_estimate=COST,
        name="finish",
    )(*operands)


def widen_bands(bands, stacks):
    for j, stack_ref in enumerate(stacks):

        def widen(place, band, i, j=j, stack_ref=stack_ref):
            stack_ref[place] = stack_taps(band[j, i].astype(F32), 0.0)

        over_planes(bands, 0, 0, 20, widen)


TAPS = (((1, 0),), ((2, 0), (0, 1)))


def upsample_kernel(
    order_ref, beta_ref, gamma_ref, weight_ref,
    own_a, own_b, own_c, up_a, up_b, up_c,
    out_ref, fields, normed, shifted, totals,
):
    for level, (first, second, third) in enumerate(((own_a, own_b, own_c), (up_a, up_b, up_c))):
        for k in range(8):
            rows = pl.ds(pl.multiple_of(order_ref[k] * SW, 8), SW)
            for x in range(5):
                if k < 5:
                    plane = first[k, x]
                elif k < 7 or x < 4:
                    plane = second[5 * (k - 5) + x]
                else:
                    plane = third[0]
                fields[level, x, rows, :] = plane.astype(F32)
    gamma = gamma_ref[...].astype(BF)
    lane = lax.broadcasted_iota(jnp.int32, (320, LAT), 1)

    for level in range(2):

        @pl.loop(0, 5)
        def _(x, level=level):
            value = fields[level, x]
            energy = jnp.dot(gamma, (value * value).astype(BF), preferred_element_type=F32)
            field = (value * jnp.sqrt(energy + beta_ref[...])).astype(BF)
            normed[level, x] = field
            later = pltpu.roll(field.astype(F32), LAT - 1, 1)
            shifted[level, x] = jnp.where(lane == LAT - 1, 0.0, later).astype(BF)

    y_id = lax.axis_index("chan") % 4
    started = set()
    for dl in range(2):
        for dx in range(2):
            for dt in range(2):
                pars, rows = [], []
                for p in range(2):
                    for q in range(2):
                        for r in range(2):
                            for kl, ol in TAPS[p]:
                                for kx, ox in TAPS[q]:
                                    for kt, ot in TAPS[r]:
                                        if (ol, ox, ot) == (dl, dx, dt):
                                            tap = kl * 9 + kx * 3 + kt
                                            pars.append(4 * p + 2 * q + r)
                                            rows.append(weight_ref[32 * tap : 32 * tap + 32, :])
                source = (normed, shifted)[dt]
                field = jnp.concatenate([source[dl, dx + x] for x in range(4)], axis=1)
                got = jnp.dot(jnp.concatenate(rows, axis=0), field, preferred_element_type=F32)
                for i, par in enumerate(pars):
                    piece = got[32 * i : 32 * i + 32]
                    if par in started:
                        totals[par] += piece
                    else:
                        totals[par] = piece
                        started.add(par)
    source = lax.broadcasted_iota(jnp.int32, (2 * LAT, 2 * LAT), 0)
    target = lax.broadcasted_iota(jnp.int32, (2 * LAT, 2 * LAT), 1)
    mixing = (target == jnp.where(source < LAT, 2 * source, 2 * source - 2 * LAT + 1)).astype(F32).astype(BF)
    for p in range(2):
        rows = []
        for x in range(4):
            for q in range(2):
                even = totals[4 * p + 2 * q, :, LAT * x : LAT * x + LAT]
                odd = totals[4 * p + 2 * q + 1, :, LAT * x : LAT * x + LAT]
                rows.append(jnp.concatenate([even, odd], axis=1))
        mixed = jnp.dot(jnp.concatenate(rows, axis=0).astype(BF), mixing, preferred_element_type=F32)
        mixed = mixed.reshape(8, 4, 8, 2 * LAT)
        for relative in range(4):
            piece = jnp.transpose(mixed[:, relative], (1, 0, 2)).astype(BF)
            out_ref[(y_id + relative) % 4, :, p] = piece


def upsample(slice_order, beta, gamma, weight, own, up):
    return pl.pallas_call(
        upsample_kernel,
        out_shape=jax.ShapeDtypeStruct((4, 8, 2, 8, 2 * LAT), BF),
        in_specs=[SMEM] + [VMEM] * 9,
        out_specs=VMEM,
        scratch_shapes=[
            pltpu.VMEM((2, 5, 320, LAT), F32),
            pltpu.VMEM((2, 5, 320, LAT), BF),
            pltpu.VMEM((2, 5, 320, LAT), BF),
            pltpu.VMEM((8, 32, 4 * LAT), F32),
        ],
        compiler_params=PARAMS,
        cost_estimate=COST,
        name="upsample",
    )(slice_order, beta, gamma, weight, *own, *up)


def place_kernel(in_ref, out_ref):
    for level in range(4):
        for o in range(8):
            for p in range(2):
                out_ref[o, 2 * level + p] = in_ref[level, o, p]


def place(pieces):
    return pl.pallas_call(
        place_kernel,
        out_shape=jax.ShapeDtypeStruct((8, 8, 8, 2 * LAT), BF),
        in_specs=[VMEM],
        out_specs=VMEM,
        compiler_params=PARAMS,
        cost_estimate=COST,
        name="place",
    )(pieces)


def local(
    symbols,
    hyper_mean,
    slice_order,
    hyper_weight,
    ctx_weight,
    ctx_bias,
    out_weight,
    gdn_beta,
    gdn_gamma,
    tconv_weight,
):
    both = jnp.stack([symbols.astype(BF), hyper_mean])
    send = jnp.transpose(both, (2, 0, 3, 1, 4))
    send, pack_order = tie(jnp.concatenate([send, send]), slice_order)
    recv = lax.all_to_all(send, "chan", 0, 0)
    weights = (hyper_weight, ctx_weight, ctx_bias, out_weight)
    packed = pack(0, pack_order, *weights)
    later_order, _ = tie(slice_order, packed[0])
    later = pack(1, later_order, *weights)
    first, halos, (keep, keep_other, got) = first_spread(*packed, recv, slice_order, later)
    ranked = halos[2]
    chunks = [first]

    def centre(value, count):
        start = value.shape[0] // 2 - 2
        return value[start : start + count]

    def around(value):
        return [from_lon(value, d) if d else value for d in (-2, -1, 0, 1, 2)]

    values, stacks, part = [], [], None
    for k in range(8):
        if k == 4:
            acc, outs, last = early(k, slice_order, chunks, halos, [], 4)
            acc, tconv_weight = tie(acc, tconv_weight)
            tconv = [tconv_weight] + [from_y(tconv_weight, r) for r in range(1, 4)]
            part, *more = finish("widened", acc, outs, last, *wide)
            stacks = [(-8, stack) for stack in more]
        elif k == 0:
            acc, outs = early(k, slice_order, chunks, halos, [], 0)
            (part,) = finish("plain", acc, outs)
        else:
            acc, outs, last = early(k, slice_order, chunks, halos, stacks, 1)
            swapped = x_swap(part)
            if k == 1:
                acc, got, swapped = tie(acc, got, swapped)
                pair = jnp.concatenate([keep, got])
                up, down = from_y(pair, -1), from_y(pair, 1)
            elif k == 3:
                acc, up, down, swapped = tie(acc, up, down, swapped)
                far_k, far_g = from_y(up[:HALF], -1), from_y(down[HALF:], 1)
                near_o = core_swap(jnp.concatenate([up, down, got]))
            elif k == 5:
                acc, *tconv = tie(acc, *tconv)
            elif k == 7:
                acc, up_a = tie(acc, up_a)
            part, value, stack = finish(
                "newest", acc, outs, last, part, swapped, rank=k - 1, halos=halos
            )
            values.append(value)
            stacks.append((-2 * (3 - (k - 1) % 4), stack))
        if k == 3:
            mean = part.astype(F32) + x_swap(part).astype(F32)
            newest = (ranked[k, 0].astype(F32) + mean).astype(BF)
            far_k, far_g, _ = tie(far_k, far_g, newest)
            newest, near_o = tie(newest, near_o)
            far_o = core_swap(jnp.concatenate([far_k, far_g]))
            chunks = [first, [pair, up, down, far_k, far_g, keep_other, near_o, far_o]]
            wide = around(jnp.stack([centre(value, 4) for value in values] + [newest]))
        if k == 5:
            block = jnp.concatenate([wide[2], wide[3][:, :1]], axis=1)
            own_a = jnp.concatenate([block] + [jnp.stack([centre(value, 5) for value in values[3:]])])
            down_one = [(i + 1, i) for i in range(8) if i % 4 < 3]
            up_a = lax.ppermute(own_a, "chan", down_one)
    mean = part.astype(F32) + x_swap(part).astype(F32)
    newest = (ranked[7, 0].astype(F32) + mean).astype(BF)
    own_b = jnp.concatenate([centre(values[-2], 5), centre(values[-1], 5), newest])
    edge = newest[:1]
    corner = [(i * 32 + (j + 1) % 32, (i - 1) * 32 + j) for i in range(8) if i % 4 > 0 for j in range(32)]
    own = [own_a, own_b, from_lon(edge, 1)]
    up = [up_a, lax.ppermute(own_b, "chan", down_one), lax.ppermute(edge, ("chan", "lon"), corner)]
    rows = jnp.stack(tconv, axis=1).reshape(27 * 32, 320)
    pieces = upsample(slice_order, gdn_beta[:, None], gdn_gamma, rows, own, up)
    groups = [[0, 1, 2, 3], [4, 5, 6, 7]]
    return place(lax.all_to_all(pieces, "chan", 0, 0, axis_index_groups=groups))


def solution(mesh):
    placed = (
        P("chan", None, "lon", None),
        P("chan", None, "lon", None),
        P(),
        P("chan", None, None, None),
        P("chan", None, None, None),
        P("chan", None),
        P("chan", None, None),
        P(),
        P(),
        P(None, "chan", None),
    )
    return jax.shard_map(
        local, mesh=mesh, in_specs=placed, out_specs=P("chan", None, "lon", None), check_vma=False
    )
```

```python
import functools
import jax
import jax.numpy as jnp
from jax import lax
from jax.experimental import pallas as pl
from jax.experimental.pallas import tpu as pltpu
from jax.sharding import PartitionSpec as P

BF = jnp.bfloat16
F32 = jnp.float32
SW = 40
HALF = 112
LAT = 128
UNIT = 640
LANES = (2816, 2560)
ANY = pl.BlockSpec(memory_space=pl.ANY)
VMEM = pl.BlockSpec(memory_space=pltpu.VMEM)
HBM = pl.BlockSpec(memory_space=pltpu.HBM)
SMEM = pl.BlockSpec(memory_space=pltpu.SMEM)
COST = pl.CostEstimate(flops=200_000_000, bytes_accessed=1 << 20, transcendentals=0)
PARAMS = pltpu.CompilerParams(vmem_limit_bytes=16 << 20)


def x_swap(value):
    return lax.ppermute(value, "chan", [(i, i ^ 4) for i in range(8)])


def core_swap(value):
    return lax.ppermute(value, "lon", [(i, i ^ 1) for i in range(32)])


def from_y(value, distance):
    return lax.ppermute(
        value, "chan", [(i, (i // 4) * 4 + (i - distance) % 4) for i in range(8)]
    )


def from_lon(value, distance):
    return lax.ppermute(value, "lon", [(i, (i - distance) % 32) for i in range(32)])


def pack_kernel(chunk, order_ref, bias_ref, hyper_hbm, ctx_hbm, out_hbm, keep, keep_other, give, hyper_ref, out_ref, blocks, packed, sem):
    x_id = lax.axis_index("chan") // 4
    core = lax.axis_index("lon") % 2
    copies = []
    if chunk == 0:
        copies += [
            pltpu.make_async_copy(hyper_hbm, hyper_ref, sem.at[4]),
            pltpu.make_async_copy(out_hbm, out_ref, sem.at[5]),
        ]
    for j in range(3 + chunk):
        rows = pl.ds(pl.multiple_of(order_ref[3 * chunk + j] * SW, 8), SW)
        copies.append(pltpu.make_async_copy(ctx_hbm.at[:, rows, :], blocks.at[j], sem.at[j]))
    for copy in copies:
        copy.start()

    def put(u, taps, parts=None):
        for a in range(5):
            tail = jnp.zeros((8, 224), F32) if parts is None or a != 2 else parts
            block = jnp.concatenate([taps[3 * a + b].astype(F32) for b in range(3)] + [tail], axis=0)
            block = jnp.concatenate([block, jnp.zeros((128, 32), F32)], axis=1)
            lanes = UNIT * u + 128 * a
            packed[:, lanes : lanes + 128] = block.T[:224].astype(BF)

    if chunk == 0:
        bias = bias_ref[...]
        high = bias.astype(BF).astype(F32)
        mid = (bias - high).astype(BF).astype(F32)
        low = (bias - high - mid).astype(BF).astype(F32)
        copies.pop(0).wait()
        put(0, hyper_ref, jnp.concatenate([high, mid, low, jnp.zeros((5, 224), F32)], axis=0))
        copies.pop(0).wait()
        outs = jnp.concatenate([out_ref[...].astype(F32), jnp.zeros((88, 224), F32)], axis=0)
        outs = jnp.concatenate([outs, jnp.zeros((128, 32), F32)], axis=1)
        packed[:, 4 * UNIT : 4 * UNIT + 128] = outs.T[:224].astype(BF)
        packed[:, 4 * UNIT + 128 :] = jnp.zeros((224, 128), BF)
    for j, copy in enumerate(copies):
        copy.wait()
        put(1 - chunk + j, blocks.at[j])
    lanes = LANES[chunk] // 2
    near = pl.ds(pl.multiple_of(core * lanes, 128), lanes)
    away = pl.ds(pl.multiple_of((1 - core) * lanes, 128), lanes)
    own = pl.ds(pl.multiple_of(HALF * x_id, 16), HALF)
    theirs = pl.ds(pl.multiple_of(HALF * (1 - x_id), 16), HALF)
    keep[...] = packed[own, near]
    keep_other[...] = packed[own, away]
    give[...] = packed[theirs, near]


def pack(chunk, slice_order, hyper_weight, ctx_weight, ctx_bias, out_weight):
    ctx = jnp.transpose(ctx_weight[0], (0, 2, 1))
    hyper = jnp.transpose(hyper_weight[0], (0, 2, 1))
    return pl.pallas_call(
        functools.partial(pack_kernel, chunk),
        out_shape=[jax.ShapeDtypeStruct((HALF, LANES[chunk] // 2), BF)] * 3,
        in_specs=[SMEM, VMEM, HBM, HBM, HBM],
        out_specs=[VMEM] * 3,
        scratch_shapes=[
            pltpu.VMEM((15, SW, 224), BF),
            pltpu.VMEM((SW, 224), BF),
            pltpu.VMEM((4, 15, SW, 224), BF),
            pltpu.VMEM((224, LANES[chunk]), BF),
            pltpu.SemaphoreType.DMA((6,)),
        ],
        compiler_params=pltpu.CompilerParams(vmem_limit_bytes=(60, 16)[chunk] << 20),
        cost_estimate=COST,
        name="pack",
    )(slice_order, ctx_bias, hyper, ctx, out_weight[0])


def tie(*values):
    return lax.optimization_barrier(values)


def first_spread(keep, keep_other, give, recv, slice_order, later):
    up_k, down_k = from_y(keep, -1), from_y(keep, 1)
    got = x_swap(give)
    ranked, far = to_ranks(slice_order, recv)
    up_k, down_k, got, *later = tie(up_k, down_k, got, *later)
    up_g, down_g = from_y(got, -1), from_y(got, 1)
    far_k = from_y(up_k, -1)
    left2, right2 = from_lon(far, -2), from_lon(far, 2)
    up_g, down_g, far_k, left2, right2, ranked, later_give = tie(
        up_g, down_g, far_k, left2, right2, ranked, later[2]
    )
    later_got = x_swap(later_give)
    far_g = from_y(down_g, 1)
    left1, right1 = from_lon(ranked, -1), from_lon(ranked, 1)
    near_o = core_swap(jnp.concatenate([up_k, up_g, down_k, down_g, got]))
    far_o = core_swap(jnp.concatenate([far_k, far_g]))
    chunk = [keep, got, up_k, up_g, down_k, down_g, far_k, far_g, keep_other, near_o, far_o]
    return chunk, (left2, left1, ranked, right1, right2), (later[0], later[1], later_got)


def chunk_views(chunk, refs):
    def rows(ref, i):
        return ref.at[pl.ds(HALF * i, HALF)]

    if chunk == 0:
        views = refs[:8]
        keep_o, near_o, far_o = refs[8:]
    else:
        pair, up, down, far_k, far_g, keep_o, near_o, far_o = refs
        views = [rows(ref, i) for ref in (pair, up, down) for i in range(2)] + [far_k, far_g]
    keep, got, up_k, up_g, down_k, down_g, far_k, far_g = views
    return {
        (0, 0): (keep, keep_o),
        (0, 1): (got, rows(near_o, 4)),
        (1, 0): (down_k, rows(near_o, 2)),
        (1, 1): (down_g, rows(near_o, 3)),
        (2, 0): (far_k, rows(far_o, 0)),
        (2, 1): (far_g, rows(far_o, 1)),
        (3, 0): (up_k, rows(near_o, 0)),
        (3, 1): (up_g, rows(near_o, 1)),
    }


def fetch_weights(chunk_id, refs, slice_id, dest, sem):
    chan = lax.axis_index("chan")
    core = lax.axis_index("lon") % 2
    relative = (slice_id + 4 - chan % 4) % 4
    side = (slice_id // 4 + chan // 4) % 2
    lanes = LANES[chunk_id] // 2
    mine = dest.at[:, pl.ds(pl.multiple_of(core * lanes, 128), lanes)]
    other = dest.at[:, pl.ds(pl.multiple_of((1 - core) * lanes, 128), lanes)]
    choices = chunk_views(chunk_id, refs)
    for (r, i), (first, second) in choices.items():

        @pl.when((relative == r) & (side == i))
        def _(first=first, second=second):
            pltpu.make_async_copy(first, mine, sem.at[0]).start()
            pltpu.make_async_copy(second, other, sem.at[1]).start()

    def wait():
        pltpu.make_async_copy(choices[2, 0][0], mine, sem.at[0]).wait()
        pltpu.make_async_copy(choices[0, 0][1], other, sem.at[1]).wait()

    return wait


def rank_kernel(order_ref, recv_ref, ranked_ref, far_ref):
    for k in range(8):
        s = order_ref[k]

        @pl.loop(0, 8)
        def _(i, s=s, k=k):
            plane = recv_ref[s * 8 + i]
            ranked_ref[k * 8 + i] = plane
            if k % 4 < 2:
                far_ref[(k // 4 * 2 + k % 4) * 8 + i] = plane


def to_ranks(slice_order, recv):
    ranked, far = pl.pallas_call(
        rank_kernel,
        out_shape=[jax.ShapeDtypeStruct((64, SW, LAT), BF), jax.ShapeDtypeStruct((32, SW, LAT), BF)],
        in_specs=[SMEM, VMEM],
        out_specs=[VMEM] * 2,
        compiler_params=PARAMS,
        cost_estimate=COST,
        name="rank",
    )(slice_order, recv.reshape(64, SW, LAT))
    return ranked.reshape(8, 2, 4, SW, LAT), far.reshape(4, 2, 4, SW, LAT)


def stack_taps(plane, fill):
    lane = lax.broadcasted_iota(jnp.int32, plane.shape, 1)
    before = jnp.where(lane == 0, 0.0, pltpu.roll(plane, 1, 1))
    after = jnp.where(lane == LAT - 1, 0.0, pltpu.roll(plane, LAT - 1, 1))
    tail = jnp.full((8, LAT), fill, F32)
    return jnp.concatenate([before, plane, after, tail], axis=0).astype(BF)


def tap_group(stack_ref, start):
    longitudes = [stack_ref[pl.ds(start + i, 5)].reshape(UNIT, LAT) for i in range(4)]
    return jnp.concatenate(longitudes, axis=1)


def bands_of(k, halos):
    left2, left1, ranked, right1, right2 = halos
    if k % 4 < 2:
        j = k // 4 * 2 + k % 4
        return [(left2, j), (left1, k), (ranked, k), (right1, k), (right2, j)], -8
    return [(left1, k), (ranked, k), (right1, k)], -4


def band_spec(rank, kind):
    return pl.BlockSpec((1, 1, 4, SW, LAT), lambda i: (rank, kind, 0, 0, 0))


def whole(value):
    return pl.BlockSpec(value.shape, lambda i: (0,) * value.ndim)


def over_planes(bands, base, low, count, body):
    for b, band in enumerate(bands):
        for i in range(4):
            spot = base + 4 * b + i - low
            if 0 <= spot < count:
                body(spot, band, i)


COUNTS = (11, 8)


def early_kernel(rank, n_bands, base, low, n_chunks, n_prior, offsets, n_last, *refs):
    order_ref = refs[0]
    chunks = [refs[1:12], refs[12:20]][:n_chunks]
    at = 1 + sum(COUNTS[:n_chunks])
    bands = refs[at : at + n_bands]
    at += n_bands
    prior_hbm = refs[at : at + n_prior]
    at += n_prior
    acc_ref, out_ref = refs[at : at + 2]
    at += 2
    if n_last:
        last_ref = refs[at]
        at += 1
    hyper_stack = refs[at]
    weights = refs[at + 1 : at + 1 + n_chunks]
    at += 1 + n_chunks
    priors, sem = refs[at : at + n_prior], refs[at + n_prior]
    waits = [
        fetch_weights(i, chunks[i], order_ref[rank], weights[i], sem.at[pl.ds(2 * i, 2)])
        for i in range(n_chunks)
    ]
    planes = hyper_stack.shape[0]
    copies = []
    for j in range(n_prior):
        copies.append(
            pltpu.make_async_copy(prior_hbm[j].at[pl.ds(offsets[j], planes)], priors[j], sem.at[4 + j])
        )
        copies[-1].start()

    def stack_hyper(place, band, i):
        hyper_stack[place] = stack_taps(band[0, 0, i].astype(F32), 1.0)

    over_planes(bands, base, low, planes, stack_hyper)
    for wait in waits:
        wait()

    def weight(u):
        return weights[u // 4][:, UNIT * (u % 4) : UNIT * (u % 4 + 1)]

    outs = weights[0][:, 4 * UNIT : 4 * UNIT + 128].astype(F32)
    outs = jnp.concatenate([outs, jnp.zeros((16, 128), F32)], axis=0)
    out_ref[...] = outs.T.astype(BF)
    for j in range(n_last):
        last_ref[:, UNIT * j : UNIT * (j + 1)] = weight(n_prior + 1 + j)
    for copy in copies:
        copy.wait()

    @pl.loop(0, acc_ref.shape[0])
    def _(p):
        total = jnp.dot(weight(0), tap_group(hyper_stack, 4 * p), preferred_element_type=F32)
        for j in range(n_prior):
            total = total + jnp.dot(
                weight(j + 1),
                tap_group(priors[j], 4 * p),
                preferred_element_type=F32,
            )
        acc_ref[p] = total


def early(rank, slice_order, chunks, halos, stacks, n_last):
    reach = 2 * (3 - rank % 4)
    bands, base = bands_of(rank, halos)
    low, planes = -reach - 2, 8 + 2 * reach
    groups = (planes - 4) // 4
    shapes = [jax.ShapeDtypeStruct((groups, HALF, 4 * LAT), F32), jax.ShapeDtypeStruct((128, 128), BF)]
    if n_last:
        shapes.append(jax.ShapeDtypeStruct((HALF, UNIT * n_last), BF))
    offsets = [low - start for start, _ in stacks]
    priors = [stack for _, stack in stacks]
    return pl.pallas_call(
        functools.partial(early_kernel, rank, len(bands), base, low, len(chunks), len(priors), offsets, n_last),
        grid=(1,),
        out_shape=shapes,
        in_specs=[SMEM] + [ANY] * sum(COUNTS[: len(chunks)]) + [band_spec(j, 1) for _, j in bands] + [HBM] * len(priors),
        out_specs=[whole(shape) for shape in shapes],
        scratch_shapes=[pltpu.VMEM((planes, 128, LAT), BF)]
        + [pltpu.VMEM((HALF, LANES[i]), BF) for i in range(len(chunks))]
        + [pltpu.VMEM((planes, 128, LAT), BF)] * len(priors)
        + [pltpu.SemaphoreType.DMA((4 + len(priors),))],
        compiler_params=PARAMS,
        cost_estimate=COST,
        name="early",
    )(slice_order, *[ref for chunk in chunks for ref in chunk], *[band for band, _ in bands], *priors)


ERF_TOP = (0.00022905065861350646, 0.0034082910107109506, 0.050955695062380861, 0.18520832239976145, 1.128379143519084)
ERF_LOW = (-1.1791602954361697e-7, 0.000023547966471313185, 0.0010179625278914885, 0.014070470171167667, 0.11098505178285362, 0.49746925110067538, 1.0)


def gelu(v):
    z = jnp.clip(v * 0.7071067811865476, -3.7439211627767994, 3.7439211627767994)
    square = z * z
    top = jnp.full_like(z, ERF_TOP[0])
    for c in ERF_TOP[1:]:
        top = top * square + c
    low = jnp.full_like(z, ERF_LOW[0])
    for c in ERF_LOW[1:]:
        low = low * square + c
    half = 0.5 * v
    return half + half * (z * top / low)


def finish_kernel(kind, n_bands, base, low, *refs):
    acc_hbm, out_ref = refs[:2]
    acc_ref, sem = refs[-2:]
    refs = refs[2:-2]
    copy = pltpu.make_async_copy(acc_hbm, acc_ref, sem)
    copy.start()
    stacks = []
    if kind == "newest":
        last_ref, own_ref, got_ref = refs[:3]
        bands = refs[3 : 3 + n_bands]
        part_ref, value_ref, stack_ref = refs[3 + n_bands :]
        stacks = [stack_ref]

        def decode(place, band, i):
            mean = own_ref[place].astype(F32) + got_ref[place].astype(F32)
            value = (band[0, 0, i].astype(F32) + mean).astype(BF)
            value_ref[place] = value
            stack_ref[place] = stack_taps(value.astype(F32), 0.0)

        over_planes(bands, base, low, own_ref.shape[0], decode)
    elif kind == "widened":
        last_ref = refs[0]
        part_ref, *stacks = refs[6:]
        widen_bands(refs[1:6], stacks)
    else:
        part_ref = refs[0]
    copy.wait()

    @pl.loop(0, acc_ref.shape[0])
    def _(p):
        total = acc_ref[p]
        for j, stack_ref in enumerate(stacks):
            total = total + jnp.dot(
                last_ref[:, UNIT * j : UNIT * (j + 1)], tap_group(stack_ref, 4 * p), preferred_element_type=F32
            )
        for h in range(2):
            hidden = gelu(total[:, 2 * LAT * h : 2 * LAT * (h + 1)]).astype(BF)
            part = jnp.dot(out_ref[:SW, :HALF], hidden, preferred_element_type=F32).astype(BF)
            part_ref[4 * p + 2 * h] = part[:, :LAT]
            part_ref[4 * p + 2 * h + 1] = part[:, LAT:]


def finish(kind, acc, outs, *more, rank=None, halos=None):
    lons = 4 * acc.shape[0]
    shapes = [jax.ShapeDtypeStruct((lons, SW, LAT), BF)]
    operands = [acc, outs, *more]
    specs = [HBM] + [whole(value) for value in operands[1:]]
    bands, base, low = [], 0, 0
    if kind == "newest":
        bands, base = bands_of(rank, halos)
        low = -2 * (3 - rank % 4)
        operands += [band for band, _ in bands]
        specs += [band_spec(j, 0) for _, j in bands]
        shapes.append(jax.ShapeDtypeStruct(more[1].shape, BF))
        shapes.append(jax.ShapeDtypeStruct((more[1].shape[0], 128, LAT), BF))
    elif kind == "widened":
        shapes += [jax.ShapeDtypeStruct((20, 128, LAT), BF)] * 4
    return pl.pallas_call(
        functools.partial(finish_kernel, kind, len(bands), base, low),
        grid=(1,),
        out_shape=shapes,
        in_specs=specs,
        out_specs=[whole(shape) for shape in shapes],
        scratch_shapes=[pltpu.VMEM(acc.shape, F32), pltpu.SemaphoreType.DMA],
        compiler_params=PARAMS,
        cost_estimate=COST,
        name="finish",
    )(*operands)


def widen_bands(bands, stacks):
    for j, stack_ref in enumerate(stacks):

        def widen(place, band, i, j=j, stack_ref=stack_ref):
            stack_ref[place] = stack_taps(band[j, i].astype(F32), 0.0)

        over_planes(bands, 0, 0, 20, widen)


TAPS = (((1, 0),), ((2, 0), (0, 1)))


def upsample_kernel(
    order_ref, beta_ref, gamma_ref, weight_ref,
    own_a, own_b, own_c, up_a, up_b, up_c,
    out0, out1, out2, out3, fields, normed, shifted, totals,
):
    for level, (first, second, third) in enumerate(((own_a, own_b, own_c), (up_a, up_b, up_c))):
        for k in range(8):
            rows = pl.ds(pl.multiple_of(order_ref[k] * SW, 8), SW)
            for x in range(5):
                if k < 5:
                    plane = first[k, x]
                elif k < 7 or x < 4:
                    plane = second[5 * (k - 5) + x]
                else:
                    plane = third[0]
                fields[level, x, rows, :] = plane.astype(F32)
    gamma = gamma_ref[...].astype(BF)
    lane = lax.broadcasted_iota(jnp.int32, (320, LAT), 1)

    for level in range(2):

        @pl.loop(0, 5)
        def _(x, level=level):
            value = fields[level, x]
            energy = jnp.dot(gamma, (value * value).astype(BF), preferred_element_type=F32)
            field = (value * jnp.sqrt(energy + beta_ref[...])).astype(BF)
            normed[level, x] = field
            later = pltpu.roll(field.astype(F32), LAT - 1, 1)
            shifted[level, x] = jnp.where(lane == LAT - 1, 0.0, later).astype(BF)

    started = set()
    for dl in range(2):
        for dx in range(2):
            for dt in range(2):
                pars, rows = [], []
                for p in range(2):
                    for q in range(2):
                        for r in range(2):
                            for kl, ol in TAPS[p]:
                                for kx, ox in TAPS[q]:
                                    for kt, ot in TAPS[r]:
                                        if (ol, ox, ot) == (dl, dx, dt):
                                            tap = kl * 9 + kx * 3 + kt
                                            pars.append(4 * p + 2 * q + r)
                                            rows.append(weight_ref[32 * tap : 32 * tap + 32, :])
                source = (normed, shifted)[dt]
                field = jnp.concatenate([source[dl, dx + x] for x in range(4)], axis=1)
                got = jnp.dot(jnp.concatenate(rows, axis=0), field, preferred_element_type=F32)
                for i, par in enumerate(pars):
                    piece = got[32 * i : 32 * i + 32]
                    if par in started:
                        totals[par] += piece
                    else:
                        totals[par] = piece
                        started.add(par)
    source = lax.broadcasted_iota(jnp.int32, (2 * LAT, 2 * LAT), 0)
    target = lax.broadcasted_iota(jnp.int32, (2 * LAT, 2 * LAT), 1)
    mixing = (target == jnp.where(source < LAT, 2 * source, 2 * source - 2 * LAT + 1)).astype(F32).astype(BF)
    for p in range(2):
        rows = []
        for x in range(4):
            for q in range(2):
                even = totals[4 * p + 2 * q, :, LAT * x : LAT * x + LAT]
                odd = totals[4 * p + 2 * q + 1, :, LAT * x : LAT * x + LAT]
                rows.append(jnp.concatenate([even, odd], axis=1))
        mixed = jnp.dot(jnp.concatenate(rows, axis=0).astype(BF), mixing, preferred_element_type=F32)
        mixed = mixed.reshape(8, 4, 8, 2 * LAT)
        for relative, out_ref in enumerate((out0, out1, out2, out3)):
            out_ref[:, p] = jnp.transpose(mixed[:, relative], (1, 0, 2)).astype(BF)


def upsample(slice_order, beta, gamma, weight, own, up):
    shape = jax.ShapeDtypeStruct((8, 2, 8, 2 * LAT), BF)
    return pl.pallas_call(
        upsample_kernel,
        out_shape=[shape] * 4,
        in_specs=[SMEM] + [VMEM] * 9,
        out_specs=[VMEM] * 4,
        scratch_shapes=[
            pltpu.VMEM((2, 5, 320, LAT), F32),
            pltpu.VMEM((2, 5, 320, LAT), BF),
            pltpu.VMEM((2, 5, 320, LAT), BF),
            pltpu.VMEM((8, 32, 4 * LAT), F32),
        ],
        compiler_params=PARAMS,
        cost_estimate=COST,
        name="upsample",
    )(slice_order, beta, gamma, weight, *own, *up)


def place_kernel(in0, in1, in2, in3, out_ref):
    y_id = lax.axis_index("chan") % 4
    for relative, in_ref in enumerate((in0, in1, in2, in3)):
        level = (y_id + 4 - relative) % 4
        for o in range(8):
            for p in range(2):
                out_ref[o, 2 * level + p] = in_ref[o, p]


def place(pieces):
    return pl.pallas_call(
        place_kernel,
        out_shape=jax.ShapeDtypeStruct((8, 8, 8, 2 * LAT), BF),
        in_specs=[VMEM] * 4,
        out_specs=VMEM,
        compiler_params=PARAMS,
        cost_estimate=COST,
        name="place",
    )(*pieces)


def local(
    symbols,
    hyper_mean,
    slice_order,
    hyper_weight,
    ctx_weight,
    ctx_bias,
    out_weight,
    gdn_beta,
    gdn_gamma,
    tconv_weight,
):
    both = jnp.stack([symbols.astype(BF), hyper_mean])
    send = jnp.transpose(both, (2, 0, 3, 1, 4))
    send, pack_order = tie(jnp.concatenate([send, send]), slice_order)
    recv = lax.all_to_all(send, "chan", 0, 0)
    weights = (hyper_weight, ctx_weight, ctx_bias, out_weight)
    packed = pack(0, pack_order, *weights)
    later_order, _ = tie(slice_order, packed[0])
    later = pack(1, later_order, *weights)
    first, halos, (keep, keep_other, got) = first_spread(*packed, recv, slice_order, later)
    ranked = halos[2]
    chunks = [first]

    def centre(value, count):
        start = value.shape[0] // 2 - 2
        return value[start : start + count]

    def around(value):
        return [from_lon(value, d) if d else value for d in (-2, -1, 0, 1, 2)]

    values, stacks, part = [], [], None
    for k in range(8):
        if k == 4:
            acc, outs, last = early(k, slice_order, chunks, halos, [], 4)
            acc, tconv_weight = tie(acc, tconv_weight)
            tconv = [tconv_weight] + [from_y(tconv_weight, r) for r in range(1, 4)]
            part, *more = finish("widened", acc, outs, last, *wide)
            stacks = [(-8, stack) for stack in more]
        elif k == 0:
            acc, outs = early(k, slice_order, chunks, halos, [], 0)
            (part,) = finish("plain", acc, outs)
        else:
            acc, outs, last = early(k, slice_order, chunks, halos, stacks, 1)
            swapped = x_swap(part)
            if k == 1:
                acc, got, swapped = tie(acc, got, swapped)
                pair = jnp.concatenate([keep, got])
                up, down = from_y(pair, -1), from_y(pair, 1)
            elif k == 3:
                acc, up, down, swapped = tie(acc, up, down, swapped)
                far_k, far_g = from_y(up[:HALF], -1), from_y(down[HALF:], 1)
                near_o = core_swap(jnp.concatenate([up, down, got]))
            elif k == 5:
                acc, *tconv = tie(acc, *tconv)
            elif k == 7:
                acc, up_a = tie(acc, up_a)
            part, value, stack = finish(
                "newest", acc, outs, last, part, swapped, rank=k - 1, halos=halos
            )
            values.append(value)
            stacks.append((-2 * (3 - (k - 1) % 4), stack))
        if k == 3:
            mean = part.astype(F32) + x_swap(part).astype(F32)
            newest = (ranked[k, 0].astype(F32) + mean).astype(BF)
            far_k, far_g, _ = tie(far_k, far_g, newest)
            newest, near_o = tie(newest, near_o)
            far_o = core_swap(jnp.concatenate([far_k, far_g]))
            chunks = [first, [pair, up, down, far_k, far_g, keep_other, near_o, far_o]]
            wide = around(jnp.stack([centre(value, 4) for value in values] + [newest]))
        if k == 5:
            block = jnp.concatenate([wide[2], wide[3][:, :1]], axis=1)
            own_a = jnp.concatenate([block] + [jnp.stack([centre(value, 5) for value in values[3:]])])
            down_one = [(i + 1, i) for i in range(8) if i % 4 < 3]
            up_a = lax.ppermute(own_a, "chan", down_one)
    mean = part.astype(F32) + x_swap(part).astype(F32)
    newest = (ranked[7, 0].astype(F32) + mean).astype(BF)
    own_b = jnp.concatenate([centre(values[-2], 5), centre(values[-1], 5), newest])
    edge = newest[:1]
    corner = [(i * 32 + (j + 1) % 32, (i - 1) * 32 + j) for i in range(8) if i % 4 > 0 for j in range(32)]
    own = [own_a, own_b, from_lon(edge, 1)]
    up = [up_a, lax.ppermute(own_b, "chan", down_one), lax.ppermute(edge, ("chan", "lon"), corner)]
    rows = jnp.stack(tconv, axis=1).reshape(27 * 32, 320)
    pieces = upsample(slice_order, gdn_beta[:, None], gdn_gamma, rows, own, up)
    return place([from_y(v, -r) if r else v for r, v in enumerate(pieces)])


def solution(mesh):
    placed = (
        P("chan", None, "lon", None),
        P("chan", None, "lon", None),
        P(),
        P("chan", None, None, None),
        P("chan", None, None, None),
        P("chan", None),
        P("chan", None, None),
        P(),
        P(),
        P(None, "chan", None),
    )
    return jax.shard_map(
        local, mesh=mesh, in_specs=placed, out_specs=P("chan", None, "lon", None), check_vma=False
    )
```
